128 devices in a mesh: ka: 16 (over z_lo, x, core), grid: 8 (over y, z_hi).
Axes of the slice: x: 4, y: 4, z: 4 (z_hi: 2, z_lo: 2; z = z_hi * 2 + z_lo), core: 2. Of those that a mesh axis runs over, the one named last changes fastest.
Arguments:
- orbitals: float32 [32, 3, 2, 64, 9216], P('ka', None, None, 'grid'), may hold values from -6 to 6
- partner_map: int32 [32], P('ka'), may hold values from 0 to 31, as said below
- wave_vectors: float32 [32, 3], P('ka'), may hold values from -0.5 to 0.5
- levels: float32 [32, 3], P('ka'), may hold values from 0.5 to 2
- potential: float32 [64, 9216], P('grid'), may hold values from 0 to 2
- perturbation: float32 [2, 64, 9216], P(None, 'grid'), may hold values from -0.5 to 1.5
- step_weights: int32 [4], replicated, may hold values from 2 to 12
Outputs:
- density: float32 [2, 64, 9216], P(None, 'grid')
The draws below stay inside these ranges and needn't reach their ends.
Inputs may be any that keep to these rules, and one draw needn't show every extreme that they name: partner_map is a permutation; it maps the 2 k-points starting at j * 2 onto the 2 k-points starting at ((j + 8) mod (16)) * 2, in an order of its own for each j.
All inputs are finite; a program needn't handle non-finite values.
Results may differ from the reference program's by a relative error of at most 0.00007.
Values sent between devices are 32-bit elements; how exact they have to be, the bound alone decides.
No kernel may reach another device: no remote copies, remote signals or barrier semaphores. Data moves between devices by JAX's collectives and lax.ppermute only.
A program may use at most 192 MiB of HBM per device.

```python
import math
import jax
import jax.numpy as jnp
from jax import lax

NX = 96
NY = 96
KDEV = 2
BANDS = 3
ITERS = 4
K = 32
NZ = 64


def draw_orbitals(key, part):
    base = jax.random.fold_in(key, 31)
    key_common, key_rough = jax.random.split(base, 2)
    shape = (K, BANDS, 2, NZ, NX * NY)
    common = jax.random.normal(key_common, (1, BANDS, 2, NZ, NX * NY), jnp.float32)
    rough = jax.random.normal(key_rough, shape, jnp.float32)
    field = common + 0.7 * rough
    return jnp.clip(field, -6.0, 6.0)


def draw_partner_map(key, part):
    blocks = K // KDEV
    keys = jax.random.split(jax.random.fold_in(key, 7), blocks)
    slots = jax.vmap(lambda single: jax.random.permutation(single, KDEV))(keys)
    partner = (jnp.arange(blocks, dtype=jnp.int32) + blocks // 2) % blocks
    return (partner[:, None] * KDEV + slots.astype(jnp.int32)).reshape(-1).astype(jnp.int32)


def place_ends(drawn, stream_key, low, largest):
    shape = drawn.shape
    index_at = [jax.random.randint(jax.random.fold_in(stream_key, axis), (), 0, shape[axis]) for axis in range(len(shape))]
    drawn = drawn.at[tuple(index_at)].set(low)
    longest = shape.index(max(shape))
    index_at[longest] = (index_at[longest] + 1) % shape[longest]
    return drawn.at[tuple(index_at)].set(largest)


def block_levels(stream_key, dims, cuts, least, high):
    gain, own = 1.0, jax.random.fold_in(stream_key, 6)
    for position, shards_of in cuts:
        steps = jnp.exp(jax.random.uniform(jax.random.fold_in(own, position), (shards_of,), jnp.float32, least / len(cuts), high / len(cuts)))
        gain = gain * jnp.repeat(steps, dims[position] // shards_of).reshape([-1 if axis == position else 1 for axis in range(len(dims))])
    return gain


def setup_inputs(seed: int = 0) -> dict:
    key_of = jax.random.split(jax.random.key(seed), 8)
    return {
        "orbitals": draw_orbitals(jax.random.fold_in(key_of[7], 71), 0),
        "partner_map": draw_partner_map(jax.random.fold_in(key_of[7], 71), 0),
        "wave_vectors": jnp.clip(jax.random.uniform(key_of[2], (K, 3), jnp.float32, -0.5, 0.5) * block_levels(key_of[2], (K, 3), ((0, 16),), -0.4, 0.0), -0.5, 0.5),
        "levels": jnp.clip(jnp.exp(math.log(2.0) - 1.3862944 * jax.random.uniform(key_of[3], (K, BANDS), jnp.float32) ** block_levels(key_of[3], (K, BANDS), ((0, 16),), -0.2, 0.2)), 0.5, 2.0),
        "potential": jnp.clip(2.0 * jax.random.uniform(key_of[4], (NZ, NX * NY), jnp.float32) ** block_levels(key_of[4], (NZ, NX * NY), ((0, 8),), -0.2, 0.2), 0.0, 2.0),
        "perturbation": jnp.clip(-0.5 + 2.0 * jax.random.uniform(key_of[5], (2, NZ, NX * NY), jnp.float32) ** block_levels(key_of[5], (2, NZ, NX * NY), ((1, 8),), -0.2, 0.2), -0.5, 1.5),
        "step_weights": place_ends(jax.random.randint(key_of[6], (ITERS,), 2, 13), jax.random.fold_in(key_of[6], 1), 2, 12).astype(jnp.int32),
    }


def along(field, offset, dimension):
    return jnp.roll(field, -offset, dimension)


def second_diff(field, dimension):
    return (16.0 * (along(field, 1, dimension) + along(field, -1, dimension)) - (along(field, 2, dimension) + along(field, -2, dimension)) - 30.0 * field) / 12.0


def first_diff(field, dimension):
    return (8.0 * (along(field, 1, dimension) - along(field, -1, dimension)) - (along(field, 2, dimension) - along(field, -2, dimension))) / 12.0


def hamiltonian(real_part, imag_part, wave, level, potential):
    shape4 = (real_part.shape[0], NZ, NY, NX)
    real4 = real_part.reshape(shape4)
    imag4 = imag_part.reshape(shape4)
    lap_real = second_diff(real4, 3) + second_diff(real4, 2) + second_diff(real4, 1)
    lap_imag = second_diff(imag4, 3) + second_diff(imag4, 2) + second_diff(imag4, 1)
    grad_real = wave[0] * first_diff(real4, 3) + wave[1] * first_diff(real4, 2) + wave[2] * first_diff(real4, 1)
    grad_imag = wave[0] * first_diff(imag4, 3) + wave[1] * first_diff(imag4, 2) + wave[2] * first_diff(imag4, 1)
    square = wave[0] * wave[0] + wave[1] * wave[1] + wave[2] * wave[2]
    total_pot = (potential[None] + level[:, None, None]).reshape(shape4)
    out_real = -0.5 * (lap_real - 2.0 * grad_imag - square * real4) + total_pot * real4
    out_imag = -0.5 * (lap_imag + 2.0 * grad_real - square * imag4) + total_pot * imag4
    return out_real.reshape(real_part.shape), out_imag.reshape(imag_part.shape)


def reference(orbitals, partner_map, wave_vectors, levels, potential, perturbation, step_weights):
    ncells = NX * NY * NZ
    highest = lax.Precision.HIGHEST
    weights = step_weights.astype(jnp.float32) / 100.0
    pert_real = perturbation[0]
    pert_imag = perturbation[1]

    def one_point(index):
        own = orbitals[index]
        mate = orbitals[partner_map[index]]
        own_real, own_imag = own[:, 0], own[:, 1]
        mate_real, mate_imag = mate[:, 0], mate[:, 1]
        w_real = pert_real * own_real - pert_imag * own_imag
        w_imag = pert_real * own_imag + pert_imag * own_real
        prod_real = (jnp.einsum('mzc,nzc->mn', mate_real, w_real, precision=highest) + jnp.einsum('mzc,nzc->mn', mate_imag, w_imag, precision=highest)) / ncells
        prod_imag = (jnp.einsum('mzc,nzc->mn', mate_real, w_imag, precision=highest) - jnp.einsum('mzc,nzc->mn', mate_imag, w_real, precision=highest)) / ncells
        proj_real = jnp.einsum('mn,mzc->nzc', prod_real, mate_real, precision=highest) - jnp.einsum('mn,mzc->nzc', prod_imag, mate_imag, precision=highest)
        proj_imag = jnp.einsum('mn,mzc->nzc', prod_imag, mate_real, precision=highest) + jnp.einsum('mn,mzc->nzc', prod_real, mate_imag, precision=highest)
        right_real = -(w_real - proj_real)
        right_imag = -(w_imag - proj_imag)
        wave = wave_vectors[index]
        level = levels[index]
        sol_real = jnp.zeros_like(right_real)
        sol_imag = jnp.zeros_like(right_imag)
        for count in range(ITERS):
            image_real, image_imag = hamiltonian(sol_real, sol_imag, wave, level, potential)
            sol_real = sol_real + weights[count] * (right_real - image_real)
            sol_imag = sol_imag + weights[count] * (right_imag - image_imag)
        dens_real = jnp.sum(own_real * sol_real + own_imag * sol_imag, 0)
        dens_imag = jnp.sum(own_real * sol_imag - own_imag * sol_real, 0)
        return jnp.stack([dens_real, dens_imag], 0)

    per_point = lax.map(one_point, jnp.arange(K, dtype=jnp.int32))
    return jnp.sum(per_point, 0) / K
```

```python
import functools

import jax
import jax.numpy as jnp
from jax import lax
from jax.experimental import pallas as pl
from jax.experimental.pallas import tpu as pltpu
from jax.sharding import Mesh
from jax.sharding import PartitionSpec as P

NX = 96
ITERS = 4
ROWS = 24
CHUNK = ROWS * NX
GROUP = 4 * NX
F32 = jnp.float32
ZAX = ("zl", "zh")
PIECE = CHUNK // 2


def z_perm(to):
    index = lambda z: (z & 1) * 2 + (z >> 1)
    return [(index(z), index(to(z))) for z in range(4)]


def z_xor(value, m):
    return lax.ppermute(value, ZAX, z_perm(lambda z: z ^ m))


def z_ring(value, by):
    return lax.ppermute(value, ZAX, z_perm(lambda z: (z + by) % 4))


def y_ring(value, by):
    return lax.ppermute(value, "y", [(i, (i + by) % 4) for i in range(4)])


def lane_ids():
    return lax.broadcasted_iota(jnp.int32, (8, 128), 1)


def unpack_rows(a, b, c, lanes):
    r0 = a
    r1 = jnp.where(lanes < 32, pltpu.roll(a, 32, 1), pltpu.roll(b, 32, 1))
    r2 = jnp.where(lanes < 64, pltpu.roll(b, 64, 1), pltpu.roll(c, 64, 1))
    r3 = pltpu.roll(c, 96, 1)
    return r0, r1, r2, r3


def pack_rows(r0, r1, r2, r3, lanes):
    r1s = pltpu.roll(r1, 96, 1)
    r2s = pltpu.roll(r2, 64, 1)
    r3s = pltpu.roll(r3, 32, 1)
    return (
        jnp.where(lanes < 96, r0, r1s),
        jnp.where(lanes < 64, r1s, r2s),
        jnp.where(lanes < 32, r2s, r3s),
    )


def wrap_x(value, lanes):
    return jnp.where(
        lanes < 96, value, jnp.where(lanes < 112, pltpu.roll(value, 96, 1), pltpu.roll(value, 32, 1))
    )


def perturbed(field, pert_r, pert_i):
    re, im = field
    return pert_r * re - pert_i * im, pert_r * im + pert_i * re


def products_kernel(slot_ref, o0, o1, o2, o3, p0, p1, out_ref, acc_ref):
    step = pl.program_id(0)

    @pl.when(step == 0)
    def _():
        acc_ref[...] = jnp.zeros_like(acc_ref)

    slabs = (((o0, o1), p0), ((o2, o3), p1))
    for k in range(4):
        block, kk = k // 2, k % 2
        slot = slot_ref[k]
        acc = [acc_ref[k * 18 + i] for i in range(18)]
        for pair, pert in slabs:
            own, mate = pair[block], pair[1 - block]
            for v in range(3):
                at = pl.ds(v * 128, 128)
                pr, pi = pert[1, :, at], pert[2, :, at]
                w = [perturbed((own[kk, n, 0, :, at], own[kk, n, 1, :, at]), pr, pi) for n in range(3)]
                for m in range(3):
                    mr, mi = mate[slot, m, 0, :, at], mate[slot, m, 1, :, at]
                    for n in range(3):
                        i = (m * 3 + n) * 2
                        acc[i] = acc[i] + (mr * w[n][0] + mi * w[n][1])
                        acc[i + 1] = acc[i + 1] + (mr * w[n][1] - mi * w[n][0])
        for i in range(18):
            acc_ref[k * 18 + i] = acc[i]

    @pl.when(step == pl.num_programs(0) - 1)
    def _():
        for i in range(72):
            out_ref[pl.ds(i, 1), :] = jnp.sum(acc_ref[i], axis=0, keepdims=True)


def orbital_specs():
    block = pl.BlockSpec((2, 3, 2, 8, GROUP), lambda i: (0, 0, 0, 0, i))
    pert = pl.BlockSpec((3, 8, GROUP), lambda i: (0, 0, i))
    return [block] * 4 + [pert] * 2


def products(slots, fields, perts):
    return pl.pallas_call(
        products_kernel,
        grid=(CHUNK // GROUP,),
        in_specs=[pl.BlockSpec(memory_space=pltpu.SMEM)] + orbital_specs(),
        out_specs=pl.BlockSpec((72, 128), lambda i: (0, 0)),
        out_shape=jax.ShapeDtypeStruct((72, 128), F32),
        scratch_shapes=[pltpu.VMEM((72, 8, 128), F32)],
        cost_estimate=pl.CostEstimate(flops=20_000_000, bytes_accessed=4_000_000, transcendentals=0),
        name="products",
    )(slots, *fields, *perts)


def right_kernel(ncells, slot_ref, half_ref, s0, s1, s2, s3, o0, o1, o2, o3, p0, p1, r_ref, orb_ref, v_ref, prod_ref):
    @pl.when(pl.program_id(0) == 0)
    def _():
        total = (s0[...] + s1[...]) + (s2[...] + s3[...])
        ones = jnp.full((128, 128), 1.0, F32)
        prod_ref[...] = jnp.dot(total, ones, precision=lax.Precision.HIGHEST, preferred_element_type=F32) / ncells

    lanes = lane_ids()
    half = half_ref[0]
    slabs = (((o0, o1), p0, half), ((o2, o3), p1, 1 - half))
    for pair, pert, z in slabs:
        planes = pl.ds(pl.multiple_of(z * 8, 8), 8)
        rows = unpack_rows(*[pert[0, :, pl.ds(v * 128, 128)] for v in range(3)], lanes)
        for j in range(4):
            v_ref[j, planes, :] = rows[j]
        for k in range(4):
            block, kk = k // 2, k % 2
            slot = slot_ref[k]
            own, mate = pair[block], pair[1 - block]
            right = [[[], []] for _ in range(3)]
            for v in range(3):
                at = pl.ds(v * 128, 128)
                pr, pi = pert[1, :, at], pert[2, :, at]
                mates = [(mate[slot, m, 0, :, at], mate[slot, m, 1, :, at]) for m in range(3)]
                for n in range(3):
                    wr, wi = perturbed((own[kk, n, 0, :, at], own[kk, n, 1, :, at]), pr, pi)
                    gr, gi = -wr, -wi
                    for m in range(3):
                        row = k * 18 + (m * 3 + n) * 2
                        qr = prod_ref[pl.ds(row, 1), :]
                        qi = prod_ref[pl.ds(row + 1, 1), :]
                        mr, mi = mates[m]
                        gr = gr + (qr * mr - qi * mi)
                        gi = gi + (qi * mr + qr * mi)
                    right[n][0].append(gr)
                    right[n][1].append(gi)
            for n in range(3):
                for c in range(2):
                    rows = unpack_rows(*right[n][c], lanes)
                    orb = unpack_rows(*[own[kk, n, c, :, pl.ds(v * 128, 128)] for v in range(3)], lanes)
                    for j in range(4):
                        r_ref[k * 3 + n, c, j, planes, :] = wrap_x(rows[j], lanes)
                        orb_ref[k * 3 + n, c, j, planes, :] = orb[j]


def right_sides(ncells, slots, half, sums, fields, perts):
    smem = pl.BlockSpec(memory_space=pltpu.SMEM)
    whole = pl.BlockSpec((72, 128), lambda i: (0, 0))
    rows = pl.BlockSpec((12, 2, 4, 16, 128), lambda i: (0, 0, i, 0, 0))
    shape = jax.ShapeDtypeStruct((12, 2, ROWS, 16, 128), F32)
    return pl.pallas_call(
        functools.partial(right_kernel, ncells),
        grid=(CHUNK // GROUP,),
        in_specs=[smem, smem] + [whole] * 4 + orbital_specs(),
        out_specs=[rows, rows, pl.BlockSpec((4, 16, 128), lambda i: (i, 0, 0))],
        out_shape=[shape, shape, jax.ShapeDtypeStruct((ROWS, 16, 128), F32)],
        scratch_shapes=[pltpu.VMEM((72, 128), F32)],
        cost_estimate=pl.CostEstimate(flops=20_000_000, bytes_accessed=14_000_000, transcendentals=0),
        name="right_sides",
    )(slots, half, *sums, *fields, *perts)


def step_kernel(last, coef_ref, u_ref, r_ref, v_ref, zm, zp, ym, yp, *refs):
    if last:
        orb_ref, out_ref, dens_ref, pad = refs
    else:
        out_ref, pad = refs
    kn = pl.program_id(0)
    coef = [coef_ref[kn * 16 + i] for i in range(9)]
    diag, minus_wt, wt, c1, c2, kx, ky, kz, scale = coef
    for c in range(2):
        pad[c, 2:26, 8:24, :] = u_ref[0, c] * scale
        pad[c, 2:26, 6:8, :] = zm[0, c] * scale
        pad[c, 2:26, 24:26, :] = zp[0, c] * scale
        pad[c, 0:2, 8:24, :] = ym[0, c] * scale
        pad[c, 26:28, 8:24, :] = yp[0, c] * scale
    lanes = lax.broadcasted_iota(jnp.int32, (16, 128), 1)

    if last:
        @pl.when(kn == 0)
        def _():
            dens_ref[...] = jnp.zeros_like(dens_ref)

    def row(r, carry):
        cells, first, second, grad = [], [], [], []
        for c in range(2):
            u = pad[c, r + 2, 8:24, :]
            xp1, xm1 = pltpu.roll(u, 127, 1), pltpu.roll(u, 1, 1)
            xp2, xm2 = pltpu.roll(u, 126, 1), pltpu.roll(u, 2, 1)
            yp1, ym1 = pad[c, r + 3, 8:24, :], pad[c, r + 1, 8:24, :]
            yp2, ym2 = pad[c, r + 4, 8:24, :], pad[c, r, 8:24, :]
            zp1, zm1 = pad[c, r + 2, 9:25, :], pad[c, r + 2, 7:23, :]
            zp2, zm2 = pad[c, r + 2, 10:26, :], pad[c, r + 2, 6:22, :]
            cells.append(u)
            first.append((xp1 + xm1) + (yp1 + ym1) + (zp1 + zm1))
            second.append((xp2 + xm2) + (yp2 + ym2) + (zp2 + zm2))
            gx = (xp1 - xm1) - 0.125 * (xp2 - xm2)
            gy = (yp1 - ym1) - 0.125 * (yp2 - ym2)
            gz = (zp1 - zm1) - 0.125 * (zp2 - zm2)
            grad.append(kx * gx + ky * gy + kz * gz)
        center = diag + minus_wt * v_ref[r]
        new = []
        for c in range(2):
            value = center * cells[c] + wt * r_ref[0, c, r] + (c1 * first[c] + c2 * second[c])
            value = value - grad[1] if c == 0 else value + grad[0]
            new.append(value)
        if last:
            orb_r, orb_i = orb_ref[0, 0, r], orb_ref[0, 1, r]
            dens_ref[0, r] += orb_r * new[0] + orb_i * new[1]
            dens_ref[1, r] += orb_r * new[1] - orb_i * new[0]
        else:
            for c in range(2):
                wrapped = jnp.where(
                    lanes < 96,
                    new[c],
                    jnp.where(lanes < 112, pltpu.roll(new[c], 96, 1), pltpu.roll(new[c], 32, 1)),
                )
                out_ref[0, c, r] = wrapped
        return carry

    lax.fori_loop(0, ROWS, row, 0, unroll=2)

    if last:
        @pl.when(kn == pl.num_programs(0) - 1)
        def _():
            ids = lane_ids()
            for c in range(2):
                for z in range(2):
                    for g in range(6):
                        rows = [dens_ref[c, 4 * g + j, 8 * z : 8 * z + 8, :] * (1.0 / 32.0) for j in range(4)]
                        packed = pack_rows(*rows, ids)
                        for v in range(3):
                            at = (g % 3) * GROUP + v * 128
                            out_ref[(c * 2 + g // 3) * 2 + z, :, at : at + 128] = packed[v]


def richardson_step(coef, u, right, pot, halos, orb=None):
    last = orb is not None
    field = pl.BlockSpec((1, 2, ROWS, 16, 128), lambda i: (i, 0, 0, 0, 0))
    zspec = pl.BlockSpec((1, 2, ROWS, 2, 128), lambda i: (i, 0, 0, 0, 0))
    yspec = pl.BlockSpec((1, 2, 2, 16, 128), lambda i: ((i + 6) % 12, 0, 0, 0, 0))
    vspec = pl.BlockSpec((ROWS, 16, 128), lambda i: (0, 0, 0))
    scratch = [pltpu.VMEM((2, ROWS + 4, 32, 128), F32)]
    if last:
        out_spec = pl.BlockSpec((8, 8, PIECE), lambda i: (0, 0, 0))
        out_shape = jax.ShapeDtypeStruct((8, 8, PIECE), F32)
        scratch = [pltpu.VMEM((2, ROWS, 16, 128), F32)] + scratch
    else:
        out_spec, out_shape = field, jax.ShapeDtypeStruct((12, 2, ROWS, 16, 128), F32)
    return pl.pallas_call(
        functools.partial(step_kernel, last),
        grid=(12,),
        in_specs=[pl.BlockSpec(memory_space=pltpu.SMEM), field, field, vspec, zspec, zspec, yspec, yspec]
        + ([field] if last else []),
        out_specs=out_spec,
        out_shape=out_shape,
        scratch_shapes=scratch,
        cost_estimate=pl.CostEstimate(flops=40_000_000, bytes_accessed=16_000_000, transcendentals=0),
        name="last_step" if last else "step",
    )(coef, u, right, pot, *halos, *([orb] if last else []))


def assemble_kernel(pos_ref, b0, b1, b2, b3, out_ref):
    x, z = pos_ref[0], pos_ref[1]
    for d, block in enumerate((b0, b1, b2, b3)):
        part = x ^ d
        for m in range(4):
            q = z ^ m
            at = pl.multiple_of(q * CHUNK + (part & 1) * PIECE, 128)
            out_ref[part >> 1, :, pl.ds(at, PIECE)] = block[m]


def assemble(pos, blocks):
    return pl.pallas_call(
        assemble_kernel,
        in_specs=[pl.BlockSpec(memory_space=pltpu.SMEM)] + [pl.BlockSpec(memory_space=pltpu.VMEM)] * 4,
        out_specs=pl.BlockSpec(memory_space=pltpu.VMEM),
        out_shape=jax.ShapeDtypeStruct((2, 8, 4 * CHUNK), F32),
        name="assemble",
    )(pos, *blocks)


def exchange(field):
    zm = y_ring(field[:, :, :, 14:16, :], 1)
    zp = y_ring(field[:, :, :, 0:2, :], 3)
    ym = z_ring(field[:, :, ROWS - 2 :], 1)
    yp = z_ring(field[:, :, :2], 3)
    return zm, zp, ym, yp


def on_device(orbitals, partner_map, wave_vectors, levels, potential, perturbation, step_weights):
    zl, zh = lax.axis_index("zl"), lax.axis_index("zh")
    x, core = lax.axis_index("x"), lax.axis_index("c")
    z = zh * 2 + zl
    ncells = 64 * 4 * CHUNK

    def chunk(array, q):
        return lax.dynamic_slice_in_dim(array, q * CHUNK, CHUNK, axis=array.ndim - 1)

    pots = jnp.concatenate([potential[None], perturbation], 0)
    moved = [z_xor(chunk(orbitals, z ^ m), m) for m in (1, 2, 3)]
    fields = [chunk(orbitals, z)] + moved
    perts = [chunk(pots, z), z_xor(chunk(pots, z ^ 3), 3)]
    slot = (partner_map % 2).astype(F32)
    mine = jnp.concatenate([wave_vectors, levels, slot[:, None], jnp.zeros((2, 1), F32)], 1)
    other = z_xor(mine, 1)
    both = jnp.concatenate([mine, other], 0)
    slots = both[:, 6].astype(jnp.int32)

    weights = step_weights.astype(F32) / 100.0
    wave = jnp.repeat(both[:, :3], 3, axis=0)
    level = both[:, 3:6].reshape(12)
    square = wave[:, 0] * wave[:, 0] + wave[:, 1] * wave[:, 1] + wave[:, 2] * wave[:, 2]
    base = 3.75 + 0.5 * square + level

    def coefficients(count):
        wt = weights[count]
        one = jnp.ones((12,), F32)
        scale = weights[0] if count == 1 else jnp.float32(1.0)
        cols = [
            1.0 - wt * base,
            -wt * one,
            wt * one,
            (wt * 2.0 / 3.0) * one,
            (-wt / 24.0) * one,
            (wt * 2.0 / 3.0) * wave[:, 0],
            (wt * 2.0 / 3.0) * wave[:, 1],
            (wt * 2.0 / 3.0) * wave[:, 2],
            scale * one,
        ]
        cols += [jnp.zeros((12,), F32)] * 7
        return jnp.stack(cols, 1).reshape(-1)

    part = products(slots, fields, perts)

    def swapped(value):
        return jnp.concatenate([value[36:], value[:36]], 0)

    part = part + swapped(z_xor(part, 1)) + z_xor(part, 2) + swapped(z_xor(part, 3))
    sums = [part] + [y_ring(part, by) for by in (1, 2, 3)]
    right, orb, pot = right_sides(float(ncells), slots, zh[None].astype(jnp.int32), sums, fields, perts)
    u = right
    for count in range(1, ITERS):
        halos = exchange(u)
        u = richardson_step(coefficients(count), u, right, pot, halos, orb if count == ITERS - 1 else None)

    me = x * 2 + core
    piece = lax.dynamic_index_in_dim(u, me, 0, keepdims=False)
    for m in range(1, 8):
        send = lax.dynamic_index_in_dim(u, me ^ m, 0, keepdims=False)
        piece = piece + lax.ppermute(send, ("x", "c"), [(i, i ^ m) for i in range(8)])
    got = [piece]
    for m in (1, 2, 3):
        pairs = []
        for zz in range(4):
            to = zz ^ m
            c = to >> 1
            index = lambda w: (w & 1) * 4 + c * 2 + (w >> 1)
            pairs.append((index(zz), index(to)))
        got.append(lax.ppermute(piece, ("zl", "c", "zh"), pairs))
    slab = jnp.stack(got)
    same = core == zh
    blocks = []
    for d in range(4):
        index = lambda xx, c, h: xx * 4 + c * 2 + h
        across = lax.ppermute(slab, ("x", "c", "zh"), [(index(i, h, h), index(i ^ d, 1 - h, h)) for i in range(4) for h in range(2)])
        straight = slab
        if d:
            straight = lax.ppermute(slab, ("x", "c", "zh"), [(index(i, h, h), index(i ^ d, h, h)) for i in range(4) for h in range(2)])
        blocks.append(jnp.where(same, straight, across))
    return assemble(jnp.stack([x, z]).astype(jnp.int32), blocks)


def solution(mesh):
    fine = Mesh(mesh.devices.reshape(2, 4, 2, 4, 2), ("zl", "x", "c", "y", "zh"))
    ka, grid = ("zl", "x", "c"), ("y", "zh")
    return jax.shard_map(
        on_device,
        mesh=fine,
        in_specs=(
            P(ka, None, None, grid, None),
            P(ka),
            P(ka, None),
            P(ka, None),
            P(grid, None),
            P(None, grid, None),
            P(),
        ),
        out_specs=P(None, grid, None),
        check_vma=False,
    )
```

```python
import functools

import jax
import jax.numpy as jnp
import numpy as np
from jax import lax
from jax.experimental import pallas as pl
from jax.experimental.pallas import tpu as pltpu
from jax.sharding import Mesh
from jax.sharding import PartitionSpec as P

NX = 96
ITERS = 4
ROWS = 24
CHUNK = ROWS * NX
GROUP = 4 * NX
F32 = jnp.float32
ZAX = ("zl", "zh")
PIECE = CHUNK // 2


def z_perm(to):
    index = lambda z: (z & 1) * 2 + (z >> 1)
    return [(index(z), index(to(z))) for z in range(4)]


def z_xor(value, m):
    return lax.ppermute(value, ZAX, z_perm(lambda z: z ^ m))


def z_ring(value, by):
    return lax.ppermute(value, ZAX, z_perm(lambda z: (z + by) % 4))


def y_ring(value, by):
    return lax.ppermute(value, "y", [(i, (i + by) % 4) for i in range(4)])


def lane_ids():
    return lax.broadcasted_iota(jnp.int32, (8, 128), 1)


def unpack_rows(a, b, c, lanes):
    r0 = a
    r1 = jnp.where(lanes < 32, pltpu.roll(a, 32, 1), pltpu.roll(b, 32, 1))
    r2 = jnp.where(lanes < 64, pltpu.roll(b, 64, 1), pltpu.roll(c, 64, 1))
    r3 = pltpu.roll(c, 96, 1)
    return r0, r1, r2, r3


def pack_rows(r0, r1, r2, r3, lanes):
    r1s = pltpu.roll(r1, 96, 1)
    r2s = pltpu.roll(r2, 64, 1)
    r3s = pltpu.roll(r3, 32, 1)
    return (
        jnp.where(lanes < 96, r0, r1s),
        jnp.where(lanes < 64, r1s, r2s),
        jnp.where(lanes < 32, r2s, r3s),
    )


def in_vmem(shape):
    return pltpu.VMEM(shape, F32)


def call(kernel, name, args, outs, scratch=(), scalars=0, aliases=None, flops=10_000_000, limit=8):
    specs = [pl.BlockSpec(memory_space=pltpu.SMEM)] * scalars
    specs += [pl.BlockSpec(memory_space=pltpu.VMEM)] * (len(args) - scalars)
    args = list(args[:scalars]) + [pltpu.with_memory_space_constraint(a, pltpu.VMEM) for a in args[scalars:]]
    return pl.pallas_call(
        kernel,
        in_specs=specs,
        out_specs=[pl.BlockSpec(memory_space=pltpu.VMEM)] * len(outs),
        out_shape=[in_vmem(o) for o in outs],
        scratch_shapes=list(scratch),
        input_output_aliases=aliases or {},
        compiler_params=pltpu.CompilerParams(vmem_limit_bytes=limit * 2**20),
        cost_estimate=pl.CostEstimate(flops=flops, bytes_accessed=10_000_000, transcendentals=0),
        name=name,
    )(*args)


def lanes_at(group, v):
    return pl.ds(pl.multiple_of(group * GROUP + v * 128, 128), 128)


def perturbed(field, pert_r, pert_i):
    re, im = field
    return pert_r * re - pert_i * im, pert_r * im + pert_i * re


def products_kernel(slot_ref, o0, o1, o2, o3, p0, p1, out_ref):
    slabs = (((o0, o1), p0), ((o2, o3), p1))
    for k in range(4):
        block, kk = k // 2, k % 2
        slot = slot_ref[k]

        def body(g, acc, block=block, kk=kk, slot=slot):
            acc = list(acc)
            for pair, pert in slabs:
                own, mate = pair[block], pair[1 - block]
                for v in range(3):
                    at = lanes_at(g, v)
                    pr, pi = pert[1, :, at], pert[2, :, at]
                    w = [perturbed((own[kk, n, 0, :, at], own[kk, n, 1, :, at]), pr, pi) for n in range(3)]
                    for m in range(3):
                        mr, mi = mate[slot, m, 0, :, at], mate[slot, m, 1, :, at]
                        for n in range(3):
                            i = (m * 3 + n) * 2
                            acc[i] = acc[i] + (mr * w[n][0] + mi * w[n][1])
                            acc[i + 1] = acc[i + 1] + (mr * w[n][1] - mi * w[n][0])
            return tuple(acc)

        acc = lax.fori_loop(0, CHUNK // GROUP, body, (jnp.zeros((8, 128), F32),) * 18)
        for i in range(18):
            out_ref[pl.ds(k * 18 + i, 1), :] = jnp.sum(acc[i], axis=0, keepdims=True)


def products(slots, fields, perts):
    return call(products_kernel, "products", (slots, *fields, *perts), [(72, 128)], scalars=1, flops=20_000_000)[0]


def rows_at(kn, c, r):
    return ((kn * 2 + c) * ROWS + r) * 16


def orbital_rows_kernel(half_ref, o0, o1, o2, o3, p0, p1, orb_ref, v_ref):
    lanes = lane_ids()
    half = half_ref[0]

    def body(g, carry):
        for pair, pert, z in (((o0, o1), p0, half), ((o2, o3), p1, 1 - half)):
            rows = unpack_rows(*[pert[0, :, lanes_at(g, v)] for v in range(3)], lanes)
            for j in range(4):
                v_ref[pl.ds(pl.multiple_of((4 * g + j) * 16 + 8 * z, 8), 8), :] = rows[j]
            for k in range(4):
                for n in range(3):
                    for c in range(2):
                        rows = unpack_rows(*[pair[k // 2][k % 2, n, c, :, lanes_at(g, v)] for v in range(3)], lanes)
                        for j in range(4):
                            at = pl.multiple_of(rows_at(k * 3 + n, c, 4 * g + j) + 8 * z, 8)
                            orb_ref[pl.ds(at, 8), :] = rows[j]
        return carry

    lax.fori_loop(0, CHUNK // GROUP, body, 0)


def orbital_rows(half, fields, perts):
    outs = [(24 * ROWS * 16, 128), (ROWS * 16, 128)]
    return call(orbital_rows_kernel, "orbital_rows", (half, *fields, *perts), outs, scalars=1)


ZHALO, YHALO = (48 * ROWS, 128), (24 * 32, 128)


def cut_halos(u_ref, kn, zdn, zup, ydn, yup):
    for c in range(2):
        base = rows_at(kn, c, 0)
        for p in range(2):
            to = pl.ds(pl.multiple_of(((kn * 2 + c) * 2 + p) * ROWS, 8), ROWS)
            zdn[to, :] = u_ref[pl.ds(base + p, ROWS, stride=16), :]
            zup[to, :] = u_ref[pl.ds(base + 14 + p, ROWS, stride=16), :]
        to = pl.ds(pl.multiple_of((kn * 2 + c) * 32, 8), 32)
        ydn[to, :] = u_ref[pl.ds(pl.multiple_of(base, 8), 32), :]
        yup[to, :] = u_ref[pl.ds(pl.multiple_of(base + 22 * 16, 8), 32), :]


def exchange(zdn, zup, ydn, yup):
    return y_ring(zup, 1), y_ring(zdn, 3), z_ring(yup, 1), z_ring(ydn, 3)


def right_kernel(ncells, slot_ref, half_ref, s0, s1, s2, s3, o0, o1, o2, o3, p0, p1, r_ref, zdn, zup, ydn, yup, prod_ref):
    total = (s0[...] + s1[...]) + (s2[...] + s3[...])
    ones = jnp.full((128, 128), 1.0, F32)
    prod_ref[...] = jnp.dot(total, ones, precision=lax.Precision.HIGHEST, preferred_element_type=F32) / ncells
    lanes = lane_ids()
    half = half_ref[0]
    slabs = (((o0, o1), p0, half), ((o2, o3), p1, 1 - half))
    for k in range(4):
        block, kk = k // 2, k % 2
        slot = slot_ref[k]

        def body(g, carry, k=k, block=block, kk=kk, slot=slot):
            for pair, pert, z in slabs:
                own, mate = pair[block], pair[1 - block]
                right = [[[], []] for _ in range(3)]
                for v in range(3):
                    at = lanes_at(g, v)
                    pr, pi = pert[1, :, at], pert[2, :, at]
                    mates = [(mate[slot, m, 0, :, at], mate[slot, m, 1, :, at]) for m in range(3)]
                    for n in range(3):
                        wr, wi = perturbed((own[kk, n, 0, :, at], own[kk, n, 1, :, at]), pr, pi)
                        gr, gi = -wr, -wi
                        for m in range(3):
                            row = k * 18 + (m * 3 + n) * 2
                            qr = prod_ref[pl.ds(row, 1), :]
                            qi = prod_ref[pl.ds(row + 1, 1), :]
                            mr, mi = mates[m]
                            gr = gr + (qr * mr - qi * mi)
                            gi = gi + (qi * mr + qr * mi)
                        right[n][0].append(gr)
                        right[n][1].append(gi)
                for n in range(3):
                    for c in range(2):
                        rows = unpack_rows(*right[n][c], lanes)
                        for j in range(4):
                            at = pl.multiple_of(rows_at(k * 3 + n, c, 4 * g + j) + 8 * z, 8)
                            r_ref[pl.ds(at, 8), :] = rows[j]
            return carry

        lax.fori_loop(0, CHUNK // GROUP, body, 0)

    def cut(kn, carry):
        cut_halos(r_ref, kn, zdn, zup, ydn, yup)
        return carry

    lax.fori_loop(0, 12, cut, 0)


def right_sides(ncells, slots, half, sums, fields, perts):
    return call(
        functools.partial(right_kernel, ncells),
        "right_sides",
        (slots, half, *sums, *fields, *perts),
        [(24 * ROWS * 16, 128), ZHALO, ZHALO, YHALO, YHALO],
        scratch=[pltpu.VMEM((72, 128), F32)],
        scalars=2,
        flops=20_000_000,
    )


def x_matrix():
    m = np.zeros((128, 256), np.float32)
    for i in range(NX):
        for s, lap, grad in ((1, 16, 8), (-1, 16, -8), (2, -1, -1), (-2, -1, 1)):
            m[(i + s) % NX, i] += lap
            m[(i + s) % NX, 128 + i] += grad
    return np.concatenate([m, m], 0)


def scalars_of(count, par_ref, w_ref, kn):
    k, n = kn // 3, kn % 3
    kx, ky, kz = par_ref[k * 8], par_ref[k * 8 + 1], par_ref[k * 8 + 2]
    base = 3.75 + 0.5 * (kx * kx + ky * ky + kz * kz) + par_ref[k * 8 + 3 + n]
    wt = w_ref[count]
    scale = w_ref[0] if count == 1 else jnp.float32(1.0)
    return kx, ky, kz, base, wt, scale


def step_kernel(count, par_ref, w_ref, u_ref, r_ref, v_ref, m_ref, *refs):
    last = count == ITERS - 1
    if last:
        orb_ref, out_ref, pad, flat = refs
        out_ref[...] = jnp.zeros_like(out_ref)
    else:
        out_ref, pad, flat = refs
    pad[...] = jnp.zeros_like(pad)

    def orbital(kn, carry):
        kx, ky, kz, base, wt, scale = scalars_of(count, par_ref, w_ref, kn)
        whole = pl.ds(pl.multiple_of(rows_at(kn, 0, 0), 8), 48 * 16)
        u2 = u_ref[whole, :] * scale
        hi = u2.astype(jnp.bfloat16)
        lo = (u2 - hi.astype(F32)).astype(jnp.bfloat16)
        flat[...] = jnp.dot(jnp.concatenate([hi, lo], 1), m_ref[...], preferred_element_type=F32)
        for c in range(2):
            for r in range(ROWS):
                pad[c, r + 2, 8:24, :] = u2[(c * ROWS + r) * 16 : (c * ROWS + r + 1) * 16]
        lap = wt / 24.0
        gx, gy, gz = wt * kx / 12.0, wt * ky * (2.0 / 3.0), wt * kz * (2.0 / 3.0)
        keep = 1.0 - wt * base

        def row(r, carry):
            cells, second, grad = [], [], []
            for c in range(2):
                at = pl.multiple_of((c * ROWS + r) * 16, 16)
                yp1, ym1 = pad[c, r + 3, 8:24, :], pad[c, r + 1, 8:24, :]
                yp2, ym2 = pad[c, r + 4, 8:24, :], pad[c, r, 8:24, :]
                zp1, zm1 = pad[c, r + 2, 9:25, :], pad[c, r + 2, 7:23, :]
                zp2, zm2 = pad[c, r + 2, 10:26, :], pad[c, r + 2, 6:22, :]
                cells.append(pad[c, r + 2, 8:24, :])
                one = (yp1 + ym1) + (zp1 + zm1)
                two = (yp2 + ym2) + (zp2 + zm2)
                second.append(flat[pl.ds(at, 16), 0:128] + (16.0 * one - two))
                dy = (yp1 - ym1) - 0.125 * (yp2 - ym2)
                dz = (zp1 - zm1) - 0.125 * (zp2 - zm2)
                grad.append(gx * flat[pl.ds(at, 16), 128:256] + (gy * dy + gz * dz))
            center = keep - wt * v_ref[pl.ds(pl.multiple_of(r * 16, 16), 16), :]
            new = []
            for c in range(2):
                at = pl.multiple_of(rows_at(kn, c, r), 16)
                value = (center * cells[c] + wt * r_ref[pl.ds(at, 16), :]) + lap * second[c]
                new.append(value - grad[1] if c == 0 else value + grad[0])
            if last:
                orb_r = orb_ref[pl.ds(pl.multiple_of(rows_at(kn, 0, r), 16), 16), :]
                orb_i = orb_ref[pl.ds(pl.multiple_of(rows_at(kn, 1, r), 16), 16), :]
                out_ref[pl.ds(pl.multiple_of(r * 16, 16), 16), :] += orb_r * new[0] + orb_i * new[1]
                out_ref[pl.ds(pl.multiple_of((ROWS + r) * 16, 16), 16), :] += orb_r * new[1] - orb_i * new[0]
            else:
                for c in range(2):
                    out_ref[pl.ds(pl.multiple_of(rows_at(kn, c, r), 16), 16), :] = new[c]
            return carry

        lax.fori_loop(0, ROWS, row, 0)
        return carry

    lax.fori_loop(0, 12, orbital, 0)


def inner_step(count, par, weights, u, right, pot, matrix, orb):
    last = count == ITERS - 1
    return call(
        functools.partial(step_kernel, count),
        "last_step" if last else "step",
        (par, weights, u, right, pot, matrix) + ((orb,) if last else ()),
        [(2 * ROWS * 16, 128) if last else (24 * ROWS * 16, 128)],
        scratch=[pltpu.VMEM((2, ROWS + 4, 32, 128), F32), pltpu.VMEM((2 * ROWS * 16, 256), F32)],
        scalars=2,
        flops=60_000_000,
    )[0]


def face_terms(lap, g, beyond1, beyond2, sign):
    first = [lap * (16.0 * beyond1[c] - beyond2[c]) for c in range(2)]
    grad1 = [(sign * g) * (beyond1[c] - 0.125 * beyond2[c]) for c in range(2)]
    second = [-lap * beyond1[c] for c in range(2)]
    grad2 = [(-0.125 * sign * g) * beyond1[c] for c in range(2)]
    return (
        (first[0] - grad1[1], first[1] + grad1[0]),
        (second[0] - grad2[1], second[1] + grad2[0]),
    )


def faces(count, par_ref, w_ref, kn, zm, zp, ym, yp, add):
    kx, ky, kz, base, wt, scale = scalars_of(count, par_ref, w_ref, kn)
    ws = wt * scale
    lap = ws / 24.0
    gy, gz = ws * ky * (2.0 / 3.0), ws * kz * (2.0 / 3.0)

    def plane(ref, p):
        return [ref[pl.ds(pl.multiple_of(((kn * 2 + c) * 2 + p) * ROWS, 8), ROWS), :] for c in range(2)]

    from_z = (kn + 6) % 12

    def line(ref, r):
        return [ref[pl.ds(pl.multiple_of(((from_z * 2 + c) * 2 + r) * 16, 8), 16), :] for c in range(2)]

    for ref, near, far, sign, cells in ((zm, 1, 0, -1.0, (0, 1)), (zp, 0, 1, 1.0, (15, 14))):
        terms = face_terms(lap, gz, plane(ref, near), plane(ref, far), sign)
        for cell, term in zip(cells, terms):
            add([pl.ds(rows_at(kn, c, 0) + cell, ROWS, stride=16) for c in range(2)],
                [pl.ds(c * ROWS * 16 + cell, ROWS, stride=16) for c in range(2)], term)
    for ref, near, far, sign, cells in ((ym, 1, 0, -1.0, (0, 1)), (yp, 0, 1, 1.0, (23, 22))):
        terms = face_terms(lap, gy, line(ref, near), line(ref, far), sign)
        for cell, term in zip(cells, terms):
            add([pl.ds(pl.multiple_of(rows_at(kn, c, cell), 16), 16) for c in range(2)],
                [pl.ds((c * ROWS + cell) * 16, 16) for c in range(2)], term)


def faces_kernel(count, par_ref, w_ref, u_in, zm, zp, ym, yp, u_ref, zdn, zup, ydn, yup):
    def orbital(kn, carry):
        def add(at, _, term):
            for c in range(2):
                u_ref[at[c], :] = u_ref[at[c], :] + term[c]

        faces(count, par_ref, w_ref, kn, zm, zp, ym, yp, add)
        cut_halos(u_ref, kn, zdn, zup, ydn, yup)
        return carry

    lax.fori_loop(0, 12, orbital, 0)


def add_faces(count, par, weights, u, halos):
    return call(
        functools.partial(faces_kernel, count),
        "faces",
        (par, weights, u, *halos),
        [(24 * ROWS * 16, 128), ZHALO, ZHALO, YHALO, YHALO],
        scalars=2,
        aliases={2: 0},
    )


def density_kernel(par_ref, w_ref, d_in, zm, zp, ym, yp, orb_ref, out_ref, d_ref):
    d_ref[...] = d_in[...]

    def orbital(kn, carry):
        def add(at, to, term):
            orb_r, orb_i = orb_ref[at[0], :], orb_ref[at[1], :]
            d_ref[to[0], :] = d_ref[to[0], :] + (orb_r * term[0] + orb_i * term[1])
            d_ref[to[1], :] = d_ref[to[1], :] + (orb_r * term[1] - orb_i * term[0])

        faces(ITERS - 1, par_ref, w_ref, kn, zm, zp, ym, yp, add)
        return carry

    lax.fori_loop(0, 12, orbital, 0)
    ids = lane_ids()
    for c in range(2):
        for z in range(2):
            for g in range(6):
                rows = [d_ref[pl.ds((c * ROWS + 4 * g + j) * 16 + 8 * z, 8), :] * (1.0 / 32.0) for j in range(4)]
                packed = pack_rows(*rows, ids)
                for v in range(3):
                    at = (g % 3) * GROUP + v * 128
                    out_ref[(c * 2 + g // 3) * 2 + z, :, at : at + 128] = packed[v]


def density_pieces(par, weights, dens, halos, orb):
    return call(
        density_kernel,
        "density",
        (par, weights, dens, *halos, orb),
        [(8, 8, PIECE)],
        scratch=[pltpu.VMEM((2 * ROWS * 16, 128), F32)],
        scalars=2,
    )[0]


def assemble_kernel(pos_ref, b0, b1, b2, b3, out_ref):
    x, z = pos_ref[0], pos_ref[1]
    for d, block in enumerate((b0, b1, b2, b3)):
        part = x ^ d
        for m in range(4):
            q = z ^ m
            at = pl.multiple_of(q * CHUNK + (part & 1) * PIECE, 128)
            out_ref[part >> 1, :, pl.ds(at, PIECE)] = block[m]


def assemble(pos, blocks):
    return pl.pallas_call(
        assemble_kernel,
        in_specs=[pl.BlockSpec(memory_space=pltpu.SMEM)] + [pl.BlockSpec(memory_space=pltpu.VMEM)] * 4,
        out_specs=pl.BlockSpec(memory_space=pltpu.VMEM),
        out_shape=jax.ShapeDtypeStruct((2, 8, 4 * CHUNK), F32),
        name="assemble",
    )(pos, *blocks)


def on_device(orbitals, partner_map, wave_vectors, levels, potential, perturbation, step_weights):
    zl, zh = lax.axis_index("zl"), lax.axis_index("zh")
    x, core = lax.axis_index("x"), lax.axis_index("c")
    z = zh * 2 + zl
    ncells = 64 * 4 * CHUNK

    def chunk(array, q):
        return lax.dynamic_slice_in_dim(array, q * CHUNK, CHUNK, axis=array.ndim - 1)

    pots = jnp.concatenate([potential[None], perturbation], 0)
    moved = [z_xor(chunk(orbitals, z ^ m), m) for m in (1, 2, 3)]
    fields = [chunk(orbitals, z)] + moved
    perts = [chunk(pots, z), z_xor(chunk(pots, z ^ 3), 3)]
    slot = (partner_map % 2).astype(F32)
    mine = jnp.concatenate([wave_vectors, levels, slot[:, None], jnp.zeros((2, 1), F32)], 1)
    other = z_xor(mine, 1)
    both = jnp.concatenate([mine, other], 0)
    slots = both[:, 6].astype(jnp.int32)

    weights = step_weights.astype(F32) / 100.0
    par = both.reshape(32)
    half = zh[None].astype(jnp.int32)
    matrix = jnp.asarray(x_matrix(), jnp.bfloat16)

    part = products(slots, fields, perts)
    orb, pot = orbital_rows(half, fields, perts)

    def swapped(value):
        return jnp.concatenate([value[36:], value[:36]], 0)

    part = part + swapped(z_xor(part, 1)) + z_xor(part, 2) + swapped(z_xor(part, 3))
    sums = [part] + [y_ring(part, by) for by in (1, 2, 3)]
    right, *cut = right_sides(float(ncells), slots, half, sums, fields, perts)
    u = right
    for count in range(1, ITERS):
        halos = exchange(*cut)
        u = inner_step(count, par, weights, u, right, pot, matrix, orb)
        if count < ITERS - 1:
            u, *cut = add_faces(count, par, weights, u, halos)
    u = density_pieces(par, weights, u, halos, orb)

    me = x * 2 + core
    piece = lax.dynamic_index_in_dim(u, me, 0, keepdims=False)
    for m in range(1, 8):
        send = lax.dynamic_index_in_dim(u, me ^ m, 0, keepdims=False)
        piece = piece + lax.ppermute(send, ("x", "c"), [(i, i ^ m) for i in range(8)])
    got = [piece]
    for m in (1, 2, 3):
        pairs = []
        for zz in range(4):
            to = zz ^ m
            c = to >> 1
            index = lambda w: (w & 1) * 4 + c * 2 + (w >> 1)
            pairs.append((index(zz), index(to)))
        got.append(lax.ppermute(piece, ("zl", "c", "zh"), pairs))
    slab = jnp.stack(got)
    same = core == zh
    blocks = []
    for d in range(4):
        index = lambda xx, c, h: xx * 4 + c * 2 + h
        across = lax.ppermute(slab, ("x", "c", "zh"), [(index(i, h, h), index(i ^ d, 1 - h, h)) for i in range(4) for h in range(2)])
        straight = slab
        if d:
            straight = lax.ppermute(slab, ("x", "c", "zh"), [(index(i, h, h), index(i ^ d, h, h)) for i in range(4) for h in range(2)])
        blocks.append(jnp.where(same, straight, across))
    return assemble(jnp.stack([x, z]).astype(jnp.int32), blocks)


def solution(mesh):
    fine = Mesh(mesh.devices.reshape(2, 4, 2, 4, 2), ("zl", "x", "c", "y", "zh"))
    ka, grid = ("zl", "x", "c"), ("y", "zh")
    return jax.shard_map(
        on_device,
        mesh=fine,
        in_specs=(
            P(ka, None, None, grid, None),
            P(ka),
            P(ka, None),
            P(ka, None),
            P(grid, None),
            P(None, grid, None),
            P(),
        ),
        out_specs=P(None, grid, None),
        check_vma=False,
    )
```

```python
import functools

import jax
import jax.numpy as jnp
import numpy as np
from jax import lax
from jax.experimental import pallas as pl
from jax.experimental.pallas import tpu as pltpu
from jax.sharding import Mesh
from jax.sharding import PartitionSpec as P

NX = 96
ITERS = 4
ROWS = 24
CHUNK = ROWS * NX
GROUP = 4 * NX
F32 = jnp.float32
ZAX = ("zl", "zh")


def z_perm(to):
    index = lambda z: (z & 1) * 2 + (z >> 1)
    return [(index(z), index(to(z))) for z in range(4)]


def z_xor(value, m):
    return lax.ppermute(value, ZAX, z_perm(lambda z: z ^ m))


def y_xor(value, m):
    return lax.ppermute(value, "y", [(i, i ^ m) for i in range(4)])


def lane_ids():
    return lax.broadcasted_iota(jnp.int32, (8, 128), 1)


def unpack_rows(a, b, c, lanes):
    r0 = a
    r1 = jnp.where(lanes < 32, pltpu.roll(a, 32, 1), pltpu.roll(b, 32, 1))
    r2 = jnp.where(lanes < 64, pltpu.roll(b, 64, 1), pltpu.roll(c, 64, 1))
    r3 = pltpu.roll(c, 96, 1)
    return r0, r1, r2, r3


def pack_rows(r0, r1, r2, r3, lanes):
    r1s = pltpu.roll(r1, 96, 1)
    r2s = pltpu.roll(r2, 64, 1)
    r3s = pltpu.roll(r3, 32, 1)
    return (
        jnp.where(lanes < 96, r0, r1s),
        jnp.where(lanes < 64, r1s, r2s),
        jnp.where(lanes < 32, r2s, r3s),
    )


def in_vmem(shape):
    return pltpu.VMEM(shape, F32)


def call(kernel, name, args, outs, scratch=(), scalars=0, aliases=None, flops=10_000_000, limit=8):
    specs = [pl.BlockSpec(memory_space=pltpu.SMEM)] * scalars
    specs += [pl.BlockSpec(memory_space=pltpu.VMEM)] * (len(args) - scalars)
    args = list(args[:scalars]) + [pltpu.with_memory_space_constraint(a, pltpu.VMEM) for a in args[scalars:]]
    return pl.pallas_call(
        kernel,
        in_specs=specs,
        out_specs=[pl.BlockSpec(memory_space=pltpu.VMEM)] * len(outs),
        out_shape=[in_vmem(o) for o in outs],
        scratch_shapes=list(scratch),
        input_output_aliases=aliases or {},
        compiler_params=pltpu.CompilerParams(vmem_limit_bytes=limit * 2**20),
        cost_estimate=pl.CostEstimate(flops=flops, bytes_accessed=10_000_000, transcendentals=0),
        name=name,
    )(*args)


def lanes_at(group, v):
    return pl.ds(pl.multiple_of(group * GROUP + v * 128, 128), 128)


def perturbed(field, pert_r, pert_i):
    re, im = field
    return pert_r * re - pert_i * im, pert_r * im + pert_i * re


def products_kernel(slot_ref, o0, o1, o2, o3, p0, p1, out_ref):
    slabs = (((o0, o1), p0), ((o2, o3), p1))
    for k in range(4):
        block, kk = k // 2, k % 2
        slot = slot_ref[k]

        def body(g, acc, block=block, kk=kk, slot=slot):
            acc = list(acc)
            for pair, pert in slabs:
                own, mate = pair[block], pair[1 - block]
                for v in range(3):
                    at = lanes_at(g, v)
                    pr, pi = pert[1, :, at], pert[2, :, at]
                    w = [perturbed((own[kk, n, 0, :, at], own[kk, n, 1, :, at]), pr, pi) for n in range(3)]
                    for m in range(3):
                        mr, mi = mate[slot, m, 0, :, at], mate[slot, m, 1, :, at]
                        for n in range(3):
                            i = (m * 3 + n) * 2
                            acc[i] = acc[i] + (mr * w[n][0] + mi * w[n][1])
                            acc[i + 1] = acc[i + 1] + (mr * w[n][1] - mi * w[n][0])
            return tuple(acc)

        acc = lax.fori_loop(0, CHUNK // GROUP, body, (jnp.zeros((8, 128), F32),) * 18)
        for i in range(18):
            out_ref[pl.ds(k * 18 + i, 1), :] = jnp.sum(acc[i], axis=0, keepdims=True)


def products(slots, fields, perts):
    return call(products_kernel, "products", (slots, *fields, *perts), [(72, 128)], scalars=1, flops=20_000_000)[0]


TALL, DEEP = ROWS + 4, 32
FIELD = (24, TALL, DEEP, 128)
ORBITALS = (24 * ROWS * 16, 128)


def rows_at(kn, c, r):
    return ((kn * 2 + c) * ROWS + r) * 16


def orbital_rows_kernel(pos_ref, o0, o1, o2, o3, p0, p1, orb_ref, v_ref):
    lanes = lane_ids()
    half = pos_ref[0]

    def body(g, carry):
        for pair, pert, z in (((o0, o1), p0, half), ((o2, o3), p1, 1 - half)):
            rows = unpack_rows(*[pert[0, :, lanes_at(g, v)] for v in range(3)], lanes)
            for j in range(4):
                v_ref[pl.ds(pl.multiple_of((4 * g + j) * 16 + 8 * z, 8), 8), :] = rows[j]
            for k in range(4):
                for n in range(3):
                    for c in range(2):
                        rows = unpack_rows(*[pair[k // 2][k % 2, n, c, :, lanes_at(g, v)] for v in range(3)], lanes)
                        for j in range(4):
                            at = pl.multiple_of(rows_at(k * 3 + n, c, 4 * g + j) + 8 * z, 8)
                            orb_ref[pl.ds(at, 8), :] = rows[j]
        return carry

    lax.fori_loop(0, CHUNK // GROUP, body, 0)


def orbital_rows(pos, fields, perts):
    return call(orbital_rows_kernel, "orbital_rows", (pos, *fields, *perts), [ORBITALS, (ROWS * 16, 128)], scalars=1)


ZHALO, YHALO = (48 * ROWS, 128), (24 * 32, 128)


def field_rows(kn, c, r, plane):
    return ((kn * 2 + c) * TALL + r + 2) * DEEP + 8 + plane


def clear_margin(u_ref):
    def body(i, carry):
        for r in (0, 1, TALL - 2, TALL - 1):
            u_ref[i, r] = jnp.zeros((DEEP, 128), F32)
        for r in range(2, TALL - 2):
            u_ref[i, r, 0:8] = jnp.zeros((8, 128), F32)
            u_ref[i, r, 24:32] = jnp.zeros((8, 128), F32)
        return carry

    lax.fori_loop(0, 24, body, 0)


def near_face(parity, size):
    return (1 - parity) * (size - 2)


def cut_planes(flat, pos_ref, kn, za, zb):
    up = near_face(pos_ref[4] & 1, 16)
    for ref, first in ((za, up), (zb, 14 - up)):
        for c in range(2):
            for p in range(2):
                to = pl.ds(pl.multiple_of(((kn * 2 + c) * 2 + p) * ROWS, 8), ROWS)
                ref[to, :] = flat[pl.ds(field_rows(kn, c, 0, first + p), ROWS, stride=DEEP), :]


def cut_rows(u_ref, pos_ref, kn, ya, yb):
    up = near_face(pos_ref[1] & 1, ROWS)
    for ref, first in ((ya, up), (yb, ROWS - 2 - up)):
        for c in range(2):
            i = kn * 2 + c
            for p in range(2):
                to = pl.ds(pl.multiple_of((i * 2 + p) * 16, 8), 16)
                ref[to, :] = u_ref[i, 2 + first + p, 8:24, :]


def exchange(za, zb, ya, yb):
    return y_xor(za, 1), y_xor(zb, 3), z_xor(ya, 1), z_xor(yb, 3)


def right_kernel(ncells, slot_ref, pos_ref, s0, s1, s2, s3, o0, o1, o2, o3, p0, p1, r_ref, za, zb, ya, yb, prod_ref):
    total = (s0[...] + s1[...]) + (s2[...] + s3[...])
    ones = jnp.full((128, 128), 1.0, F32)
    prod_ref[...] = jnp.dot(total, ones, precision=lax.Precision.HIGHEST, preferred_element_type=F32) / ncells
    clear_margin(r_ref)
    lanes = lane_ids()
    half = pos_ref[0]
    slabs = (((o0, o1), p0, half), ((o2, o3), p1, 1 - half))
    for k in range(4):
        block, kk = k // 2, k % 2
        slot = slot_ref[k]

        def body(g, carry, k=k, block=block, kk=kk, slot=slot):
            for pair, pert, z in slabs:
                own, mate = pair[block], pair[1 - block]
                right = [[[], []] for _ in range(3)]
                for v in range(3):
                    at = lanes_at(g, v)
                    pr, pi = pert[1, :, at], pert[2, :, at]
                    mates = [(mate[slot, m, 0, :, at], mate[slot, m, 1, :, at]) for m in range(3)]
                    for n in range(3):
                        wr, wi = perturbed((own[kk, n, 0, :, at], own[kk, n, 1, :, at]), pr, pi)
                        gr, gi = -wr, -wi
                        for m in range(3):
                            row = k * 18 + (m * 3 + n) * 2
                            qr = prod_ref[pl.ds(row, 1), :]
                            qi = prod_ref[pl.ds(row + 1, 1), :]
                            mr, mi = mates[m]
                            gr = gr + (qr * mr - qi * mi)
                            gi = gi + (qi * mr + qr * mi)
                        right[n][0].append(gr)
                        right[n][1].append(gi)
                for n in range(3):
                    for c in range(2):
                        rows = unpack_rows(*right[n][c], lanes)
                        for j in range(4):
                            planes = pl.ds(pl.multiple_of(8 + 8 * z, 8), 8)
                            r_ref[(k * 3 + n) * 2 + c, 2 + 4 * g + j, planes, :] = rows[j]
            return carry

        lax.fori_loop(0, CHUNK // GROUP, body, 0)

    flat = r_ref.reshape(24 * TALL * DEEP, 128)

    def cut(kn, carry):
        cut_planes(flat, pos_ref, kn, za, zb)
        cut_rows(r_ref, pos_ref, kn, ya, yb)
        return carry

    lax.fori_loop(0, 12, cut, 0)


def right_sides(ncells, slots, pos, sums, fields, perts):
    return call(
        functools.partial(right_kernel, ncells),
        "right_sides",
        (slots, pos, *sums, *fields, *perts),
        [FIELD, ZHALO, ZHALO, YHALO, YHALO],
        scratch=[pltpu.VMEM((72, 128), F32)],
        scalars=2,
        flops=20_000_000,
    )


def x_matrix():
    m = np.zeros((128, 256), np.float32)
    for i in range(NX):
        for s, lap, grad in ((1, 16, 8), (-1, 16, -8), (2, -1, -1), (-2, -1, 1)):
            m[(i + s) % NX, i] += lap
            m[(i + s) % NX, 128 + i] += grad
    return np.concatenate([m, m], 0)


def scalars_of(count, par_ref, w_ref, kn):
    k, n = kn // 3, kn % 3
    kx, ky, kz = par_ref[k * 8], par_ref[k * 8 + 1], par_ref[k * 8 + 2]
    base = 3.75 + 0.5 * (kx * kx + ky * ky + kz * kz) + par_ref[k * 8 + 3 + n]
    wt = w_ref[count]
    scale = w_ref[0] if count == 1 else jnp.float32(1.0)
    return kx, ky, kz, base, wt, scale


def step_kernel(count, par_ref, w_ref, *refs):
    last, first = count == ITERS - 1, count == 1
    if first:
        r_ref, v_ref, m_ref, *refs = refs
        u_ref = r_ref
    else:
        u_ref, r_ref, v_ref, m_ref, *refs = refs
    if last:
        orb_ref, out_ref, *flats = refs
        out_ref[...] = jnp.zeros_like(out_ref)
    else:
        out_ref, *flats = refs

    def along_x(kn, g, flat):
        cells = [u_ref[kn * 2 + c, 2 + 8 * g : 10 + 8 * g, 8:24, :].reshape(128, 128) for c in range(2)]
        u2 = jnp.concatenate(cells, 0)
        hi = u2.astype(jnp.bfloat16)
        lo = (u2 - hi.astype(F32)).astype(jnp.bfloat16)
        flat[...] = jnp.dot(jnp.concatenate([hi, lo], 1), m_ref[...], preferred_element_type=F32)

    def rows_of(kn, g, flat, coef):
        lap, gx, gy, gz, keep, pull, wt = coef
        for r in range(8 * g, 8 * g + 8):
            cells, second, grad = [], [], []
            for c in range(2):
                i = kn * 2 + c
                at = slice((c * 8 + r - 8 * g) * 16, (c * 8 + r - 8 * g + 1) * 16)
                yp1, ym1 = u_ref[i, r + 3, 8:24, :], u_ref[i, r + 1, 8:24, :]
                yp2, ym2 = u_ref[i, r + 4, 8:24, :], u_ref[i, r, 8:24, :]
                zp1, zm1 = u_ref[i, r + 2, 9:25, :], u_ref[i, r + 2, 7:23, :]
                zp2, zm2 = u_ref[i, r + 2, 10:26, :], u_ref[i, r + 2, 6:22, :]
                cells.append(u_ref[i, r + 2, 8:24, :])
                one = (yp1 + ym1) + (zp1 + zm1)
                two = (yp2 + ym2) + (zp2 + zm2)
                second.append(flat[at, 0:128] + (16.0 * one - two))
                dy = (yp1 - ym1) - 0.125 * (yp2 - ym2)
                dz = (zp1 - zm1) - 0.125 * (zp2 - zm2)
                grad.append(gx * flat[at, 128:256] + (gy * dy + gz * dz))
            center = keep - pull * v_ref[16 * r : 16 * r + 16, :]
            new = []
            for c in range(2):
                i = kn * 2 + c
                value = center * cells[c] + lap * second[c]
                if not first:
                    value = value + wt * r_ref[i, r + 2, 8:24, :]
                new.append(value - grad[1] if c == 0 else value + grad[0])
            if last:
                orb_r = orb_ref[pl.ds(pl.multiple_of(rows_at(kn, 0, r), 16), 16), :]
                orb_i = orb_ref[pl.ds(pl.multiple_of(rows_at(kn, 1, r), 16), 16), :]
                out_ref[16 * r : 16 * r + 16, :] += orb_r * new[0] + orb_i * new[1]
                out_ref[16 * (ROWS + r) : 16 * (ROWS + r) + 16, :] += orb_r * new[1] - orb_i * new[0]
            else:
                for c in range(2):
                    out_ref[pl.ds(pl.multiple_of(rows_at(kn, c, r), 16), 16), :] = new[c]

    along_x(0, 0, flats[0])

    def orbital(kn, carry):
        kx, ky, kz, base, wt, scale = scalars_of(count, par_ref, w_ref, kn)
        ws = wt * scale
        keep = scale - ws * base
        if first:
            keep = keep + wt
        coef = (ws / 24.0, ws * kx / 12.0, ws * ky * (2.0 / 3.0), ws * kz * (2.0 / 3.0), keep, ws, wt)
        ahead = jnp.minimum(kn + 1, 11)
        for g in range(3):
            along_x(kn if g < 2 else ahead, (g + 1) % 3, flats[(g + 1) % 3])
            rows_of(kn, g, flats[g], coef)
        return carry

    lax.fori_loop(0, 12, orbital, 0)


def inner_step(count, par, weights, u, right, pot, matrix, orb):
    last = count == ITERS - 1
    return call(
        functools.partial(step_kernel, count),
        "last_step" if last else "step",
        (par, weights) + ((u,) if count > 1 else ()) + (right, pot, matrix) + ((orb,) if last else ()),
        [(2 * ROWS * 16, 128) if last else ORBITALS],
        scratch=[pltpu.VMEM((256, 256), F32)] * 3,
        scalars=2,
        flops=60_000_000,
    )[0]


def face_terms(lap, g, beyond1, beyond2):
    first = [lap * (16.0 * beyond1[c] - beyond2[c]) for c in range(2)]
    grad1 = [g * (beyond1[c] - 0.125 * beyond2[c]) for c in range(2)]
    second = [-lap * beyond1[c] for c in range(2)]
    grad2 = [(-0.125 * g) * beyond1[c] for c in range(2)]
    return (
        (first[0] - grad1[1], first[1] + grad1[0]),
        (second[0] - grad2[1], second[1] + grad2[0]),
    )


def faces(count, par_ref, w_ref, pos_ref, kn, za, zb, ya, yb, add_plane, add_row):
    kx, ky, kz, base, wt, scale = scalars_of(count, par_ref, w_ref, kn)
    ws = wt * scale
    lap = ws / 24.0
    gy, gz = ws * ky * (2.0 / 3.0), ws * kz * (2.0 / 3.0)
    from_z = (kn + 6) % 12

    def plane(ref, p):
        return [ref[pl.ds(pl.multiple_of(((kn * 2 + c) * 2 + p) * ROWS, 8), ROWS), :] for c in range(2)]

    def line(ref, r):
        return [ref[pl.ds(pl.multiple_of(((from_z * 2 + c) * 2 + r) * 16, 8), 16), :] for c in range(2)]

    def side(ref, layer, size, g, below, add):
        sign = (1 - 2 * below).astype(F32)
        first = (1 - below) * (size - 1)
        terms = face_terms(lap, sign * g, layer(ref, below), layer(ref, 1 - below))
        add(first, terms[0])
        add(first + 2 * below - 1, terms[1])

    odd = pos_ref[1] & 1
    side(ya, line, ROWS, gy, odd, add_row)
    side(yb, line, ROWS, gy, 1 - odd, add_row)
    odd = pos_ref[4] & 1
    side(za, plane, 16, gz, odd, add_plane)
    side(zb, plane, 16, gz, 1 - odd, add_plane)


def faces_kernel(count, par_ref, w_ref, pos_ref, u_in, za_in, zb_in, ya_in, yb_in, u_ref, za, zb, ya, yb):
    clear_margin(u_ref)
    flat = u_ref.reshape(24 * TALL * DEEP, 128)

    def orbital(kn, carry):
        for c in range(2):
            for r in range(ROWS):
                u_ref[kn * 2 + c, r + 2, 8:24, :] = u_in[pl.ds(pl.multiple_of(rows_at(kn, c, r), 16), 16), :]

        def add_plane(p, term):
            for c in range(2):
                at = pl.ds(field_rows(kn, c, 0, p), ROWS, stride=DEEP)
                flat[at, :] = flat[at, :] + term[c]

        def add_row(r, term):
            for c in range(2):
                u_ref[kn * 2 + c, r + 2, 8:24, :] = u_ref[kn * 2 + c, r + 2, 8:24, :] + term[c]

        faces(count, par_ref, w_ref, pos_ref, kn, za_in, zb_in, ya_in, yb_in, add_plane, add_row)
        cut_planes(flat, pos_ref, kn, za, zb)
        cut_rows(u_ref, pos_ref, kn, ya, yb)
        return carry

    lax.fori_loop(0, 12, orbital, 0)


def add_faces(count, par, weights, pos, u, halos):
    return call(
        functools.partial(faces_kernel, count),
        "faces",
        (par, weights, pos, u, *halos),
        [FIELD, ZHALO, ZHALO, YHALO, YHALO],
        scalars=3,
    )


def density_kernel(par_ref, w_ref, pos_ref, d_in, za, zb, ya, yb, orb_ref, keep_ref, send_ref, d_ref):
    d_ref[...] = d_in[...]

    def orbital(kn, carry):
        def add(at, to, term):
            orb_r, orb_i = orb_ref[at[0], :], orb_ref[at[1], :]
            d_ref[to[0], :] = d_ref[to[0], :] + (orb_r * term[0] + orb_i * term[1])
            d_ref[to[1], :] = d_ref[to[1], :] + (orb_r * term[1] - orb_i * term[0])

        def add_plane(p, term):
            add(
                [pl.ds(rows_at(kn, c, 0) + p, ROWS, stride=16) for c in range(2)],
                [pl.ds(c * ROWS * 16 + p, ROWS, stride=16) for c in range(2)],
                term,
            )

        def add_row(r, term):
            add(
                [pl.ds(pl.multiple_of(rows_at(kn, c, r), 16), 16) for c in range(2)],
                [pl.ds(pl.multiple_of((c * ROWS + r) * 16, 16), 16) for c in range(2)],
                term,
            )

        faces(ITERS - 1, par_ref, w_ref, pos_ref, kn, za, zb, ya, yb, add_plane, add_row)
        return carry

    lax.fori_loop(0, 12, orbital, 0)
    ids = lane_ids()
    core = pos_ref[3]
    for ref, c in ((send_ref, 1 - core), (keep_ref, core)):
        for z in range(2):
            for g in range(6):
                rows = [
                    d_ref[pl.ds(pl.multiple_of((c * ROWS + 4 * g + j) * 16 + 8 * z, 8), 8), :] * (1.0 / 32.0)
                    for j in range(4)
                ]
                packed = pack_rows(*rows, ids)
                for v in range(3):
                    at = g * GROUP + v * 128
                    ref[z, :, at : at + 128] = packed[v]


TILE = (2, 8, CHUNK)


def tile_density(par, weights, pos, dens, halos, orb):
    return call(
        density_kernel,
        "density",
        (par, weights, pos, dens, *halos, orb),
        [TILE, TILE],
        scratch=[pltpu.VMEM((2 * ROWS * 16, 128), F32)],
        scalars=3,
    )


def pair_kernel(a, b, out):
    out[...] = a[...] + b[...]


def split_kernel(pos_ref, s0, s1, s2, s3, mine, other):
    half = pos_ref[0]
    mine[...] = (s0[half] + s1[half]) + (s2[half] + s3[half])
    half = 1 - half
    other[...] = (s0[half] + s1[half]) + (s2[half] + s3[half])


def place_kernel(pos_ref, t0, t1, t2, t3, out_ref):
    z = pos_ref[1]
    for m, tile in enumerate((t0, t1, t2, t3)):
        out_ref[:, pl.ds(pl.multiple_of((z ^ m) * CHUNK, 128), CHUNK)] = tile[...]


def both_kernel(pos_ref, mine, other, out_ref):
    core = pos_ref[3]
    out_ref[core] = mine[...]
    out_ref[1 - core] = other[...]


def both_components(pos, mine, other):
    return pl.pallas_call(
        both_kernel,
        in_specs=[pl.BlockSpec(memory_space=pltpu.SMEM)] + [pl.BlockSpec(memory_space=pltpu.VMEM)] * 2,
        out_specs=pl.BlockSpec(memory_space=pltpu.VMEM),
        out_shape=jax.ShapeDtypeStruct((2, 8, 4 * CHUNK), F32),
        compiler_params=pltpu.CompilerParams(vmem_limit_bytes=8 * 2**20),
        name="both_components",
    )(pos, mine, other)


def on_device(orbitals, partner_map, wave_vectors, levels, potential, perturbation, step_weights):
    zl, zh = lax.axis_index("zl"), lax.axis_index("zh")
    z = zh * 2 + zl
    pos = jnp.stack([zh, z, lax.axis_index("x"), lax.axis_index("c"), lax.axis_index("y")]).astype(jnp.int32)
    ncells = 64 * 4 * CHUNK

    def chunk(array, q):
        return lax.dynamic_slice_in_dim(array, q * CHUNK, CHUNK, axis=array.ndim - 1)

    fields = [None] * 4
    for m in (1, 3, 2):
        part = chunk(orbitals, z ^ m)
        fields[m] = z_xor(part, m)
        orbitals, part = lax.optimization_barrier((orbitals, part))
    partner_map, wave_vectors, levels, potential, perturbation, step_weights, part = lax.optimization_barrier(
        (partner_map, wave_vectors, levels, potential, perturbation, step_weights, part)
    )
    pots = jnp.concatenate([potential[None], perturbation], 0)
    perts = [chunk(pots, z), z_xor(chunk(pots, z ^ 3), 3)]
    slot = (partner_map % 2).astype(F32)
    mine = jnp.concatenate([wave_vectors, levels, slot[:, None], jnp.zeros((2, 1), F32)], 1)
    weights = step_weights.astype(F32) / 100.0
    both = jnp.concatenate([mine, z_xor(mine, 1)], 0)
    slots = both[:, 6].astype(jnp.int32)
    par = both.reshape(32)
    matrix = jnp.asarray(x_matrix(), jnp.bfloat16)
    pos, slots, par, weights, orbitals = lax.optimization_barrier((pos, slots, par, weights, orbitals))
    fields[0] = chunk(orbitals, z)
    pos, slots, par, weights, fields, perts = lax.optimization_barrier((pos, slots, par, weights, fields, perts))

    part = products(slots, fields, perts)
    orb, pot = orbital_rows(pos, fields, perts)

    def swapped(value):
        return jnp.concatenate([value[36:], value[:36]], 0)

    part = part + swapped(z_xor(part, 1)) + z_xor(part, 2) + swapped(z_xor(part, 3))
    sums = [part] + [y_xor(part, m) for m in (1, 2, 3)]
    orb, pot, sums = lax.optimization_barrier((orb, pot, sums))
    right, *cut = right_sides(float(ncells), slots, pos, sums, fields, perts)
    u = right
    for count in range(1, ITERS):
        halos = exchange(*cut)
        u = inner_step(count, par, weights, u, right, pot, matrix, orb)
        if count < ITERS - 1:
            u, *cut = add_faces(count, par, weights, pos, u, halos)
    keep, send = tile_density(par, weights, pos, u, halos, orb)

    def other_core(value):
        return lax.ppermute(value, "c", [(0, 1), (1, 0)])

    chip = call(pair_kernel, "pair", (keep, other_core(send)), [TILE])[0]
    parts = [chip] + [lax.ppermute(chip, "x", [(i, i ^ m) for i in range(4)]) for m in (1, 2, 3)]
    same, cross = call(split_kernel, "split", (pos, *parts), [(8, CHUNK)] * 2, scalars=1)
    tiles = [same, z_xor(same, 1), z_xor(cross, 2), z_xor(cross, 3)]
    slab = call(place_kernel, "place", (pos, *tiles), [(8, 4 * CHUNK)], scalars=1)[0]
    return both_components(pos, slab, other_core(slab))


def solution(mesh):
    fine = Mesh(mesh.devices.reshape(2, 4, 2, 4, 2), ("zl", "x", "c", "y", "zh"))
    ka, grid = ("zl", "x", "c"), ("y", "zh")
    return jax.shard_map(
        on_device,
        mesh=fine,
        in_specs=(
            P(ka, None, None, grid, None),
            P(ka),
            P(ka, None),
            P(ka, None),
            P(grid, None),
            P(None, grid, None),
            P(),
        ),
        out_specs=P(None, grid, None),
        check_vma=False,
    )
```

```python
import functools

import jax
import jax.numpy as jnp
import numpy as np
from jax import lax
from jax.experimental import pallas as pl
from jax.experimental.pallas import tpu as pltpu
from jax.sharding import Mesh
from jax.sharding import PartitionSpec as P


NX = 96
ITERS = 4
ROWS = 24
CHUNK = ROWS * NX
GROUP = 4 * NX
F32 = jnp.float32
ZAX = ("zl", "zh")


def z_perm(to):
    index = lambda z: (z & 1) * 2 + (z >> 1)
    return [(index(z), index(to(z))) for z in range(4)]


def z_xor(value, m):
    return lax.ppermute(value, ZAX, z_perm(lambda z: z ^ m))


def other_core(value):
    return lax.ppermute(value, "c", [(0, 1), (1, 0)])


def y_xor(value, m):
    return lax.ppermute(value, "y", [(i, i ^ m) for i in range(4)])


def lane_ids():
    return lax.broadcasted_iota(jnp.int32, (8, 128), 1)


def unpack_rows(a, b, c, lanes):
    r1 = pltpu.roll(jnp.where(lanes < 96, b, a), 32, 1)
    r2 = pltpu.roll(jnp.where(lanes < 64, c, b), 64, 1)
    r3 = pltpu.roll(c, 96, 1)
    return a, r1, r2, r3


def pack_rows(r0, r1, r2, r3, lanes):
    r1s = pltpu.roll(r1, 96, 1)
    r2s = pltpu.roll(r2, 64, 1)
    r3s = pltpu.roll(r3, 32, 1)
    return (
        jnp.where(lanes < 96, r0, r1s),
        jnp.where(lanes < 64, r1s, r2s),
        jnp.where(lanes < 32, r2s, r3s),
    )


def in_vmem(shape):
    return pltpu.VMEM(shape, F32)


def call(kernel, args, outs, scratch=(), scalars=0, aliases=None, flops=10_000_000, limit=8):
    specs = [pl.BlockSpec(memory_space=pltpu.SMEM)] * scalars
    specs += [pl.BlockSpec(memory_space=pltpu.VMEM)] * (len(args) - scalars)
    args = list(args[:scalars]) + [pltpu.with_memory_space_constraint(a, pltpu.VMEM) for a in args[scalars:]]
    return pl.pallas_call(
        kernel,
        in_specs=specs,
        out_specs=[pl.BlockSpec(memory_space=pltpu.VMEM)] * len(outs),
        out_shape=[in_vmem(o) for o in outs],
        scratch_shapes=list(scratch),
        input_output_aliases=aliases or {},
        compiler_params=pltpu.CompilerParams(vmem_limit_bytes=limit * 2**20),
        cost_estimate=pl.CostEstimate(flops=flops, bytes_accessed=10_000_000, transcendentals=0),
    )(*args)


def lanes_at(group, v, base=0):
    return pl.ds(pl.multiple_of(base + group * GROUP + v * 128, 128), 128)


HALF = CHUNK // 2
IN_HBM = pl.BlockSpec(memory_space=pltpu.HBM)


def rows_of_chunk(ref, z, extra=0, width=CHUNK):
    index = (slice(None),) * (len(ref.shape) - 1) + (pl.ds(pl.multiple_of(z * CHUNK + extra, 128), width),)
    return ref.at[index]


def cut_near_kernel(pos_ref, orb, pert, wave, level, partner, send3, send1, small, mine, wave_s, level_s, partner_s, sems):
    z, core = pos_ref[1], pos_ref[3]
    moves = [
        (wave, wave_s),
        (level, level_s),
        (partner, partner_s),
        (rows_of_chunk(pert, z ^ 3, core * HALF, HALF), small.at[:, :, pl.ds(0, HALF)]),
        (rows_of_chunk(orb, z ^ 3), send3),
        (rows_of_chunk(orb, z ^ 1), send1),
    ]
    copies = [pltpu.make_async_copy(source, target, sems.at[i]) for i, (source, target) in enumerate(moves)]
    for copy in copies:
        copy.start()
    rows = lax.broadcasted_iota(jnp.int32, (8, 128), 0)
    cols = lax.broadcasted_iota(jnp.int32, (8, 128), 1)
    out = jnp.zeros((8, 128), F32)
    for copy in copies[:3]:
        copy.wait()
    for k in range(2):
        values = [wave_s[k, d] for d in range(3)] + [level_s[k, n] for n in range(3)]
        values.append((partner_s[k] & 1).astype(F32))
        for j, value in enumerate(values):
            out = jnp.where((rows == k) & (cols == j), value, out)
    mine[...] = out
    small[0, :, HALF:] = out
    small[1, :, HALF:] = out
    for copy in copies[3:]:
        copy.wait()


def cut_near(pos, orbitals, perturbation, wave, level, partner_map):
    chunk = orbitals.shape[:-1] + (CHUNK,)
    return pl.pallas_call(
        cut_near_kernel,
        in_specs=[pl.BlockSpec(memory_space=pltpu.SMEM)] + [IN_HBM] * 5,
        out_specs=[pl.BlockSpec(memory_space=pltpu.VMEM)] * 4,
        out_shape=[in_vmem(chunk), in_vmem(chunk), in_vmem((2, 8, HALF + 128)), in_vmem((8, 128))],
        scratch_shapes=[
            pltpu.SMEM((2, 3), F32),
            pltpu.SMEM((2, 3), F32),
            pltpu.SMEM((2,), jnp.int32),
            pltpu.SemaphoreType.DMA((6,)),
        ],
        compiler_params=pltpu.CompilerParams(vmem_limit_bytes=4 * 2**20),
        name="cut_near",
    )(pos, *[pltpu.with_memory_space_constraint(a, pltpu.HBM) for a in (orbitals, perturbation, wave, level, partner_map)])


def cut_far_kernel(pos_ref, orb, pot, after, send2, pot_send, sems):
    z = pos_ref[1]
    moves = ((rows_of_chunk(orb, z ^ 2), send2), (rows_of_chunk(pot, z ^ 3), pot_send))
    copies = [pltpu.make_async_copy(source, target, sems.at[i]) for i, (source, target) in enumerate(moves)]
    for copy in copies:
        copy.start()
    for copy in copies:
        copy.wait()


def cut_far(pos, orbitals, potential, after):
    return pl.pallas_call(
        cut_far_kernel,
        in_specs=[pl.BlockSpec(memory_space=pltpu.SMEM), IN_HBM, IN_HBM, pl.BlockSpec(memory_space=pl.ANY)],
        out_specs=[pl.BlockSpec(memory_space=pltpu.VMEM)] * 2,
        out_shape=[in_vmem(orbitals.shape[:-1] + (CHUNK,)), in_vmem((8, CHUNK))],
        scratch_shapes=[pltpu.SemaphoreType.DMA((2,))],
        compiler_params=pltpu.CompilerParams(vmem_limit_bytes=4 * 2**20),
        name="cut_far",
    )(pos, *[pltpu.with_memory_space_constraint(a, pltpu.HBM) for a in (orbitals, potential)], after)


def perturbed(field, pert_r, pert_i):
    re, im = field
    return pert_r * re - pert_i * im, pert_r * im + pert_i * re


def join_halves(pos_ref, got, swap, joined):
    core = pos_ref[3]
    joined[:, :, pl.ds(pl.multiple_of(core * HALF, 128), HALF)] = got[:, :, :HALF]
    joined[:, :, pl.ds(pl.multiple_of((1 - core) * HALF, 128), HALF)] = swap[:, :, :HALF]


def products_kernel(near, pos_ref, slot_ref, o0, o1, *refs):
    if near:
        pert, out_ref = refs
        base = pos_ref[1] * CHUNK
    else:
        got, swap, near_ref, out_ref, pert = refs
        join_halves(pos_ref, got, swap, pert)
        base = 0
    pair, bases = (o0, o1), (base, 0)
    for k in range(4):
        block, kk = k // 2, k % 2
        slot = slot_ref[k]

        def body(g, acc, block=block, kk=kk, slot=slot):
            acc = list(acc)
            own, mate = pair[block], pair[1 - block]
            for v in range(3):
                at, mate_at, pert_at = (lanes_at(g, v, start) for start in (bases[block], bases[1 - block], base))
                pr, pi = pert[0, :, pert_at], pert[1, :, pert_at]
                w = [perturbed((own[kk, n, 0, :, at], own[kk, n, 1, :, at]), pr, pi) for n in range(3)]
                for m in range(3):
                    mr, mi = mate[slot, m, 0, :, mate_at], mate[slot, m, 1, :, mate_at]
                    for n in range(3):
                        i = (m * 3 + n) * 2
                        acc[i] = acc[i] + (mr * w[n][0] + mi * w[n][1])
                        acc[i + 1] = acc[i + 1] + (mr * w[n][1] - mi * w[n][0])
            return tuple(acc)

        acc = lax.fori_loop(0, CHUNK // GROUP, body, (jnp.zeros((8, 128), F32),) * 18)
        for i in range(18):
            at = pl.ds(block * 40 + kk * 18 + i, 1)
            value = jnp.sum(acc[i], axis=0, keepdims=True)
            out_ref[at, :] = value if near else near_ref[at, :] + value
    for block in range(2):
        out_ref[block * 40 + 36 : block * 40 + 40, :] = jnp.zeros((4, 128), F32)


def products(pos, slots, o0, o1, *pert):
    near = len(pert) == 1
    return call(
        functools.partial(products_kernel, near),
        (pos, slots, o0, o1, *pert),
        [(80, 128)],
        scratch=() if near else [pltpu.VMEM((2, 8, CHUNK), F32)],
        scalars=2,
        flops=20_000_000,
    )[0]


TALL, DEEP = ROWS + 4, 32
FIELD = (24, TALL, DEEP, 128)
ORBITALS = (24 * ROWS * 16, 128)


def rows_at(kn, c, r):
    return ((kn * 2 + c) * ROWS + r) * 16


def orbital_rows_kernel(pos_ref, o0, o1, o2, o3, pot, pot1, orb_ref, v_ref):
    lanes = lane_ids()
    half = pos_ref[0]

    def body(g, carry):
        for pair, pot_ref, z, base in (((o0, o1), pot, half, pos_ref[1] * CHUNK), ((o2, o3), pot1, 1 - half, 0)):
            rows = unpack_rows(*[pot_ref[:, lanes_at(g, v, base)] for v in range(3)], lanes)
            for j in range(4):
                v_ref[pl.ds(pl.multiple_of((4 * g + j) * 16 + 8 * z, 8), 8), :] = rows[j]
            for k in range(4):
                start = base if k < 2 else 0
                for n in range(3):
                    for c in range(2):
                        cells = [pair[k // 2][k % 2, n, c, :, lanes_at(g, v, start)] for v in range(3)]
                        rows = unpack_rows(*cells, lanes)
                        for j in range(4):
                            at = pl.multiple_of(rows_at(k * 3 + n, c, 4 * g + j) + 8 * z, 8)
                            orb_ref[pl.ds(at, 8), :] = rows[j]
        return carry

    lax.fori_loop(0, CHUNK // GROUP, body, 0)


def orbital_rows(pos, fields, pots):
    return call(orbital_rows_kernel, (pos, *fields, *pots), [ORBITALS, (ROWS * 16, 128)], scalars=1)


ZHALO, YHALO = (48 * ROWS, 128), (24 * 32, 128)


def field_rows(kn, c, r, plane):
    return ((kn * 2 + c) * TALL + r + 2) * DEEP + 8 + plane


def clear_margin(u_ref, kn):
    for i in (kn * 2, kn * 2 + 1):
        for r in (0, 1, TALL - 2, TALL - 1):
            u_ref[i, r] = jnp.zeros((DEEP, 128), F32)
        for r in range(2, TALL - 2):
            u_ref[i, r, 0:8] = jnp.zeros((8, 128), F32)
            u_ref[i, r, 24:32] = jnp.zeros((8, 128), F32)


def near_face(parity, size):
    return (1 - parity) * (size - 2)


def cut_planes(flat, pos_ref, kn, za, zb):
    up = near_face(pos_ref[4] & 1, 16)
    for ref, first in ((za, up), (zb, 14 - up)):
        for c in range(2):
            for p in range(2):
                to = pl.ds(pl.multiple_of(((kn * 2 + c) * 2 + p) * ROWS, 8), ROWS)
                ref[to, :] = flat[pl.ds(field_rows(kn, c, 0, first + p), ROWS, stride=DEEP), :]


def cut_rows(u_ref, pos_ref, kn, ya, yb):
    up = near_face(pos_ref[1] & 1, ROWS)
    for ref, first in ((ya, up), (yb, ROWS - 2 - up)):
        for c in range(2):
            i = kn * 2 + c
            for p in range(2):
                to = pl.ds(pl.multiple_of((i * 2 + p) * 16, 8), 16)
                ref[to, :] = u_ref[i, 2 + first + p, 8:24, :]


def exchange(za, zb, ya, yb):
    return y_xor(za, 1), y_xor(zb, 3), z_xor(ya, 1), z_xor(yb, 3)


def right_kernel(ncells, slot_ref, pos_ref, s0, s1, s2, s3, o0, o1, o2, o3, pert0, got, swap, r_ref, za, zb, ya, yb, prod_ref, pert1):
    join_halves(pos_ref, got, swap, pert1)
    total = (s0[...] + s1[...]) + (s2[...] + s3[...])
    ones = jnp.full((128, 128), 1.0, F32)
    prod_ref[...] = jnp.dot(total, ones, precision=lax.Precision.HIGHEST, preferred_element_type=F32) / ncells
    lanes = lane_ids()
    half = pos_ref[0]
    slabs = (((o0, o1), pert0, half, pos_ref[1] * CHUNK), ((o2, o3), pert1, 1 - half, 0))
    for k in range(4):
        block, kk = k // 2, k % 2
        slot = slot_ref[k]

        def body(g, carry, k=k, block=block, kk=kk, slot=slot):
            for pair, pert, z, base in slabs:
                own, mate = pair[block], pair[1 - block]
                own_base, mate_base = (base, 0) if block == 0 else (0, base)
                right = [[[], []] for _ in range(3)]
                for v in range(3):
                    at, mate_at, pert_at = (lanes_at(g, v, start) for start in (own_base, mate_base, base))
                    pr, pi = pert[0, :, pert_at], pert[1, :, pert_at]
                    mates = [(mate[slot, m, 0, :, mate_at], mate[slot, m, 1, :, mate_at]) for m in range(3)]
                    for n in range(3):
                        wr, wi = perturbed((own[kk, n, 0, :, at], own[kk, n, 1, :, at]), pr, pi)
                        gr, gi = -wr, -wi
                        for m in range(3):
                            row = block * 40 + kk * 18 + (m * 3 + n) * 2
                            qr = prod_ref[pl.ds(row, 1), :]
                            qi = prod_ref[pl.ds(row + 1, 1), :]
                            mr, mi = mates[m]
                            gr = gr + (qr * mr - qi * mi)
                            gi = gi + (qi * mr + qr * mi)
                        right[n][0].append(gr)
                        right[n][1].append(gi)
                for n in range(3):
                    for c in range(2):
                        rows = unpack_rows(*right[n][c], lanes)
                        for j in range(4):
                            planes = pl.ds(pl.multiple_of(8 + 8 * z, 8), 8)
                            r_ref[(k * 3 + n) * 2 + c, 2 + 4 * g + j, planes, :] = rows[j]
            return carry

        lax.fori_loop(0, CHUNK // GROUP, body, 0)

    flat = r_ref.reshape(24 * TALL * DEEP, 128)

    def cut(kn, carry):
        clear_margin(r_ref, kn)
        cut_planes(flat, pos_ref, kn, za, zb)
        cut_rows(r_ref, pos_ref, kn, ya, yb)
        return carry

    lax.fori_loop(0, 12, cut, 0)


def right_sides(ncells, slots, pos, sums, fields, perts):
    return call(
        functools.partial(right_kernel, ncells),
        (slots, pos, *sums, *fields, *perts),
        [FIELD, ZHALO, ZHALO, YHALO, YHALO],
        scratch=[pltpu.VMEM((80, 128), F32), pltpu.VMEM((2, 8, CHUNK), F32)],
        scalars=2,
        flops=20_000_000,
    )


def x_matrix():
    m = np.zeros((128, 256), np.float32)
    for i in range(NX):
        for s, lap, grad in ((1, 16, 8), (-1, 16, -8), (2, -1, -1), (-2, -1, 1)):
            m[(i + s) % NX, i] += lap
            m[(i + s) % NX, 128 + i] += grad
    return np.concatenate([m, m], 0)


def scalars_of(count, par_ref, w_ref, kn):
    k, n = kn // 3, kn % 3
    kx, ky, kz = par_ref[k, 0], par_ref[k, 1], par_ref[k, 2]
    base = 3.75 + 0.5 * (kx * kx + ky * ky + kz * kz) + par_ref[k, 3 + n]
    wt = w_ref[count]
    scale = w_ref[0] if count == 1 else jnp.float32(1.0)
    return kx, ky, kz, base, wt, scale


def step_kernel(count, par_ref, w_ref, *refs):
    last, first = count == ITERS - 1, count == 1
    if first:
        r_ref, v_ref, m_ref, *refs = refs
        u_ref = r_ref
    else:
        u_ref, r_ref, v_ref, m_ref, *refs = refs
    if last:
        orb_ref, out_ref, *flats = refs
        out_ref[...] = jnp.zeros_like(out_ref)
    else:
        out_ref, *flats = refs

    def along_x(kn, g, flat):
        cells = [u_ref[kn * 2 + c, 2 + 8 * g : 10 + 8 * g, 8:24, :].reshape(128, 128) for c in range(2)]
        u2 = jnp.concatenate(cells, 0)
        hi = u2.astype(jnp.bfloat16)
        lo = (u2 - hi.astype(F32)).astype(jnp.bfloat16)
        flat[...] = jnp.dot(jnp.concatenate([hi, lo], 1), m_ref[...], preferred_element_type=F32)

    def rows_of(kn, g, flat, coef):
        lap, gx, gy, gz, keep, pull, wt = coef
        for r in range(8 * g, 8 * g + 8):
            cells, second, grad = [], [], []
            for c in range(2):
                i = kn * 2 + c
                at = slice((c * 8 + r - 8 * g) * 16, (c * 8 + r - 8 * g + 1) * 16)
                yp1, ym1 = u_ref[i, r + 3, 8:24, :], u_ref[i, r + 1, 8:24, :]
                yp2, ym2 = u_ref[i, r + 4, 8:24, :], u_ref[i, r, 8:24, :]
                zp1, zm1 = u_ref[i, r + 2, 9:25, :], u_ref[i, r + 2, 7:23, :]
                zp2, zm2 = u_ref[i, r + 2, 10:26, :], u_ref[i, r + 2, 6:22, :]
                cells.append(u_ref[i, r + 2, 8:24, :])
                one = (yp1 + ym1) + (zp1 + zm1)
                two = (yp2 + ym2) + (zp2 + zm2)
                second.append(flat[at, 0:128] + (16.0 * one - two))
                dy = (yp1 - ym1) - 0.125 * (yp2 - ym2)
                dz = (zp1 - zm1) - 0.125 * (zp2 - zm2)
                grad.append(gx * flat[at, 128:256] + (gy * dy + gz * dz))
            center = keep - pull * v_ref[16 * r : 16 * r + 16, :]
            new = []
            for c in range(2):
                i = kn * 2 + c
                value = center * cells[c] + lap * second[c]
                if not first:
                    value = value + wt * r_ref[i, r + 2, 8:24, :]
                new.append(value - grad[1] if c == 0 else value + grad[0])
            if last:
                orb_r = orb_ref[pl.ds(pl.multiple_of(rows_at(kn, 0, r), 16), 16), :]
                orb_i = orb_ref[pl.ds(pl.multiple_of(rows_at(kn, 1, r), 16), 16), :]
                out_ref[16 * r : 16 * r + 16, :] += orb_r * new[0] + orb_i * new[1]
                out_ref[16 * (ROWS + r) : 16 * (ROWS + r) + 16, :] += orb_r * new[1] - orb_i * new[0]
            else:
                for c in range(2):
                    out_ref[pl.ds(pl.multiple_of(rows_at(kn, c, r), 16), 16), :] = new[c]

    along_x(0, 0, flats[0])

    def orbital(kn, carry):
        kx, ky, kz, base, wt, scale = scalars_of(count, par_ref, w_ref, kn)
        ws = wt * scale
        keep = scale - ws * base
        if first:
            keep = keep + wt
        coef = (ws / 24.0, ws * kx / 12.0, ws * ky * (2.0 / 3.0), ws * kz * (2.0 / 3.0), keep, ws, wt)
        ahead = jnp.minimum(kn + 1, 11)
        for g in range(3):
            along_x(kn if g < 2 else ahead, (g + 1) % 3, flats[(g + 1) % 3])
            rows_of(kn, g, flats[g], coef)
        return carry

    lax.fori_loop(0, 12, orbital, 0)


def inner_step(count, par, weights, u, right, pot, matrix, orb):
    last = count == ITERS - 1
    return call(
        functools.partial(step_kernel, count),
        (par, weights) + ((u,) if count > 1 else ()) + (right, pot, matrix) + ((orb,) if last else ()),
        [(2 * ROWS * 16, 128) if last else ORBITALS],
        scratch=[pltpu.VMEM((256, 256), F32)] * 3,
        scalars=2,
        flops=60_000_000,
    )[0]


def face_terms(lap, g, beyond1, beyond2):
    first = [lap * (16.0 * beyond1[c] - beyond2[c]) for c in range(2)]
    grad1 = [g * (beyond1[c] - 0.125 * beyond2[c]) for c in range(2)]
    second = [-lap * beyond1[c] for c in range(2)]
    grad2 = [(-0.125 * g) * beyond1[c] for c in range(2)]
    return (
        (first[0] - grad1[1], first[1] + grad1[0]),
        (second[0] - grad2[1], second[1] + grad2[0]),
    )


def faces(count, par_ref, w_ref, pos_ref, kn, za, zb, ya, yb, add_plane, add_row):
    _, ky, kz, _, wt, scale = scalars_of(count, par_ref, w_ref, kn)
    ws = wt * scale
    lap = ws / 24.0
    gy, gz = ws * ky * (2.0 / 3.0), ws * kz * (2.0 / 3.0)
    from_z = (kn + 6) % 12

    def plane(ref, p):
        return [ref[pl.ds(pl.multiple_of(((kn * 2 + c) * 2 + p) * ROWS, 8), ROWS), :] for c in range(2)]

    def line(ref, r):
        return [ref[pl.ds(pl.multiple_of(((from_z * 2 + c) * 2 + r) * 16, 8), 16), :] for c in range(2)]

    def side(ref, layer, size, g, below, add, which):
        sign = (1 - 2 * below).astype(F32)
        first = (1 - below) * (size - 1)
        terms = face_terms(lap, sign * g, layer(ref, below), layer(ref, 1 - below))
        add(first, terms[0], which, 1 - below)
        add(first + 2 * below - 1, terms[1], which, below)

    odd = pos_ref[1] & 1
    side(ya, line, ROWS, gy, odd, add_row, 0)
    side(yb, line, ROWS, gy, 1 - odd, add_row, 1)
    odd = pos_ref[4] & 1
    side(za, plane, 16, gz, odd, add_plane, 0)
    side(zb, plane, 16, gz, 1 - odd, add_plane, 1)


def faces_kernel(count, par_ref, w_ref, pos_ref, u_in, za_in, zb_in, ya_in, yb_in, u_ref, za, zb, ya, yb):
    flat = u_ref.reshape(24 * TALL * DEEP, 128)

    def orbital(kn, carry):
        clear_margin(u_ref, kn)
        for c in range(2):
            for r in range(ROWS):
                u_ref[kn * 2 + c, r + 2, 8:24, :] = u_in[pl.ds(pl.multiple_of(rows_at(kn, c, r), 16), 16), :]

        def add_plane(p, term, which, place):
            for c in range(2):
                at = pl.ds(field_rows(kn, c, 0, p), ROWS, stride=DEEP)
                value = flat[at, :] + term[c]
                flat[at, :] = value
                to = pl.ds(pl.multiple_of(((kn * 2 + c) * 2 + place) * ROWS, 8), ROWS)
                (za, zb)[which][to, :] = value

        def add_row(r, term, which, place):
            for c in range(2):
                u_ref[kn * 2 + c, r + 2, 8:24, :] = u_ref[kn * 2 + c, r + 2, 8:24, :] + term[c]

        faces(count, par_ref, w_ref, pos_ref, kn, za_in, zb_in, ya_in, yb_in, add_plane, add_row)
        cut_rows(u_ref, pos_ref, kn, ya, yb)
        return carry

    lax.fori_loop(0, 12, orbital, 0)


def add_faces(count, par, weights, pos, u, halos):
    return call(
        functools.partial(faces_kernel, count),
        (par, weights, pos, u, *halos),
        [FIELD, ZHALO, ZHALO, YHALO, YHALO],
        scalars=3,
    )


def density_kernel(par_ref, w_ref, pos_ref, d_in, za, zb, ya, yb, orb_ref, keep_ref, send_ref, d_ref):
    d_ref[...] = d_in[...]

    def orbital(kn, carry):
        def add(at, to, term):
            orb_r, orb_i = orb_ref[at[0], :], orb_ref[at[1], :]
            d_ref[to[0], :] = d_ref[to[0], :] + (orb_r * term[0] + orb_i * term[1])
            d_ref[to[1], :] = d_ref[to[1], :] + (orb_r * term[1] - orb_i * term[0])

        def add_plane(p, term, which, place):
            add(
                [pl.ds(rows_at(kn, c, 0) + p, ROWS, stride=16) for c in range(2)],
                [pl.ds(c * ROWS * 16 + p, ROWS, stride=16) for c in range(2)],
                term,
            )

        def add_row(r, term, which, place):
            add(
                [pl.ds(pl.multiple_of(rows_at(kn, c, r), 16), 16) for c in range(2)],
                [pl.ds(pl.multiple_of((c * ROWS + r) * 16, 16), 16) for c in range(2)],
                term,
            )

        faces(ITERS - 1, par_ref, w_ref, pos_ref, kn, za, zb, ya, yb, add_plane, add_row)
        return carry

    lax.fori_loop(0, 12, orbital, 0)
    ids = lane_ids()
    core = pos_ref[3]
    for ref, c in ((send_ref, 1 - core), (keep_ref, core)):
        for z in range(2):
            for g in range(6):
                rows = [
                    d_ref[pl.ds(pl.multiple_of((c * ROWS + 4 * g + j) * 16 + 8 * z, 8), 8), :] * (1.0 / 32.0)
                    for j in range(4)
                ]
                packed = pack_rows(*rows, ids)
                for v in range(3):
                    at = g * GROUP + v * 128
                    ref[z, :, at : at + 128] = packed[v]


TILE = (2, 8, CHUNK)


def tile_density(par, weights, pos, dens, halos, orb):
    return call(
        density_kernel,
        (par, weights, pos, dens, *halos, orb),
        [TILE, TILE],
        scratch=[pltpu.VMEM((2 * ROWS * 16, 128), F32)],
        scalars=3,
    )


def pair_kernel(a, b, out):
    out[...] = a[...] + b[...]


def split_kernel(pos_ref, s0, s1, s2, s3, mine, other):
    half = pos_ref[0]
    mine[...] = (s0[half] + s1[half]) + (s2[half] + s3[half])
    half = 1 - half
    other[...] = (s0[half] + s1[half]) + (s2[half] + s3[half])


def place_kernel(pos_ref, t0, t1, t2, t3, out_ref):
    z = pos_ref[1]
    for m, tile in enumerate((t0, t1, t2, t3)):
        out_ref[:, pl.ds(pl.multiple_of((z ^ m) * CHUNK, 128), CHUNK)] = tile[...]


def both_kernel(pos_ref, mine, other, out_ref):
    core = pos_ref[3]
    out_ref[core] = mine[...]
    out_ref[1 - core] = other[...]


def both_components(pos, mine, other):
    return pl.pallas_call(
        both_kernel,
        in_specs=[pl.BlockSpec(memory_space=pltpu.SMEM)] + [pl.BlockSpec(memory_space=pltpu.VMEM)] * 2,
        out_specs=pl.BlockSpec(memory_space=pltpu.VMEM),
        out_shape=jax.ShapeDtypeStruct((2, 8, 4 * CHUNK), F32),
        compiler_params=pltpu.CompilerParams(vmem_limit_bytes=8 * 2**20),
        name="both_components",
    )(pos, mine, other)


def program(orbitals, partner_map, wave_vectors, levels, potential, perturbation, step_weights):
    zl, zh = lax.axis_index("zl"), lax.axis_index("zh")
    z = zh * 2 + zl
    pos = jnp.stack([zh, z, lax.axis_index("x"), lax.axis_index("c"), lax.axis_index("y")]).astype(jnp.int32)
    ncells = 64 * 4 * CHUNK
    matrix = jnp.asarray(x_matrix(), jnp.bfloat16)

    send3, send1, small, mine = cut_near(pos, orbitals, perturbation, wave_vectors, levels, partner_map)
    got = z_xor(small, 3)
    o3 = z_xor(send3, 3)
    o1 = z_xor(send1, 1)
    send2, pot_send = cut_far(pos, orbitals, potential, send1)
    o2 = z_xor(send2, 2)
    pot1 = z_xor(pot_send, 3)
    swap = other_core(got)
    par = jnp.concatenate([mine[:2, :8], got[0, :2, HALF : HALF + 8]], 0)
    slots = par[:, 6].astype(jnp.int32)
    weights = step_weights.astype(F32) / 100.0

    fields, pert = [orbitals, o1, o2, o3], (perturbation, got, swap)
    part = products(pos, slots, orbitals, o1, perturbation)
    part = products(pos, slots, o2, o3, got, swap, part)
    orb, pot = orbital_rows(pos, fields, (potential, pot1))

    def swapped(value):
        return jnp.concatenate([value[40:], value[:40]], 0)

    part = part + swapped(z_xor(part, 1)) + z_xor(part, 2) + swapped(z_xor(part, 3))
    sums = [part] + [y_xor(part, m) for m in (1, 2, 3)]
    orb, pot, sums = lax.optimization_barrier((orb, pot, sums))
    right, *edge = right_sides(float(ncells), slots, pos, sums, fields, pert)
    u = right
    for count in range(1, ITERS):
        halos = exchange(*edge)
        u = inner_step(count, par, weights, u, right, pot, matrix, orb)
        if count < ITERS - 1:
            u, *edge = add_faces(count, par, weights, pos, u, halos)
    keep, send = tile_density(par, weights, pos, u, halos, orb)

    chip = call(pair_kernel, (keep, other_core(send)), [TILE])[0]
    parts = [chip] + [lax.ppermute(chip, "x", [(i, i ^ m) for i in range(4)]) for m in (1, 2, 3)]
    same, cross = call(split_kernel, (pos, *parts), [(8, CHUNK)] * 2, scalars=1)
    tiles = [same, z_xor(same, 1), z_xor(cross, 2), z_xor(cross, 3)]
    slab = call(place_kernel, (pos, *tiles), [(8, 4 * CHUNK)], scalars=1)[0]
    return both_components(pos, slab, other_core(slab))


def solution(mesh):
    fine = Mesh(mesh.devices.reshape(2, 4, 2, 4, 2), ("zl", "x", "c", "y", "zh"))
    ka, grid = ("zl", "x", "c"), ("y", "zh")
    return jax.shard_map(
        program,
        mesh=fine,
        in_specs=(
            P(ka, None, None, grid, None),
            P(ka),
            P(ka, None),
            P(ka, None),
            P(grid, None),
            P(None, grid, None),
            P(),
        ),
        out_specs=P(None, grid, None),
        check_vma=False,
    )
```

```python
import functools

import jax
import jax.numpy as jnp
import numpy as np
from jax import lax
from jax.experimental import pallas as pl
from jax.experimental.pallas import tpu as pltpu
from jax.sharding import Mesh
from jax.sharding import PartitionSpec as P


NX = 96
ITERS = 4
ROWS = 24
CHUNK = ROWS * NX
GROUP = 4 * NX
F32 = jnp.float32
ZAX = ("zl", "zh")


def z_perm(to):
    index = lambda z: (z & 1) * 2 + (z >> 1)
    return [(index(z), index(to(z))) for z in range(4)]


def z_xor(value, m):
    return lax.ppermute(value, ZAX, z_perm(lambda z: z ^ m))


def other_core(value):
    return lax.ppermute(value, "c", [(0, 1), (1, 0)])


def y_xor(value, m):
    return lax.ppermute(value, "y", [(i, i ^ m) for i in range(4)])


def lane_ids():
    return lax.broadcasted_iota(jnp.int32, (8, 128), 1)


def unpack_rows(a, b, c, lanes):
    r1 = pltpu.roll(jnp.where(lanes < 96, b, a), 32, 1)
    r2 = pltpu.roll(jnp.where(lanes < 64, c, b), 64, 1)
    r3 = pltpu.roll(c, 96, 1)
    return a, r1, r2, r3


def pack_rows(r0, r1, r2, r3, lanes):
    r1s = pltpu.roll(r1, 96, 1)
    r2s = pltpu.roll(r2, 64, 1)
    r3s = pltpu.roll(r3, 32, 1)
    return (
        jnp.where(lanes < 96, r0, r1s),
        jnp.where(lanes < 64, r1s, r2s),
        jnp.where(lanes < 32, r2s, r3s),
    )


def in_vmem(shape):
    return pltpu.VMEM(shape, F32)


def call(kernel, args, outs, scratch=(), scalars=0, aliases=None, flops=10_000_000, limit=8):
    specs = [pl.BlockSpec(memory_space=pltpu.SMEM)] * scalars
    specs += [pl.BlockSpec(memory_space=pltpu.VMEM)] * (len(args) - scalars)
    args = list(args[:scalars]) + [pltpu.with_memory_space_constraint(a, pltpu.VMEM) for a in args[scalars:]]
    return pl.pallas_call(
        kernel,
        in_specs=specs,
        out_specs=[pl.BlockSpec(memory_space=pltpu.VMEM)] * len(outs),
        out_shape=[in_vmem(o) for o in outs],
        scratch_shapes=list(scratch),
        input_output_aliases=aliases or {},
        compiler_params=pltpu.CompilerParams(vmem_limit_bytes=limit * 2**20),
        cost_estimate=pl.CostEstimate(flops=flops, bytes_accessed=10_000_000, transcendentals=0),
    )(*args)


def lanes_at(group, v, base=0):
    return pl.ds(pl.multiple_of(base + group * GROUP + v * 128, 128), 128)


HALF = CHUNK // 2
IN_HBM = pl.BlockSpec(memory_space=pltpu.HBM)


def rows_of_chunk(ref, z, extra=0, width=CHUNK):
    index = (slice(None),) * (len(ref.shape) - 1) + (pl.ds(pl.multiple_of(z * CHUNK + extra, 128), width),)
    return ref.at[index]


def cut_near_kernel(pos_ref, orb, pert, pot, wave, level, partner, send3, send1, small, mine, wave_s, level_s, partner_s, sems):
    z, core = pos_ref[1], pos_ref[3]
    moves = [
        (wave, wave_s),
        (level, level_s),
        (partner, partner_s),
        (rows_of_chunk(pert, z ^ 3, core * HALF, HALF), small.at[pl.ds(0, 2), :, pl.ds(0, HALF)]),
        (rows_of_chunk(pot, z ^ 3, core * HALF, HALF), small.at[2, :, pl.ds(0, HALF)]),
        (rows_of_chunk(orb, z ^ 3), send3),
        (rows_of_chunk(orb, z ^ 1), send1),
    ]
    copies = [pltpu.make_async_copy(source, target, sems.at[i]) for i, (source, target) in enumerate(moves)]
    for copy in copies:
        copy.start()
    rows = lax.broadcasted_iota(jnp.int32, (8, 128), 0)
    cols = lax.broadcasted_iota(jnp.int32, (8, 128), 1)
    out = jnp.zeros((8, 128), F32)
    for copy in copies[:3]:
        copy.wait()
    for k in range(2):
        values = [wave_s[k, d] for d in range(3)] + [level_s[k, n] for n in range(3)]
        values.append((partner_s[k] & 1).astype(F32))
        for j, value in enumerate(values):
            out = jnp.where((rows == k) & (cols == j), value, out)
    mine[...] = out
    for i in range(3):
        small[i, :, HALF:] = out
    for copy in copies[3:]:
        copy.wait()


def cut_near(pos, orbitals, perturbation, potential, wave, level, partner_map):
    chunk = orbitals.shape[:-1] + (CHUNK,)
    return pl.pallas_call(
        cut_near_kernel,
        in_specs=[pl.BlockSpec(memory_space=pltpu.SMEM)] + [IN_HBM] * 6,
        out_specs=[pl.BlockSpec(memory_space=pltpu.VMEM)] * 4,
        out_shape=[in_vmem(chunk), in_vmem(chunk), in_vmem((3, 8, HALF + 128)), in_vmem((8, 128))],
        scratch_shapes=[
            pltpu.SMEM((2, 3), F32),
            pltpu.SMEM((2, 3), F32),
            pltpu.SMEM((2,), jnp.int32),
            pltpu.SemaphoreType.DMA((7,)),
        ],
        compiler_params=pltpu.CompilerParams(vmem_limit_bytes=4 * 2**20),
        name="cut_near",
    )(pos, *[pltpu.with_memory_space_constraint(a, pltpu.HBM) for a in (orbitals, perturbation, potential, wave, level, partner_map)])


def cut_far_kernel(pos_ref, orb, after, send2, sem):
    copy = pltpu.make_async_copy(rows_of_chunk(orb, pos_ref[1] ^ 2), send2, sem)
    copy.start()
    copy.wait()


def cut_far(pos, orbitals, after):
    return pl.pallas_call(
        cut_far_kernel,
        in_specs=[pl.BlockSpec(memory_space=pltpu.SMEM), IN_HBM, pl.BlockSpec(memory_space=pl.ANY)],
        out_specs=pl.BlockSpec(memory_space=pltpu.VMEM),
        out_shape=in_vmem(orbitals.shape[:-1] + (CHUNK,)),
        scratch_shapes=[pltpu.SemaphoreType.DMA],
        compiler_params=pltpu.CompilerParams(vmem_limit_bytes=4 * 2**20),
        name="cut_far",
    )(pos, pltpu.with_memory_space_constraint(orbitals, pltpu.HBM), after)


def perturbed(field, pert_r, pert_i):
    re, im = field
    return pert_r * re - pert_i * im, pert_r * im + pert_i * re


def join_halves(pos_ref, got, swap, joined, fields):
    core = pos_ref[3]
    for to, i in enumerate(fields):
        joined[to, :, pl.ds(pl.multiple_of(core * HALF, 128), HALF)] = got[i, :, :HALF]
        joined[to, :, pl.ds(pl.multiple_of((1 - core) * HALF, 128), HALF)] = swap[i, :, :HALF]


def products_kernel(near, pos_ref, slot_ref, o0, o1, *refs):
    if near:
        pert, out_ref = refs
        base = pos_ref[1] * CHUNK
    else:
        got, swap, near_ref, out_ref, pert = refs
        join_halves(pos_ref, got, swap, pert, (0, 1))
        base = 0
    pair, bases = (o0, o1), (base, 0)
    for k in range(4):
        block, kk = k // 2, k % 2
        slot = slot_ref[k]

        def body(g, acc, block=block, kk=kk, slot=slot):
            acc = list(acc)
            own, mate = pair[block], pair[1 - block]
            for v in range(3):
                at, mate_at, pert_at = (lanes_at(g, v, start) for start in (bases[block], bases[1 - block], base))
                pr, pi = pert[0, :, pert_at], pert[1, :, pert_at]
                w = [perturbed((own[kk, n, 0, :, at], own[kk, n, 1, :, at]), pr, pi) for n in range(3)]
                for m in range(3):
                    mr, mi = mate[slot, m, 0, :, mate_at], mate[slot, m, 1, :, mate_at]
                    for n in range(3):
                        i = (m * 3 + n) * 2
                        acc[i] = acc[i] + (mr * w[n][0] + mi * w[n][1])
                        acc[i + 1] = acc[i + 1] + (mr * w[n][1] - mi * w[n][0])
            return tuple(acc)

        acc = lax.fori_loop(0, CHUNK // GROUP, body, (jnp.zeros((8, 128), F32),) * 18)
        for i in range(18):
            at = pl.ds(block * 40 + kk * 18 + i, 1)
            value = jnp.sum(acc[i], axis=0, keepdims=True)
            out_ref[at, :] = value if near else near_ref[at, :] + value
    for block in range(2):
        out_ref[block * 40 + 36 : block * 40 + 40, :] = jnp.zeros((4, 128), F32)


def products(pos, slots, o0, o1, *pert):
    near = len(pert) == 1
    return call(
        functools.partial(products_kernel, near),
        (pos, slots, o0, o1, *pert),
        [(80, 128)],
        scratch=() if near else [pltpu.VMEM((2, 8, CHUNK), F32)],
        scalars=2,
        flops=20_000_000,
    )[0]


TALL, DEEP = ROWS + 4, 24
FIELD = (24, TALL, DEEP, 128)
ORBITALS = (24 * ROWS * 16, 128)


def rows_at(kn, c, r):
    return ((kn * 2 + c) * ROWS + r) * 16


def orbital_rows_kernel(pos_ref, o0, o1, o2, o3, pot, got, swap, orb_ref, v_ref, joined):
    join_halves(pos_ref, got, swap, joined, (2,))
    pot1 = joined.at[0]
    lanes = lane_ids()
    half = pos_ref[0]

    def body(g, carry):
        for pair, pot_ref, z, base in (((o0, o1), pot, half, pos_ref[1] * CHUNK), ((o2, o3), pot1, 1 - half, 0)):
            rows = unpack_rows(*[pot_ref[:, lanes_at(g, v, base)] for v in range(3)], lanes)
            for j in range(4):
                v_ref[pl.ds(pl.multiple_of((4 * g + j) * 16 + 8 * z, 8), 8), :] = rows[j]
            for k in range(4):
                start = base if k < 2 else 0
                for n in range(3):
                    for c in range(2):
                        cells = [pair[k // 2][k % 2, n, c, :, lanes_at(g, v, start)] for v in range(3)]
                        rows = unpack_rows(*cells, lanes)
                        for j in range(4):
                            at = pl.multiple_of(rows_at(k * 3 + n, c, 4 * g + j) + 8 * z, 8)
                            orb_ref[pl.ds(at, 8), :] = rows[j]
        return carry

    lax.fori_loop(0, CHUNK // GROUP, body, 0)


def orbital_rows(pos, fields, pots):
    return call(orbital_rows_kernel, (pos, *fields, *pots), [ORBITALS, (ROWS * 16, 128)], scratch=[pltpu.VMEM((1, 8, CHUNK), F32)], scalars=1)


ZHALO, YHALO = (48 * ROWS, 128), (24 * 32, 128)


def field_rows(kn, c, r, plane):
    return ((kn * 2 + c) * TALL + r + 2) * DEEP + 4 + plane


def clear_margin(u_ref, kn):
    for i in (kn * 2, kn * 2 + 1):
        for r in (0, 1, TALL - 2, TALL - 1):
            u_ref[i, r] = jnp.zeros((DEEP, 128), F32)
        for r in range(2, TALL - 2):
            u_ref[i, r, 0:4] = jnp.zeros((4, 128), F32)
            u_ref[i, r, 20:24] = jnp.zeros((4, 128), F32)


def near_face(parity, size):
    return (1 - parity) * (size - 2)


def cut_planes(flat, pos_ref, kn, za, zb):
    up = near_face(pos_ref[4] & 1, 16)
    for ref, first in ((za, up), (zb, 14 - up)):
        for c in range(2):
            for p in range(2):
                to = pl.ds(pl.multiple_of(((kn * 2 + c) * 2 + p) * ROWS, 8), ROWS)
                ref[to, :] = flat[pl.ds(field_rows(kn, c, 0, first + p), ROWS, stride=DEEP), :]


def cut_rows(u_ref, pos_ref, kn, ya, yb):
    up = near_face(pos_ref[1] & 1, ROWS)
    for ref, first in ((ya, up), (yb, ROWS - 2 - up)):
        for c in range(2):
            i = kn * 2 + c
            for p in range(2):
                to = pl.ds(pl.multiple_of((i * 2 + p) * 16, 8), 16)
                ref[to, :] = u_ref[i, 2 + first + p, 4:20, :]


def exchange(za, zb, ya, yb):
    return y_xor(za, 1), y_xor(zb, 3), z_xor(ya, 1), z_xor(yb, 3)


def right_kernel(ncells, slot_ref, pos_ref, s0, s1, s2, s3, o0, o1, o2, o3, pert0, got, swap, r_ref, za, zb, ya, yb, prod_ref, pert1):
    join_halves(pos_ref, got, swap, pert1, (0, 1))
    total = (s0[...] + s1[...]) + (s2[...] + s3[...])
    ones = jnp.full((128, 128), 1.0, F32)
    prod_ref[...] = jnp.dot(total, ones, precision=lax.Precision.HIGHEST, preferred_element_type=F32) / ncells
    lanes = lane_ids()
    half = pos_ref[0]
    slabs = (((o0, o1), pert0, half, pos_ref[1] * CHUNK), ((o2, o3), pert1, 1 - half, 0))
    for k in range(4):
        block, kk = k // 2, k % 2
        slot = slot_ref[k]

        def body(g, carry, k=k, block=block, kk=kk, slot=slot):
            for pair, pert, z, base in slabs:
                own, mate = pair[block], pair[1 - block]
                own_base, mate_base = (base, 0) if block == 0 else (0, base)
                right = [[[], []] for _ in range(3)]
                for v in range(3):
                    at, mate_at, pert_at = (lanes_at(g, v, start) for start in (own_base, mate_base, base))
                    pr, pi = pert[0, :, pert_at], pert[1, :, pert_at]
                    mates = [(mate[slot, m, 0, :, mate_at], mate[slot, m, 1, :, mate_at]) for m in range(3)]
                    for n in range(3):
                        wr, wi = perturbed((own[kk, n, 0, :, at], own[kk, n, 1, :, at]), pr, pi)
                        gr, gi = -wr, -wi
                        for m in range(3):
                            row = block * 40 + kk * 18 + (m * 3 + n) * 2
                            qr = prod_ref[pl.ds(row, 1), :]
                            qi = prod_ref[pl.ds(row + 1, 1), :]
                            mr, mi = mates[m]
                            gr = gr + (qr * mr - qi * mi)
                            gi = gi + (qi * mr + qr * mi)
                        right[n][0].append(gr)
                        right[n][1].append(gi)
                for n in range(3):
                    for c in range(2):
                        rows = unpack_rows(*right[n][c], lanes)
                        for j in range(4):
                            planes = pl.ds(4 + 8 * z, 8)
                            r_ref[(k * 3 + n) * 2 + c, 2 + 4 * g + j, planes, :] = rows[j]
            return carry

        lax.fori_loop(0, CHUNK // GROUP, body, 0)

    flat = r_ref.reshape(24 * TALL * DEEP, 128)

    def cut(kn, carry):
        clear_margin(r_ref, kn)
        cut_planes(flat, pos_ref, kn, za, zb)
        cut_rows(r_ref, pos_ref, kn, ya, yb)
        return carry

    lax.fori_loop(0, 12, cut, 0)


def right_sides(ncells, slots, pos, sums, fields, perts):
    return call(
        functools.partial(right_kernel, ncells),
        (slots, pos, *sums, *fields, *perts),
        [FIELD, ZHALO, ZHALO, YHALO, YHALO],
        scratch=[pltpu.VMEM((80, 128), F32), pltpu.VMEM((2, 8, CHUNK), F32)],
        scalars=2,
        flops=20_000_000,
    )


def x_matrix():
    m = np.zeros((128, 256), np.float32)
    for i in range(NX):
        for s, lap, grad in ((1, 16, 8), (-1, 16, -8), (2, -1, -1), (-2, -1, 1)):
            m[(i + s) % NX, i] += lap
            m[(i + s) % NX, 128 + i] += grad
    return np.concatenate([m, m], 0)


def scalars_of(count, par_ref, w_ref, kn):
    k, n = kn // 3, kn % 3
    kx, ky, kz = par_ref[k, 0], par_ref[k, 1], par_ref[k, 2]
    base = 3.75 + 0.5 * (kx * kx + ky * ky + kz * kz) + par_ref[k, 3 + n]
    wt = w_ref[count]
    scale = w_ref[0] if count == 1 else jnp.float32(1.0)
    return kx, ky, kz, base, wt, scale


def step_kernel(count, par_ref, w_ref, *refs):
    last, first = count == ITERS - 1, count == 1
    if first:
        r_ref, v_ref, m_ref, *refs = refs
        u_ref = r_ref
    else:
        u_ref, r_ref, v_ref, m_ref, *refs = refs
    if last:
        orb_ref, out_ref, *flats = refs
        out_ref[...] = jnp.zeros_like(out_ref)
    else:
        out_ref, *flats = refs

    def along_x(kn, g, flat):
        cells = [u_ref[kn * 2 + c, 2 + 8 * g : 10 + 8 * g, 4:20, :].reshape(128, 128) for c in range(2)]
        u2 = jnp.concatenate(cells, 0)
        hi = u2.astype(jnp.bfloat16)
        lo = (u2 - hi.astype(F32)).astype(jnp.bfloat16)
        flat[...] = jnp.dot(jnp.concatenate([hi, lo], 1), m_ref[...], preferred_element_type=F32)

    def rows_of(kn, g, flat, coef):
        lap, gx, gy, gz, keep, pull, wt = coef
        for r in range(8 * g, 8 * g + 8):
            cells, second, grad = [], [], []
            for c in range(2):
                i = kn * 2 + c
                at = slice((c * 8 + r - 8 * g) * 16, (c * 8 + r - 8 * g + 1) * 16)
                yp1, ym1 = u_ref[i, r + 3, 4:20, :], u_ref[i, r + 1, 4:20, :]
                yp2, ym2 = u_ref[i, r + 4, 4:20, :], u_ref[i, r, 4:20, :]
                zp1, zm1 = u_ref[i, r + 2, 5:21, :], u_ref[i, r + 2, 3:19, :]
                zp2, zm2 = u_ref[i, r + 2, 6:22, :], u_ref[i, r + 2, 2:18, :]
                cells.append(u_ref[i, r + 2, 4:20, :])
                one = (yp1 + ym1) + (zp1 + zm1)
                two = (yp2 + ym2) + (zp2 + zm2)
                second.append(flat[at, 0:128] + (16.0 * one - two))
                dy = (yp1 - ym1) - 0.125 * (yp2 - ym2)
                dz = (zp1 - zm1) - 0.125 * (zp2 - zm2)
                grad.append(gx * flat[at, 128:256] + (gy * dy + gz * dz))
            center = keep - pull * v_ref[16 * r : 16 * r + 16, :]
            new = []
            for c in range(2):
                i = kn * 2 + c
                value = center * cells[c] + lap * second[c]
                if not first:
                    value = value + wt * r_ref[i, r + 2, 4:20, :]
                new.append(value - grad[1] if c == 0 else value + grad[0])
            if last:
                orb_r = orb_ref[pl.ds(pl.multiple_of(rows_at(kn, 0, r), 16), 16), :]
                orb_i = orb_ref[pl.ds(pl.multiple_of(rows_at(kn, 1, r), 16), 16), :]
                out_ref[16 * r : 16 * r + 16, :] += orb_r * new[0] + orb_i * new[1]
                out_ref[16 * (ROWS + r) : 16 * (ROWS + r) + 16, :] += orb_r * new[1] - orb_i * new[0]
            else:
                for c in range(2):
                    out_ref[pl.ds(pl.multiple_of(rows_at(kn, c, r), 16), 16), :] = new[c]

    along_x(0, 0, flats[0])

    def orbital(kn, carry):
        kx, ky, kz, base, wt, scale = scalars_of(count, par_ref, w_ref, kn)
        ws = wt * scale
        keep = scale - ws * base
        if first:
            keep = keep + wt
        coef = (ws / 24.0, ws * kx / 12.0, ws * ky * (2.0 / 3.0), ws * kz * (2.0 / 3.0), keep, ws, wt)
        ahead = jnp.minimum(kn + 1, 11)
        for g in range(3):
            along_x(kn if g < 2 else ahead, (g + 1) % 3, flats[(g + 1) % 3])
            rows_of(kn, g, flats[g], coef)
        return carry

    lax.fori_loop(0, 12, orbital, 0)


def inner_step(count, par, weights, u, right, pot, matrix, orb):
    last = count == ITERS - 1
    return call(
        functools.partial(step_kernel, count),
        (par, weights) + ((u,) if count > 1 else ()) + (right, pot, matrix) + ((orb,) if last else ()),
        [(2 * ROWS * 16, 128) if last else ORBITALS],
        scratch=[pltpu.VMEM((256, 256), F32)] * 3,
        scalars=2,
        flops=60_000_000,
    )[0]


def face_terms(lap, g, beyond1, beyond2):
    first = [lap * (16.0 * beyond1[c] - beyond2[c]) for c in range(2)]
    grad1 = [g * (beyond1[c] - 0.125 * beyond2[c]) for c in range(2)]
    second = [-lap * beyond1[c] for c in range(2)]
    grad2 = [(-0.125 * g) * beyond1[c] for c in range(2)]
    return (
        (first[0] - grad1[1], first[1] + grad1[0]),
        (second[0] - grad2[1], second[1] + grad2[0]),
    )


def faces(count, par_ref, w_ref, pos_ref, kn, za, zb, ya, yb, add_plane, add_row):
    _, ky, kz, _, wt, scale = scalars_of(count, par_ref, w_ref, kn)
    ws = wt * scale
    lap = ws / 24.0
    gy, gz = ws * ky * (2.0 / 3.0), ws * kz * (2.0 / 3.0)
    from_z = (kn + 6) % 12

    def plane(ref, p):
        return [ref[pl.ds(pl.multiple_of(((kn * 2 + c) * 2 + p) * ROWS, 8), ROWS), :] for c in range(2)]

    def line(ref, r):
        return [ref[pl.ds(pl.multiple_of(((from_z * 2 + c) * 2 + r) * 16, 8), 16), :] for c in range(2)]

    def side(ref, layer, size, g, below, add, which):
        sign = (1 - 2 * below).astype(F32)
        first = (1 - below) * (size - 1)
        terms = face_terms(lap, sign * g, layer(ref, below), layer(ref, 1 - below))
        add(first, terms[0], which, 1 - below)
        add(first + 2 * below - 1, terms[1], which, below)

    odd = pos_ref[1] & 1
    side(ya, line, ROWS, gy, odd, add_row, 0)
    side(yb, line, ROWS, gy, 1 - odd, add_row, 1)
    odd = pos_ref[4] & 1
    side(za, plane, 16, gz, odd, add_plane, 0)
    side(zb, plane, 16, gz, 1 - odd, add_plane, 1)


def faces_kernel(count, par_ref, w_ref, pos_ref, u_in, za_in, zb_in, ya_in, yb_in, u_ref, za, zb, ya, yb):
    flat = u_ref.reshape(24 * TALL * DEEP, 128)

    def orbital(kn, carry):
        clear_margin(u_ref, kn)
        for c in range(2):
            for r in range(ROWS):
                u_ref[kn * 2 + c, r + 2, 4:20, :] = u_in[pl.ds(pl.multiple_of(rows_at(kn, c, r), 16), 16), :]

        def add_plane(p, term, which, place):
            for c in range(2):
                at = pl.ds(field_rows(kn, c, 0, p), ROWS, stride=DEEP)
                value = flat[at, :] + term[c]
                flat[at, :] = value
                to = pl.ds(pl.multiple_of(((kn * 2 + c) * 2 + place) * ROWS, 8), ROWS)
                (za, zb)[which][to, :] = value

        def add_row(r, term, which, place):
            for c in range(2):
                u_ref[kn * 2 + c, r + 2, 4:20, :] = u_ref[kn * 2 + c, r + 2, 4:20, :] + term[c]

        faces(count, par_ref, w_ref, pos_ref, kn, za_in, zb_in, ya_in, yb_in, add_plane, add_row)
        cut_rows(u_ref, pos_ref, kn, ya, yb)
        return carry

    lax.fori_loop(0, 12, orbital, 0)


def add_faces(count, par, weights, pos, u, halos):
    return call(
        functools.partial(faces_kernel, count),
        (par, weights, pos, u, *halos),
        [FIELD, ZHALO, ZHALO, YHALO, YHALO],
        scalars=3,
    )


def density_kernel(par_ref, w_ref, pos_ref, d_in, za, zb, ya, yb, orb_ref, keep_ref, send_ref, d_ref):
    d_ref[...] = d_in[...]

    def orbital(kn, carry):
        def add(at, to, term):
            orb_r, orb_i = orb_ref[at[0], :], orb_ref[at[1], :]
            d_ref[to[0], :] = d_ref[to[0], :] + (orb_r * term[0] + orb_i * term[1])
            d_ref[to[1], :] = d_ref[to[1], :] + (orb_r * term[1] - orb_i * term[0])

        def add_plane(p, term, which, place):
            add(
                [pl.ds(rows_at(kn, c, 0) + p, ROWS, stride=16) for c in range(2)],
                [pl.ds(c * ROWS * 16 + p, ROWS, stride=16) for c in range(2)],
                term,
            )

        def add_row(r, term, which, place):
            add(
                [pl.ds(pl.multiple_of(rows_at(kn, c, r), 16), 16) for c in range(2)],
                [pl.ds(pl.multiple_of((c * ROWS + r) * 16, 16), 16) for c in range(2)],
                term,
            )

        faces(ITERS - 1, par_ref, w_ref, pos_ref, kn, za, zb, ya, yb, add_plane, add_row)
        return carry

    lax.fori_loop(0, 12, orbital, 0)
    ids = lane_ids()
    core = pos_ref[3]
    for ref, c in ((send_ref, 1 - core), (keep_ref, core)):
        for z in range(2):
            for g in range(6):
                rows = [
                    d_ref[pl.ds(pl.multiple_of((c * ROWS + 4 * g + j) * 16 + 8 * z, 8), 8), :] * (1.0 / 32.0)
                    for j in range(4)
                ]
                packed = pack_rows(*rows, ids)
                for v in range(3):
                    at = g * GROUP + v * 128
                    ref[z, :, at : at + 128] = packed[v]


TILE = (2, 8, CHUNK)


def tile_density(par, weights, pos, dens, halos, orb):
    return call(
        density_kernel,
        (par, weights, pos, dens, *halos, orb),
        [TILE, TILE],
        scratch=[pltpu.VMEM((2 * ROWS * 16, 128), F32)],
        scalars=3,
    )


def pair_kernel(a, b, out):
    out[...] = a[...] + b[...]


def split_kernel(pos_ref, s0, s1, s2, s3, mine, other):
    half = pos_ref[0]
    mine[...] = (s0[half] + s1[half]) + (s2[half] + s3[half])
    half = 1 - half
    other[...] = (s0[half] + s1[half]) + (s2[half] + s3[half])


def place_kernel(pos_ref, t0, t1, t2, t3, out_ref):
    z = pos_ref[1]
    for m, tile in enumerate((t0, t1, t2, t3)):
        out_ref[:, pl.ds(pl.multiple_of((z ^ m) * CHUNK, 128), CHUNK)] = tile[...]


def both_kernel(pos_ref, mine, other, out_ref):
    core = pos_ref[3]
    out_ref[core] = mine[...]
    out_ref[1 - core] = other[...]


def both_components(pos, mine, other):
    return pl.pallas_call(
        both_kernel,
        in_specs=[pl.BlockSpec(memory_space=pltpu.SMEM)] + [pl.BlockSpec(memory_space=pltpu.VMEM)] * 2,
        out_specs=pl.BlockSpec(memory_space=pltpu.VMEM),
        out_shape=jax.ShapeDtypeStruct((2, 8, 4 * CHUNK), F32),
        compiler_params=pltpu.CompilerParams(vmem_limit_bytes=8 * 2**20),
        name="both_components",
    )(pos, mine, other)


def program(orbitals, partner_map, wave_vectors, levels, potential, perturbation, step_weights):
    zl, zh = lax.axis_index("zl"), lax.axis_index("zh")
    z = zh * 2 + zl
    pos = jnp.stack([zh, z, lax.axis_index("x"), lax.axis_index("c"), lax.axis_index("y")]).astype(jnp.int32)
    ncells = 64 * 4 * CHUNK
    matrix = jnp.asarray(x_matrix(), jnp.bfloat16)

    send3, send1, small, mine = cut_near(pos, orbitals, perturbation, potential, wave_vectors, levels, partner_map)
    got = z_xor(small, 3)
    o3 = z_xor(send3, 3)
    o1 = z_xor(send1, 1)
    send2 = cut_far(pos, orbitals, send1)
    o2 = z_xor(send2, 2)
    swap = other_core(got)
    par = jnp.concatenate([mine[:2, :8], got[0, :2, HALF : HALF + 8]], 0)
    slots = par[:, 6].astype(jnp.int32)
    weights = step_weights.astype(F32) / 100.0

    fields, pert = [orbitals, o1, o2, o3], (perturbation, got, swap)
    part = products(pos, slots, orbitals, o1, perturbation)
    part = products(pos, slots, o2, o3, got, swap, part)
    orb, pot = orbital_rows(pos, fields, (potential, got, swap))

    def swapped(value):
        return jnp.concatenate([value[40:], value[:40]], 0)

    part = part + swapped(z_xor(part, 1)) + z_xor(part, 2) + swapped(z_xor(part, 3))
    sums = [part] + [y_xor(part, m) for m in (1, 2, 3)]
    orb, pot, sums = lax.optimization_barrier((orb, pot, sums))
    right, *edge = right_sides(float(ncells), slots, pos, sums, fields, pert)
    u = right
    for count in range(1, ITERS):
        halos = exchange(*edge)
        u = inner_step(count, par, weights, u, right, pot, matrix, orb)
        if count < ITERS - 1:
            u, *edge = add_faces(count, par, weights, pos, u, halos)
    keep, send = tile_density(par, weights, pos, u, halos, orb)

    chip = call(pair_kernel, (keep, other_core(send)), [TILE])[0]
    parts = [chip] + [lax.ppermute(chip, "x", [(i, i ^ m) for i in range(4)]) for m in (1, 2, 3)]
    same, cross = call(split_kernel, (pos, *parts), [(8, CHUNK)] * 2, scalars=1)
    tiles = [same, z_xor(same, 1), z_xor(cross, 2), z_xor(cross, 3)]
    slab = call(place_kernel, (pos, *tiles), [(8, 4 * CHUNK)], scalars=1)[0]
    return both_components(pos, slab, other_core(slab))


def solution(mesh):
    fine = Mesh(mesh.devices.reshape(2, 4, 2, 4, 2), ("zl", "x", "c", "y", "zh"))
    ka, grid = ("zl", "x", "c"), ("y", "zh")
    return jax.shard_map(
        program,
        mesh=fine,
        in_specs=(
            P(ka, None, None, grid, None),
            P(ka),
            P(ka, None),
            P(ka, None),
            P(grid, None),
            P(None, grid, None),
            P(),
        ),
        out_specs=P(None, grid, None),
        check_vma=False,
    )
```

```python
import functools

import jax
import jax.numpy as jnp
import numpy as np
from jax import lax
from jax.experimental import pallas as pl
from jax.experimental.pallas import tpu as pltpu
from jax.sharding import Mesh
from jax.sharding import PartitionSpec as P


NX = 96
ITERS = 4
ROWS = 24
CHUNK = ROWS * NX
GROUP = 4 * NX
F32 = jnp.float32
ZAX = ("zl", "zh")


def z_perm(to):
    index = lambda z: (z & 1) * 2 + (z >> 1)
    return [(index(z), index(to(z))) for z in range(4)]


def z_xor(value, m):
    return lax.ppermute(value, ZAX, z_perm(lambda z: z ^ m))


def other_core(value):
    return lax.ppermute(value, "c", [(0, 1), (1, 0)])


def x_xor(value, m):
    return lax.ppermute(value, "x", [(i, i ^ m) for i in range(4)])


def y_xor(value, m):
    return lax.ppermute(value, "y", [(i, i ^ m) for i in range(4)])


def lane_ids():
    return lax.broadcasted_iota(jnp.int32, (8, 128), 1)


def unpack_rows(a, b, c, lanes):
    r1 = pltpu.roll(jnp.where(lanes < 96, b, a), 32, 1)
    r2 = pltpu.roll(jnp.where(lanes < 64, c, b), 64, 1)
    r3 = pltpu.roll(c, 96, 1)
    return a, r1, r2, r3


def pack_rows(r0, r1, r2, r3, lanes):
    r1s = pltpu.roll(r1, 96, 1)
    r2s = pltpu.roll(r2, 64, 1)
    r3s = pltpu.roll(r3, 32, 1)
    return (
        jnp.where(lanes < 96, r0, r1s),
        jnp.where(lanes < 64, r1s, r2s),
        jnp.where(lanes < 32, r2s, r3s),
    )


def in_vmem(shape):
    return pltpu.VMEM(shape, F32)


def call(kernel, args, outs, scratch=(), scalars=0, aliases=None, flops=10_000_000, limit=8):
    specs = [pl.BlockSpec(memory_space=pltpu.SMEM)] * scalars
    specs += [pl.BlockSpec(memory_space=pltpu.VMEM)] * (len(args) - scalars)
    args = list(args[:scalars]) + [pltpu.with_memory_space_constraint(a, pltpu.VMEM) for a in args[scalars:]]
    return pl.pallas_call(
        kernel,
        in_specs=specs,
        out_specs=[pl.BlockSpec(memory_space=pltpu.VMEM)] * len(outs),
        out_shape=[in_vmem(o) for o in outs],
        scratch_shapes=list(scratch),
        input_output_aliases=aliases or {},
        compiler_params=pltpu.CompilerParams(vmem_limit_bytes=limit * 2**20),
        cost_estimate=pl.CostEstimate(flops=flops, bytes_accessed=10_000_000, transcendentals=0),
    )(*args)


def lanes_at(group, v, base=0):
    return pl.ds(pl.multiple_of(base + group * GROUP + v * 128, 128), 128)


HALF = CHUNK // 2
IN_HBM = pl.BlockSpec(memory_space=pltpu.HBM)


def rows_of_chunk(ref, z, extra=0, width=CHUNK):
    index = (slice(None),) * (len(ref.shape) - 1) + (pl.ds(pl.multiple_of(z * CHUNK + extra, 128), width),)
    return ref.at[index]


def cut_kernel(pos_ref, orb, pert, pot, wave, level, partner, send3, send1, send2, small, mine, wave_s, level_s, partner_s, sems):
    z, core = pos_ref[1], pos_ref[3]
    moves = [
        (wave, wave_s),
        (level, level_s),
        (partner, partner_s),
        (rows_of_chunk(orb, z ^ 3), send3),
        (rows_of_chunk(orb, z ^ 1), send1),
        (rows_of_chunk(orb, z ^ 2), send2),
    ]
    copies = [pltpu.make_async_copy(source, target, sems.at[i]) for i, (source, target) in enumerate(moves)]
    for copy in copies:
        copy.start()
    field = small.at[:, pl.ds(0, HALF)]
    of_pert = rows_of_chunk(pert, z ^ 3, core * HALF, HALF).at[jnp.minimum(pos_ref[2], 1)]
    pert_copy = pltpu.make_async_copy(of_pert, field, sems.at[6])
    pot_copy = pltpu.make_async_copy(rows_of_chunk(pot, z ^ 3, core * HALF, HALF), field, sems.at[6])
    pl.when(pos_ref[2] < 2)(pert_copy.start)
    pl.when(pos_ref[2] >= 2)(pot_copy.start)
    rows = lax.broadcasted_iota(jnp.int32, (8, 128), 0)
    cols = lax.broadcasted_iota(jnp.int32, (8, 128), 1)
    out = jnp.zeros((8, 128), F32)
    for copy in copies[:3]:
        copy.wait()
    for k in range(2):
        values = [wave_s[k, d] for d in range(3)] + [level_s[k, n] for n in range(3)]
        values.append((partner_s[k] & 1).astype(F32))
        for j, value in enumerate(values):
            out = jnp.where((rows == k) & (cols == j), value, out)
    mine[...] = out
    small[:, HALF:] = out
    pot_copy.wait()
    for copy in copies[3:]:
        copy.wait()


def cut(pos, orbitals, perturbation, potential, wave, level, partner_map):
    chunk = orbitals.shape[:-1] + (CHUNK,)
    return pl.pallas_call(
        cut_kernel,
        in_specs=[pl.BlockSpec(memory_space=pltpu.SMEM)] + [IN_HBM] * 6,
        out_specs=[pl.BlockSpec(memory_space=pltpu.VMEM)] * 5,
        out_shape=[in_vmem(chunk)] * 3 + [in_vmem((8, HALF + 128)), in_vmem((8, 128))],
        scratch_shapes=[
            pltpu.SMEM((2, 3), F32),
            pltpu.SMEM((2, 3), F32),
            pltpu.SMEM((2,), jnp.int32),
            pltpu.SemaphoreType.DMA((7,)),
        ],
        compiler_params=pltpu.CompilerParams(vmem_limit_bytes=4 * 2**20),
        name="cut",
    )(pos, *[pltpu.with_memory_space_constraint(a, pltpu.HBM) for a in (orbitals, perturbation, potential, wave, level, partner_map)])


def perturbed(field, pert_r, pert_i):
    re, im = field
    return pert_r * re - pert_i * im, pert_r * im + pert_i * re


def join_halves(pos_ref, got, swap, joined, fields):
    x, core = pos_ref[2], pos_ref[3]
    for to, i in enumerate(fields):
        joined[to, :, pl.ds(pl.multiple_of(core * HALF, 128), HALF)] = got[x ^ i, :, :HALF]
        joined[to, :, pl.ds(pl.multiple_of((1 - core) * HALF, 128), HALF)] = swap[x ^ i, :, :HALF]


def one_lane_each(rows):
    row = lax.broadcasted_iota(jnp.int32, (40, 128), 0)
    lane = lax.broadcasted_iota(jnp.int32, (40, 128), 1)
    return jnp.where(row == lane, rows, 0.0)


def over_lanes(rows):
    ones = jnp.full((128, 128), 1.0, F32)
    return jnp.dot(rows, ones, precision=lax.Precision.HIGHEST, preferred_element_type=F32)


def products_kernel(near, pos_ref, slot_ref, o0, o1, *refs):
    if near:
        pert, out_ref = refs
        base = pos_ref[1] * CHUNK
    else:
        got, swap, near_ref, sums_ref, pert, out_ref = refs
        join_halves(pos_ref, got, swap, pert, (0, 1))
        base = 0
    pair, bases = (o0, o1), (base, 0)
    for k in range(4):
        block, kk = k // 2, k % 2
        slot = slot_ref[k]

        def body(g, acc, block=block, kk=kk, slot=slot):
            acc = list(acc)
            own, mate = pair[block], pair[1 - block]
            for v in range(3):
                at, mate_at, pert_at = (lanes_at(g, v, start) for start in (bases[block], bases[1 - block], base))
                pr, pi = pert[0, :, pert_at], pert[1, :, pert_at]
                w = [perturbed((own[kk, n, 0, :, at], own[kk, n, 1, :, at]), pr, pi) for n in range(3)]
                for m in range(3):
                    mr, mi = mate[slot, m, 0, :, mate_at], mate[slot, m, 1, :, mate_at]
                    for n in range(3):
                        i = (m * 3 + n) * 2
                        acc[i] = acc[i] + (mr * w[n][0] + mi * w[n][1])
                        acc[i + 1] = acc[i + 1] + (mr * w[n][1] - mi * w[n][0])
            return tuple(acc)

        acc = lax.fori_loop(0, CHUNK // GROUP, body, (jnp.zeros((8, 128), F32),) * 18)
        for i in range(18):
            at = pl.ds(block * 40 + kk * 18 + i, 1)
            value = jnp.sum(acc[i], axis=0, keepdims=True)
            out_ref[at, :] = value if near else near_ref[at, :] + value
    for block in range(2):
        out_ref[block * 40 + 36 : block * 40 + 40, :] = jnp.zeros((4, 128), F32)
    if not near:
        total = over_lanes(out_ref[...])
        for block in range(2):
            row = jnp.sum(one_lane_each(total[block * 40 : block * 40 + 40]), axis=0, keepdims=True)
            sums_ref[block * 8 : block * 8 + 8, :] = jnp.broadcast_to(row, (8, 128))


def products(pos, slots, o0, o1, *pert):
    near = len(pert) == 1
    return call(
        functools.partial(products_kernel, near),
        (pos, slots, o0, o1, *pert),
        [(80, 128) if near else (16, 128)],
        scratch=() if near else [pltpu.VMEM((2, 8, CHUNK), F32), pltpu.VMEM((80, 128), F32)],
        scalars=2,
        flops=20_000_000,
    )[0]


TALL, DEEP = ROWS + 4, 24
FIELD = (24, TALL, DEEP, 128)
ORBITALS = (24 * ROWS * 16, 128)


def rows_at(kn, c, r):
    return ((kn * 2 + c) * ROWS + r) * 16


def orbital_rows_kernel(pos_ref, o0, o1, o2, o3, pot, got, swap, orb_ref, v_ref, joined):
    join_halves(pos_ref, got, swap, joined, (2,))
    pot1 = joined.at[0]
    lanes = lane_ids()
    half = pos_ref[0]

    def body(g, carry):
        for pair, pot_ref, z, base in (((o0, o1), pot, half, pos_ref[1] * CHUNK), ((o2, o3), pot1, 1 - half, 0)):
            rows = unpack_rows(*[pot_ref[:, lanes_at(g, v, base)] for v in range(3)], lanes)
            for j in range(4):
                v_ref[pl.ds(pl.multiple_of((4 * g + j) * 16 + 8 * z, 8), 8), :] = rows[j]
            for k in range(4):
                start = base if k < 2 else 0
                for n in range(3):
                    for c in range(2):
                        cells = [pair[k // 2][k % 2, n, c, :, lanes_at(g, v, start)] for v in range(3)]
                        rows = unpack_rows(*cells, lanes)
                        for j in range(4):
                            at = pl.multiple_of(rows_at(k * 3 + n, c, 4 * g + j) + 8 * z, 8)
                            orb_ref[pl.ds(at, 8), :] = rows[j]
        return carry

    lax.fori_loop(0, CHUNK // GROUP, body, 0)


def orbital_rows(pos, fields, pots):
    return call(orbital_rows_kernel, (pos, *fields, *pots), [ORBITALS, (ROWS * 16, 128)], scratch=[pltpu.VMEM((1, 8, CHUNK), F32)], scalars=1)


ZHALO, YHALO = (48 * ROWS, 128), (24 * 32, 128)


def field_rows(kn, c, r, plane):
    return ((kn * 2 + c) * TALL + r + 2) * DEEP + 4 + plane


def clear_margin(u_ref, kn):
    for i in (kn * 2, kn * 2 + 1):
        for r in (0, 1, TALL - 2, TALL - 1):
            u_ref[i, r] = jnp.zeros((DEEP, 128), F32)
        for r in range(2, TALL - 2):
            u_ref[i, r, 0:4] = jnp.zeros((4, 128), F32)
            u_ref[i, r, 20:24] = jnp.zeros((4, 128), F32)


def near_face(parity, size):
    return (1 - parity) * (size - 2)


def cut_planes(flat, pos_ref, kn, za, zb):
    up = near_face(pos_ref[4] & 1, 16)
    for ref, first in ((za, up), (zb, 14 - up)):
        for c in range(2):
            for p in range(2):
                to = pl.ds(pl.multiple_of(((kn * 2 + c) * 2 + p) * ROWS, 8), ROWS)
                ref[to, :] = flat[pl.ds(field_rows(kn, c, 0, first + p), ROWS, stride=DEEP), :]


def cut_rows(u_ref, pos_ref, kn, ya, yb):
    up = near_face(pos_ref[1] & 1, ROWS)
    for ref, first in ((ya, up), (yb, ROWS - 2 - up)):
        for c in range(2):
            i = kn * 2 + c
            for p in range(2):
                to = pl.ds(pl.multiple_of((i * 2 + p) * 16, 8), 16)
                ref[to, :] = u_ref[i, 2 + first + p, 4:20, :]


def exchange(za, zb, ya, yb):
    return y_xor(za, 1), y_xor(zb, 3), z_xor(ya, 1), z_xor(yb, 3)


def right_kernel(ncells, slot_ref, pos_ref, s0, s1, s2, s3, o0, o1, o2, o3, pert0, got, swap, r_ref, za, zb, ya, yb, prod_ref, pert1):
    join_halves(pos_ref, got, swap, pert1, (0, 1))
    total = (s0[...] + s1[...]) + (s2[...] + s3[...])
    spread = [one_lane_each(jnp.broadcast_to(total[8 * block : 8 * block + 1], (40, 128))) for block in range(2)]
    prod_ref[...] = over_lanes(jnp.concatenate(spread, 0)) / ncells
    lanes = lane_ids()
    half = pos_ref[0]
    slabs = (((o0, o1), pert0, half, pos_ref[1] * CHUNK), ((o2, o3), pert1, 1 - half, 0))
    for k in range(4):
        block, kk = k // 2, k % 2
        slot = slot_ref[k]

        def body(g, carry, k=k, block=block, kk=kk, slot=slot):
            for pair, pert, z, base in slabs:
                own, mate = pair[block], pair[1 - block]
                own_base, mate_base = (base, 0) if block == 0 else (0, base)
                right = [[[], []] for _ in range(3)]
                for v in range(3):
                    at, mate_at, pert_at = (lanes_at(g, v, start) for start in (own_base, mate_base, base))
                    pr, pi = pert[0, :, pert_at], pert[1, :, pert_at]
                    mates = [(mate[slot, m, 0, :, mate_at], mate[slot, m, 1, :, mate_at]) for m in range(3)]
                    for n in range(3):
                        wr, wi = perturbed((own[kk, n, 0, :, at], own[kk, n, 1, :, at]), pr, pi)
                        gr, gi = -wr, -wi
                        for m in range(3):
                            row = block * 40 + kk * 18 + (m * 3 + n) * 2
                            qr = prod_ref[pl.ds(row, 1), :]
                            qi = prod_ref[pl.ds(row + 1, 1), :]
                            mr, mi = mates[m]
                            gr = gr + (qr * mr - qi * mi)
                            gi = gi + (qi * mr + qr * mi)
                        right[n][0].append(gr)
                        right[n][1].append(gi)
                for n in range(3):
                    for c in range(2):
                        rows = unpack_rows(*right[n][c], lanes)
                        for j in range(4):
                            planes = pl.ds(4 + 8 * z, 8)
                            r_ref[(k * 3 + n) * 2 + c, 2 + 4 * g + j, planes, :] = rows[j]
            return carry

        lax.fori_loop(0, CHUNK // GROUP, body, 0)

    flat = r_ref.reshape(24 * TALL * DEEP, 128)

    def cut(kn, carry):
        clear_margin(r_ref, kn)
        cut_planes(flat, pos_ref, kn, za, zb)
        cut_rows(r_ref, pos_ref, kn, ya, yb)
        return carry

    lax.fori_loop(0, 12, cut, 0)


def right_sides(ncells, slots, pos, sums, fields, perts):
    return call(
        functools.partial(right_kernel, ncells),
        (slots, pos, *sums, *fields, *perts),
        [FIELD, ZHALO, ZHALO, YHALO, YHALO],
        scratch=[pltpu.VMEM((80, 128), F32), pltpu.VMEM((2, 8, CHUNK), F32)],
        scalars=2,
        flops=20_000_000,
    )


def x_matrix():
    m = np.zeros((128, 256), np.float32)
    for i in range(NX):
        for s, lap, grad in ((1, 16, 8), (-1, 16, -8), (2, -1, -1), (-2, -1, 1)):
            m[(i + s) % NX, i] += lap
            m[(i + s) % NX, 128 + i] += grad
    return np.concatenate([m, m], 0)


def scalars_of(count, par_ref, w_ref, kn):
    k, n = kn // 3, kn % 3
    kx, ky, kz = par_ref[k, 0], par_ref[k, 1], par_ref[k, 2]
    base = 3.75 + 0.5 * (kx * kx + ky * ky + kz * kz) + par_ref[k, 3 + n]
    wt = w_ref[count]
    scale = w_ref[0] if count == 1 else jnp.float32(1.0)
    return kx, ky, kz, base, wt, scale


def step_kernel(count, par_ref, w_ref, *refs):
    last, first = count == ITERS - 1, count == 1
    if first:
        r_ref, v_ref, m_ref, *refs = refs
        u_ref = r_ref
    else:
        u_ref, r_ref, v_ref, m_ref, *refs = refs
    if last:
        orb_ref, out_ref, *flats = refs
        out_ref[...] = jnp.zeros_like(out_ref)
    else:
        out_ref, *flats = refs

    def along_x(kn, g, flat):
        cells = [u_ref[kn * 2 + c, 2 + 8 * g : 10 + 8 * g, 4:20, :].reshape(128, 128) for c in range(2)]
        u2 = jnp.concatenate(cells, 0)
        hi = u2.astype(jnp.bfloat16)
        lo = (u2 - hi.astype(F32)).astype(jnp.bfloat16)
        flat[...] = jnp.dot(jnp.concatenate([hi, lo], 1), m_ref[...], preferred_element_type=F32)

    def rows_of(kn, g, flat, coef):
        lap, gx, gy, gz, keep, pull, wt = coef
        for r in range(8 * g, 8 * g + 8):
            cells, second, grad = [], [], []
            for c in range(2):
                i = kn * 2 + c
                at = slice((c * 8 + r - 8 * g) * 16, (c * 8 + r - 8 * g + 1) * 16)
                yp1, ym1 = u_ref[i, r + 3, 4:20, :], u_ref[i, r + 1, 4:20, :]
                yp2, ym2 = u_ref[i, r + 4, 4:20, :], u_ref[i, r, 4:20, :]
                zp1, zm1 = u_ref[i, r + 2, 5:21, :], u_ref[i, r + 2, 3:19, :]
                zp2, zm2 = u_ref[i, r + 2, 6:22, :], u_ref[i, r + 2, 2:18, :]
                cells.append(u_ref[i, r + 2, 4:20, :])
                one = (yp1 + ym1) + (zp1 + zm1)
                two = (yp2 + ym2) + (zp2 + zm2)
                second.append(flat[at, 0:128] + (16.0 * one - two))
                dy = (yp1 - ym1) - 0.125 * (yp2 - ym2)
                dz = (zp1 - zm1) - 0.125 * (zp2 - zm2)
                grad.append(gx * flat[at, 128:256] + (gy * dy + gz * dz))
            center = keep - pull * v_ref[16 * r : 16 * r + 16, :]
            new = []
            for c in range(2):
                i = kn * 2 + c
                value = center * cells[c] + lap * second[c]
                if not first:
                    value = value + wt * r_ref[i, r + 2, 4:20, :]
                new.append(value - grad[1] if c == 0 else value + grad[0])
            if last:
                orb_r = orb_ref[pl.ds(pl.multiple_of(rows_at(kn, 0, r), 16), 16), :]
                orb_i = orb_ref[pl.ds(pl.multiple_of(rows_at(kn, 1, r), 16), 16), :]
                out_ref[16 * r : 16 * r + 16, :] += orb_r * new[0] + orb_i * new[1]
                out_ref[16 * (ROWS + r) : 16 * (ROWS + r) + 16, :] += orb_r * new[1] - orb_i * new[0]
            else:
                for c in range(2):
                    out_ref[pl.ds(pl.multiple_of(rows_at(kn, c, r), 16), 16), :] = new[c]

    along_x(0, 0, flats[0])

    def orbital(kn, carry):
        kx, ky, kz, base, wt, scale = scalars_of(count, par_ref, w_ref, kn)
        ws = wt * scale
        keep = scale - ws * base
        if first:
            keep = keep + wt
        coef = (ws / 24.0, ws * kx / 12.0, ws * ky * (2.0 / 3.0), ws * kz * (2.0 / 3.0), keep, ws, wt)
        ahead = jnp.minimum(kn + 1, 11)
        for g in range(3):
            along_x(kn if g < 2 else ahead, (g + 1) % 3, flats[(g + 1) % 3])
            rows_of(kn, g, flats[g], coef)
        return carry

    lax.fori_loop(0, 12, orbital, 0)


def inner_step(count, par, weights, u, right, pot, matrix, orb):
    last = count == ITERS - 1
    return call(
        functools.partial(step_kernel, count),
        (par, weights) + ((u,) if count > 1 else ()) + (right, pot, matrix) + ((orb,) if last else ()),
        [(2 * ROWS * 16, 128) if last else ORBITALS],
        scratch=[pltpu.VMEM((256, 256), F32)] * 3,
        scalars=2,
        flops=60_000_000,
    )[0]


def face_terms(lap, g, beyond1, beyond2):
    first = [lap * (16.0 * beyond1[c] - beyond2[c]) for c in range(2)]
    grad1 = [g * (beyond1[c] - 0.125 * beyond2[c]) for c in range(2)]
    second = [-lap * beyond1[c] for c in range(2)]
    grad2 = [(-0.125 * g) * beyond1[c] for c in range(2)]
    return (
        (first[0] - grad1[1], first[1] + grad1[0]),
        (second[0] - grad2[1], second[1] + grad2[0]),
    )


def faces(count, par_ref, w_ref, pos_ref, kn, za, zb, ya, yb, add_plane, add_row):
    _, ky, kz, _, wt, scale = scalars_of(count, par_ref, w_ref, kn)
    ws = wt * scale
    lap = ws / 24.0
    gy, gz = ws * ky * (2.0 / 3.0), ws * kz * (2.0 / 3.0)
    from_z = (kn + 6) % 12

    def plane(ref, p):
        return [ref[pl.ds(pl.multiple_of(((kn * 2 + c) * 2 + p) * ROWS, 8), ROWS), :] for c in range(2)]

    def line(ref, r):
        return [ref[pl.ds(pl.multiple_of(((from_z * 2 + c) * 2 + r) * 16, 8), 16), :] for c in range(2)]

    def side(ref, layer, size, g, below, add, which):
        sign = (1 - 2 * below).astype(F32)
        first = (1 - below) * (size - 1)
        terms = face_terms(lap, sign * g, layer(ref, below), layer(ref, 1 - below))
        add(first, terms[0], which, 1 - below)
        add(first + 2 * below - 1, terms[1], which, below)

    odd = pos_ref[1] & 1
    side(ya, line, ROWS, gy, odd, add_row, 0)
    side(yb, line, ROWS, gy, 1 - odd, add_row, 1)
    odd = pos_ref[4] & 1
    side(za, plane, 16, gz, odd, add_plane, 0)
    side(zb, plane, 16, gz, 1 - odd, add_plane, 1)


def faces_kernel(count, par_ref, w_ref, pos_ref, u_in, za_in, zb_in, ya_in, yb_in, u_ref, za, zb, ya, yb):
    flat = u_ref.reshape(24 * TALL * DEEP, 128)

    def orbital(kn, carry):
        clear_margin(u_ref, kn)
        for c in range(2):
            for r in range(ROWS):
                u_ref[kn * 2 + c, r + 2, 4:20, :] = u_in[pl.ds(pl.multiple_of(rows_at(kn, c, r), 16), 16), :]

        def add_plane(p, term, which, place):
            for c in range(2):
                at = pl.ds(field_rows(kn, c, 0, p), ROWS, stride=DEEP)
                value = flat[at, :] + term[c]
                flat[at, :] = value
                to = pl.ds(pl.multiple_of(((kn * 2 + c) * 2 + place) * ROWS, 8), ROWS)
                (za, zb)[which][to, :] = value

        def add_row(r, term, which, place):
            for c in range(2):
                u_ref[kn * 2 + c, r + 2, 4:20, :] = u_ref[kn * 2 + c, r + 2, 4:20, :] + term[c]

        faces(count, par_ref, w_ref, pos_ref, kn, za_in, zb_in, ya_in, yb_in, add_plane, add_row)
        cut_rows(u_ref, pos_ref, kn, ya, yb)
        return carry

    lax.fori_loop(0, 12, orbital, 0)


def add_faces(count, par, weights, pos, u, halos):
    return call(
        functools.partial(faces_kernel, count),
        (par, weights, pos, u, *halos),
        [FIELD, ZHALO, ZHALO, YHALO, YHALO],
        scalars=3,
    )


def density_kernel(par_ref, w_ref, pos_ref, d_in, za, zb, ya, yb, orb_ref, keep_ref, send_ref, d_ref):
    d_ref[...] = d_in[...]

    def orbital(kn, carry):
        def add(at, to, term):
            orb_r, orb_i = orb_ref[at[0], :], orb_ref[at[1], :]
            d_ref[to[0], :] = d_ref[to[0], :] + (orb_r * term[0] + orb_i * term[1])
            d_ref[to[1], :] = d_ref[to[1], :] + (orb_r * term[1] - orb_i * term[0])

        def add_plane(p, term, which, place):
            add(
                [pl.ds(rows_at(kn, c, 0) + p, ROWS, stride=16) for c in range(2)],
                [pl.ds(c * ROWS * 16 + p, ROWS, stride=16) for c in range(2)],
                term,
            )

        def add_row(r, term, which, place):
            add(
                [pl.ds(pl.multiple_of(rows_at(kn, c, r), 16), 16) for c in range(2)],
                [pl.ds(pl.multiple_of((c * ROWS + r) * 16, 16), 16) for c in range(2)],
                term,
            )

        faces(ITERS - 1, par_ref, w_ref, pos_ref, kn, za, zb, ya, yb, add_plane, add_row)
        return carry

    lax.fori_loop(0, 12, orbital, 0)
    ids = lane_ids()
    core = pos_ref[3]
    for ref, c in ((send_ref, 1 - core), (keep_ref, core)):
        for z in range(2):
            for g in range(6):
                rows = [
                    d_ref[pl.ds(pl.multiple_of((c * ROWS + 4 * g + j) * 16 + 8 * z, 8), 8), :] * (1.0 / 32.0)
                    for j in range(4)
                ]
                packed = pack_rows(*rows, ids)
                for v in range(3):
                    at = g * GROUP + v * 128
                    ref[z, :, at : at + 128] = packed[v]


TILE = (2, 8, CHUNK)


def tile_density(par, weights, pos, dens, halos, orb):
    return call(
        density_kernel,
        (par, weights, pos, dens, *halos, orb),
        [TILE, TILE],
        scratch=[pltpu.VMEM((2 * ROWS * 16, 128), F32)],
        scalars=3,
    )


def pair_kernel(a, b, out):
    out[...] = a[...] + b[...]


def split_kernel(pos_ref, s0, s1, s2, s3, mine, other):
    half = pos_ref[0]
    mine[...] = (s0[half] + s1[half]) + (s2[half] + s3[half])
    half = 1 - half
    other[...] = (s0[half] + s1[half]) + (s2[half] + s3[half])


def place_kernel(pos_ref, *refs):
    tiles, out_ref, sems = refs[:8], refs[8], refs[9]
    z, core = pos_ref[1], pos_ref[3]
    copies = []
    for i, tile in enumerate(tiles):
        component = core if i < 4 else 1 - core
        target = out_ref.at[component, :, pl.ds(pl.multiple_of((z ^ (i % 4)) * CHUNK, 128), CHUNK)]
        copies.append(pltpu.make_async_copy(tile, target, sems.at[i]))
    for copy in copies:
        copy.start()
    for copy in copies:
        copy.wait()


def place(pos, tiles):
    return pl.pallas_call(
        place_kernel,
        in_specs=[pl.BlockSpec(memory_space=pltpu.SMEM)] + [pl.BlockSpec(memory_space=pl.ANY)] * 8,
        out_specs=IN_HBM,
        out_shape=jax.ShapeDtypeStruct((2, 8, 4 * CHUNK), F32),
        scratch_shapes=[pltpu.SemaphoreType.DMA((8,))],
        compiler_params=pltpu.CompilerParams(vmem_limit_bytes=4 * 2**20),
        name="place",
    )(pos, *[pltpu.with_memory_space_constraint(t, pltpu.VMEM) for t in tiles])


def program(orbitals, partner_map, wave_vectors, levels, potential, perturbation, step_weights):
    zl, zh = lax.axis_index("zl"), lax.axis_index("zh")
    z = zh * 2 + zl
    pos = jnp.stack([zh, z, lax.axis_index("x"), lax.axis_index("c"), lax.axis_index("y")]).astype(jnp.int32)
    ncells = 64 * 4 * CHUNK
    matrix = jnp.asarray(x_matrix(), jnp.bfloat16)

    send3, send1, send2, small, mine = cut(pos, orbitals, perturbation, potential, wave_vectors, levels, partner_map)
    field = z_xor(small, 3)
    o3 = z_xor(send3, 3)
    o1 = z_xor(send1, 1)
    o2 = z_xor(send2, 2)
    shared = [field]
    for m in (1, 2, 3):
        shared.append(x_xor(field, m))
    got = jnp.stack(shared)
    swap = other_core(got)
    par = jnp.concatenate([mine[:2, :8], field[:2, HALF : HALF + 8]], 0)
    slots = par[:, 6].astype(jnp.int32)
    weights = step_weights.astype(F32) / 100.0

    fields, pert = [orbitals, o1, o2, o3], (perturbation, got, swap)
    part = products(pos, slots, orbitals, o1, perturbation)
    part = products(pos, slots, o2, o3, got, swap, part)
    orb, pot = orbital_rows(pos, fields, (potential, got, swap))

    def swapped(value):
        return jnp.concatenate([value[8:], value[:8]], 0)

    part = part + swapped(z_xor(part, 1)) + z_xor(part, 2) + swapped(z_xor(part, 3))
    sums = [part] + [y_xor(part, m) for m in (1, 2, 3)]
    orb, pot, sums = lax.optimization_barrier((orb, pot, sums))
    right, *edge = right_sides(float(ncells), slots, pos, sums, fields, pert)
    u = right
    for count in range(1, ITERS):
        halos = exchange(*edge)
        u = inner_step(count, par, weights, u, right, pot, matrix, orb)
        if count < ITERS - 1:
            u, *edge = add_faces(count, par, weights, pos, u, halos)
    keep, send = tile_density(par, weights, pos, u, halos, orb)

    chip = call(pair_kernel, (keep, other_core(send)), [TILE])[0]
    parts = [chip]
    for m in (1, 2, 3):
        parts.append(x_xor(chip, m))
    same, cross = call(split_kernel, (pos, *parts), [(8, CHUNK)] * 2, scalars=1)
    tiles = [same, z_xor(same, 1), z_xor(cross, 2), z_xor(cross, 3)]
    return place(pos, tiles + [other_core(tile) for tile in tiles])


def solution(mesh):
    fine = Mesh(mesh.devices.reshape(2, 4, 2, 4, 2), ("zl", "x", "c", "y", "zh"))
    ka, grid = ("zl", "x", "c"), ("y", "zh")
    return jax.shard_map(
        program,
        mesh=fine,
        in_specs=(
            P(ka, None, None, grid, None),
            P(ka),
            P(ka, None),
            P(ka, None),
            P(grid, None),
            P(None, grid, None),
            P(),
        ),
        out_specs=P(None, grid, None),
        check_vma=False,
    )
```

```python
import functools

import jax
import jax.numpy as jnp
import numpy as np
from jax import lax
from jax.experimental import pallas as pl
from jax.experimental.pallas import tpu as pltpu
from jax.sharding import Mesh
from jax.sharding import PartitionSpec as P


NX = 96
ITERS = 4
ROWS = 24
CHUNK = ROWS * NX
GROUP = 4 * NX
F32 = jnp.float32
ZAX = ("zl", "zh")


def z_perm(to):
    index = lambda z: (z & 1) * 2 + (z >> 1)
    return [(index(z), index(to(z))) for z in range(4)]


def z_xor(value, m):
    return lax.ppermute(value, ZAX, z_perm(lambda z: z ^ m))


def other_core(value):
    return lax.ppermute(value, "c", [(0, 1), (1, 0)])


def x_xor(value, m):
    return lax.ppermute(value, "x", [(i, i ^ m) for i in range(4)])


def y_xor(value, m):
    return lax.ppermute(value, "y", [(i, i ^ m) for i in range(4)])


def lane_ids():
    return lax.broadcasted_iota(jnp.int32, (8, 128), 1)


def unpack_rows(a, b, c, lanes):
    r1 = pltpu.roll(jnp.where(lanes < 96, b, a), 32, 1)
    r2 = pltpu.roll(jnp.where(lanes < 64, c, b), 64, 1)
    r3 = pltpu.roll(c, 96, 1)
    return a, r1, r2, r3


def pack_rows(r0, r1, r2, r3, lanes):
    r1s = pltpu.roll(r1, 96, 1)
    r2s = pltpu.roll(r2, 64, 1)
    r3s = pltpu.roll(r3, 32, 1)
    return (
        jnp.where(lanes < 96, r0, r1s),
        jnp.where(lanes < 64, r1s, r2s),
        jnp.where(lanes < 32, r2s, r3s),
    )


def in_vmem(shape):
    return pltpu.VMEM(shape, F32)


def call(kernel, args, outs, scratch=(), scalars=0, aliases=None, flops=10_000_000, limit=8):
    specs = [pl.BlockSpec(memory_space=pltpu.SMEM)] * scalars
    specs += [pl.BlockSpec(memory_space=pltpu.VMEM)] * (len(args) - scalars)
    args = list(args[:scalars]) + [pltpu.with_memory_space_constraint(a, pltpu.VMEM) for a in args[scalars:]]
    return pl.pallas_call(
        kernel,
        in_specs=specs,
        out_specs=[pl.BlockSpec(memory_space=pltpu.VMEM)] * len(outs),
        out_shape=[in_vmem(o) for o in outs],
        scratch_shapes=list(scratch),
        input_output_aliases=aliases or {},
        compiler_params=pltpu.CompilerParams(vmem_limit_bytes=limit * 2**20),
        cost_estimate=pl.CostEstimate(flops=flops, bytes_accessed=10_000_000, transcendentals=0),
    )(*args)


def lanes_at(group, v, base=0):
    return pl.ds(pl.multiple_of(base + group * GROUP + v * 128, 128), 128)


HALF = CHUNK // 2
IN_HBM = pl.BlockSpec(memory_space=pltpu.HBM)


def rows_of_chunk(ref, z, extra=0, width=CHUNK):
    index = (slice(None),) * (len(ref.shape) - 1) + (pl.ds(pl.multiple_of(z * CHUNK + extra, 128), width),)
    return ref.at[index]


def cut_kernel(pos_ref, orb, pert, pot, wave, level, partner, send3, send1, send2, small, mine, wave_s, level_s, partner_s, sems):
    z, core = pos_ref[1], pos_ref[3]
    moves = [
        (wave, wave_s),
        (level, level_s),
        (partner, partner_s),
        (rows_of_chunk(orb, z ^ 3), send3),
        (rows_of_chunk(orb, z ^ 1), send1),
        (rows_of_chunk(orb, z ^ 2), send2),
    ]
    copies = [pltpu.make_async_copy(source, target, sems.at[i]) for i, (source, target) in enumerate(moves)]
    for copy in copies:
        copy.start()
    field = small.at[:, pl.ds(0, HALF)]
    of_pert = rows_of_chunk(pert, z ^ 3, core * HALF, HALF).at[jnp.minimum(pos_ref[2], 1)]
    pert_copy = pltpu.make_async_copy(of_pert, field, sems.at[6])
    pot_copy = pltpu.make_async_copy(rows_of_chunk(pot, z ^ 3, core * HALF, HALF), field, sems.at[6])
    pl.when(pos_ref[2] < 2)(pert_copy.start)
    pl.when(pos_ref[2] >= 2)(pot_copy.start)
    rows = lax.broadcasted_iota(jnp.int32, (8, 128), 0)
    cols = lax.broadcasted_iota(jnp.int32, (8, 128), 1)
    out = jnp.zeros((8, 128), F32)
    for copy in copies[:3]:
        copy.wait()
    for k in range(2):
        values = [wave_s[k, d] for d in range(3)] + [level_s[k, n] for n in range(3)]
        values.append((partner_s[k] & 1).astype(F32))
        for j, value in enumerate(values):
            out = jnp.where((rows == k) & (cols == j), value, out)
    mine[...] = out
    small[:, HALF:] = out
    pot_copy.wait()
    for copy in copies[3:]:
        copy.wait()


def cut(pos, orbitals, perturbation, potential, wave, level, partner_map):
    chunk = orbitals.shape[:-1] + (CHUNK,)
    return pl.pallas_call(
        cut_kernel,
        in_specs=[pl.BlockSpec(memory_space=pltpu.SMEM)] + [IN_HBM] * 6,
        out_specs=[pl.BlockSpec(memory_space=pltpu.VMEM)] * 5,
        out_shape=[in_vmem(chunk)] * 3 + [in_vmem((8, HALF + 128)), in_vmem((8, 128))],
        scratch_shapes=[
            pltpu.SMEM((2, 3), F32),
            pltpu.SMEM((2, 3), F32),
            pltpu.SMEM((2,), jnp.int32),
            pltpu.SemaphoreType.DMA((7,)),
        ],
        compiler_params=pltpu.CompilerParams(vmem_limit_bytes=4 * 2**20),
        name="cut",
    )(pos, *[pltpu.with_memory_space_constraint(a, pltpu.HBM) for a in (orbitals, perturbation, potential, wave, level, partner_map)])


def perturbed(field, pert_r, pert_i):
    re, im = field
    return pert_r * re - pert_i * im, pert_r * im + pert_i * re


def join_halves(pos_ref, got, swap, joined, fields):
    x, core = pos_ref[2], pos_ref[3]
    for to, i in enumerate(fields):
        joined[to, :, pl.ds(pl.multiple_of(core * HALF, 128), HALF)] = got[x ^ i, :, :HALF]
        joined[to, :, pl.ds(pl.multiple_of((1 - core) * HALF, 128), HALF)] = swap[x ^ i, :, :HALF]


def one_lane_each(rows):
    row = lax.broadcasted_iota(jnp.int32, (40, 128), 0)
    lane = lax.broadcasted_iota(jnp.int32, (40, 128), 1)
    return jnp.where(row == lane, rows, 0.0)


def over_lanes(rows):
    ones = jnp.full((128, 128), 1.0, F32)
    return jnp.dot(rows, ones, precision=lax.Precision.HIGHEST, preferred_element_type=F32)


def products_kernel(near, pos_ref, slot_ref, o0, o1, *refs):
    if near:
        pert, out_ref = refs
        base = pos_ref[1] * CHUNK
    else:
        got, swap, near_ref, sums_ref, pert, out_ref = refs
        join_halves(pos_ref, got, swap, pert, (0, 1))
        base = 0
    pair, bases = (o0, o1), (base, 0)
    for k in range(4):
        block, kk = k // 2, k % 2
        slot = slot_ref[k]

        def body(g, acc, block=block, kk=kk, slot=slot):
            acc = list(acc)
            own, mate = pair[block], pair[1 - block]
            for v in range(3):
                at, mate_at, pert_at = (lanes_at(g, v, start) for start in (bases[block], bases[1 - block], base))
                pr, pi = pert[0, :, pert_at], pert[1, :, pert_at]
                w = [perturbed((own[kk, n, 0, :, at], own[kk, n, 1, :, at]), pr, pi) for n in range(3)]
                for m in range(3):
                    mr, mi = mate[slot, m, 0, :, mate_at], mate[slot, m, 1, :, mate_at]
                    for n in range(3):
                        i = (m * 3 + n) * 2
                        acc[i] = acc[i] + (mr * w[n][0] + mi * w[n][1])
                        acc[i + 1] = acc[i + 1] + (mr * w[n][1] - mi * w[n][0])
            return tuple(acc)

        acc = lax.fori_loop(0, CHUNK // GROUP, body, (jnp.zeros((8, 128), F32),) * 18)
        for i in range(18):
            at = pl.ds(block * 40 + kk * 18 + i, 1)
            value = jnp.sum(acc[i], axis=0, keepdims=True)
            out_ref[at, :] = value if near else near_ref[at, :] + value
    for block in range(2):
        out_ref[block * 40 + 36 : block * 40 + 40, :] = jnp.zeros((4, 128), F32)
    if not near:
        total = over_lanes(out_ref[...])
        for block in range(2):
            row = jnp.sum(one_lane_each(total[block * 40 : block * 40 + 40]), axis=0, keepdims=True)
            sums_ref[block * 8 : block * 8 + 8, :] = jnp.broadcast_to(row, (8, 128))


def products(pos, slots, o0, o1, *pert):
    near = len(pert) == 1
    return call(
        functools.partial(products_kernel, near),
        (pos, slots, o0, o1, *pert),
        [(80, 128) if near else (16, 128)],
        scratch=() if near else [pltpu.VMEM((2, 8, CHUNK), F32), pltpu.VMEM((80, 128), F32)],
        scalars=2,
        flops=20_000_000,
    )[0]


TALL, DEEP = ROWS + 4, 24
FIELD = (24, TALL, DEEP, 128)
ORBITALS = (24 * ROWS * 16, 128)


def rows_at(kn, c, r):
    return ((kn * 2 + c) * ROWS + r) * 16


def orbital_rows_kernel(pos_ref, o0, o1, o2, o3, pot, pert, got, swap, orb_ref, w_ref, v_ref, joined):
    join_halves(pos_ref, got, swap, joined, (0, 1, 2))
    lanes = lane_ids()
    half = pos_ref[0]

    def rows_of(ref, index, g, base):
        return unpack_rows(*[ref[index + (slice(None), lanes_at(g, v, base))] for v in range(3)], lanes)

    def body(g, carry):
        near = pos_ref[1] * CHUNK
        fields = ((pert, (0,)), (pert, (1,)), (pot, ())), tuple((joined, (i,)) for i in range(3))
        for pair, local, z, base in (((o0, o1), fields[0], half, near), ((o2, o3), fields[1], 1 - half, 0)):
            pert_r, pert_i, rows = (rows_of(ref, index, g, base) for ref, index in local)
            for j in range(4):
                v_ref[pl.ds(pl.multiple_of((4 * g + j) * 16 + 8 * z, 8), 8), :] = rows[j]
            for k in range(4):
                start = base if k < 2 else 0
                for n in range(3):
                    field = [rows_of(pair[k // 2], (k % 2, n, c), g, start) for c in range(2)]
                    for j in range(4):
                        orb = field[0][j], field[1][j]
                        w = perturbed(orb, pert_r[j], pert_i[j])
                        for c in range(2):
                            at = pl.ds(pl.multiple_of(rows_at(k * 3 + n, c, 4 * g + j) + 8 * z, 8), 8)
                            orb_ref[at, :] = orb[c]
                            w_ref[at, :] = w[c]
        return carry

    lax.fori_loop(0, CHUNK // GROUP, body, 0)


def orbital_rows(pos, fields, *local):
    return call(
        orbital_rows_kernel,
        (pos, *fields, *local),
        [ORBITALS, ORBITALS, (ROWS * 16, 128)],
        scratch=[pltpu.VMEM((3, 8, CHUNK), F32)],
        scalars=1,
    )


ZHALO, YHALO = (48 * ROWS, 128), (24 * 32, 128)


def field_rows(kn, c, r, plane):
    return ((kn * 2 + c) * TALL + r + 2) * DEEP + 4 + plane


def clear_rows(u_ref, i):
    for r in (0, 1, TALL - 2, TALL - 1):
        u_ref[i, r] = jnp.zeros((DEEP, 128), F32)


def clear_sides(u_ref, i, r):
    u_ref[i, r, 0:4] = jnp.zeros((4, 128), F32)
    u_ref[i, r, 20:24] = jnp.zeros((4, 128), F32)


def near_face(parity, size):
    return (1 - parity) * (size - 2)


def cut_planes(flat, pos_ref, kn, za, zb):
    up = near_face(pos_ref[4] & 1, 16)
    for ref, first in ((za, up), (zb, 14 - up)):
        for c in range(2):
            for p in range(2):
                to = pl.ds(pl.multiple_of(((kn * 2 + c) * 2 + p) * ROWS, 8), ROWS)
                ref[to, :] = flat[pl.ds(field_rows(kn, c, 0, first + p), ROWS, stride=DEEP), :]


def cut_rows(u_ref, pos_ref, kn, ya, yb):
    up = near_face(pos_ref[1] & 1, ROWS)
    for ref, first in ((ya, up), (yb, ROWS - 2 - up)):
        for c in range(2):
            i = kn * 2 + c
            for p in range(2):
                to = pl.ds(pl.multiple_of((i * 2 + p) * 16, 8), 16)
                ref[to, :] = u_ref[i, 2 + first + p, 4:20, :]


def exchange(za, zb, ya, yb):
    return y_xor(za, 1), y_xor(zb, 3), z_xor(ya, 1), z_xor(yb, 3)


def right_kernel(ncells, slot_ref, pos_ref, s0, s1, s2, s3, orb_ref, w_ref, r_ref, za, zb, ya, yb, prod_ref):
    total = (s0[...] + s1[...]) + (s2[...] + s3[...])
    spread = [one_lane_each(jnp.broadcast_to(total[8 * block : 8 * block + 1], (40, 128))) for block in range(2)]
    prod_ref[...] = over_lanes(jnp.concatenate(spread, 0)) / ncells
    for k in range(4):
        block, kk = k // 2, k % 2
        mate = (2 - 2 * block + slot_ref[k]) * 3

        def body(r, carry, k=k, block=block, kk=kk, mate=mate):
            def cells(ref, kn, c):
                return ref[pl.ds(pl.multiple_of(rows_at(kn, c, r), 16), 16), :]

            mates = [(cells(orb_ref, mate + m, 0), cells(orb_ref, mate + m, 1)) for m in range(3)]
            for n in range(3):
                gr, gi = -cells(w_ref, k * 3 + n, 0), -cells(w_ref, k * 3 + n, 1)
                for m, (mr, mi) in enumerate(mates):
                    row = block * 40 + kk * 18 + (m * 3 + n) * 2
                    qr, qi = prod_ref[pl.ds(row, 1), :], prod_ref[pl.ds(row + 1, 1), :]
                    gr = gr + (qr * mr - qi * mi)
                    gi = gi + (qi * mr + qr * mi)
                for c, value in enumerate((gr, gi)):
                    i = (k * 3 + n) * 2 + c
                    clear_sides(r_ref, i, r + 2)
                    r_ref[i, r + 2, 4:20, :] = value
            return carry

        lax.fori_loop(0, ROWS, body, 0, unroll=4)
    flat = r_ref.reshape(24 * TALL * DEEP, 128)

    def cut(kn, carry):
        for c in range(2):
            clear_rows(r_ref, kn * 2 + c)
        cut_planes(flat, pos_ref, kn, za, zb)
        cut_rows(r_ref, pos_ref, kn, ya, yb)
        return carry

    lax.fori_loop(0, 12, cut, 0)


def right_sides(ncells, slots, pos, sums, orb, w):
    return call(
        functools.partial(right_kernel, ncells),
        (slots, pos, *sums, orb, w),
        [FIELD, ZHALO, ZHALO, YHALO, YHALO],
        scratch=[pltpu.VMEM((80, 128), F32)],
        scalars=2,
        flops=20_000_000,
    )


def x_matrix():
    m = np.zeros((128, 256), np.float32)
    for i in range(NX):
        for s, lap, grad in ((1, 16, 8), (-1, 16, -8), (2, -1, -1), (-2, -1, 1)):
            m[(i + s) % NX, i] += lap
            m[(i + s) % NX, 128 + i] += grad
    return np.concatenate([m, m], 0)


def scalars_of(count, par_ref, w_ref, kn):
    k, n = kn // 3, kn % 3
    kx, ky, kz = par_ref[k, 0], par_ref[k, 1], par_ref[k, 2]
    base = 3.75 + 0.5 * (kx * kx + ky * ky + kz * kz) + par_ref[k, 3 + n]
    wt = w_ref[count]
    scale = w_ref[0] if count == 1 else jnp.float32(1.0)
    return kx, ky, kz, base, wt, scale


def step_kernel(count, par_ref, w_ref, *refs):
    last, first = count == ITERS - 1, count == 1
    if first:
        r_ref, v_ref, m_ref, *refs = refs
        u_ref = r_ref
    else:
        u_ref, r_ref, v_ref, m_ref, *refs = refs
    if last:
        orb_ref, out_ref, *flats = refs
        out_ref[...] = jnp.zeros_like(out_ref)
    else:
        out_ref, *flats = refs

    def along_x(kn, g, flat):
        cells = [u_ref[kn * 2 + c, 2 + 8 * g : 10 + 8 * g, 4:20, :].reshape(128, 128) for c in range(2)]
        u2 = jnp.concatenate(cells, 0)
        hi = u2.astype(jnp.bfloat16)
        lo = (u2 - hi.astype(F32)).astype(jnp.bfloat16)
        flat[...] = jnp.dot(jnp.concatenate([hi, lo], 1), m_ref[...], preferred_element_type=F32)

    def rows_of(kn, g, flat, coef):
        lap, gx, gy, gz, keep, pull, wt = coef
        for r in range(8 * g, 8 * g + 8):
            cells, second, grad = [], [], []
            for c in range(2):
                i = kn * 2 + c
                at = slice((c * 8 + r - 8 * g) * 16, (c * 8 + r - 8 * g + 1) * 16)
                yp1, ym1 = u_ref[i, r + 3, 4:20, :], u_ref[i, r + 1, 4:20, :]
                yp2, ym2 = u_ref[i, r + 4, 4:20, :], u_ref[i, r, 4:20, :]
                zp1, zm1 = u_ref[i, r + 2, 5:21, :], u_ref[i, r + 2, 3:19, :]
                zp2, zm2 = u_ref[i, r + 2, 6:22, :], u_ref[i, r + 2, 2:18, :]
                cells.append(u_ref[i, r + 2, 4:20, :])
                one = (yp1 + ym1) + (zp1 + zm1)
                two = (yp2 + ym2) + (zp2 + zm2)
                second.append(flat[at, 0:128] + (16.0 * one - two))
                dy = (yp1 - ym1) - 0.125 * (yp2 - ym2)
                dz = (zp1 - zm1) - 0.125 * (zp2 - zm2)
                grad.append(gx * flat[at, 128:256] + (gy * dy + gz * dz))
            center = keep - pull * v_ref[16 * r : 16 * r + 16, :]
            new = []
            for c in range(2):
                i = kn * 2 + c
                value = center * cells[c] + lap * second[c]
                if not first:
                    value = value + wt * r_ref[i, r + 2, 4:20, :]
                new.append(value - grad[1] if c == 0 else value + grad[0])
            if last:
                orb_r = orb_ref[pl.ds(pl.multiple_of(rows_at(kn, 0, r), 16), 16), :]
                orb_i = orb_ref[pl.ds(pl.multiple_of(rows_at(kn, 1, r), 16), 16), :]
                out_ref[16 * r : 16 * r + 16, :] += orb_r * new[0] + orb_i * new[1]
                out_ref[16 * (ROWS + r) : 16 * (ROWS + r) + 16, :] += orb_r * new[1] - orb_i * new[0]
            else:
                for c in range(2):
                    out_ref[pl.ds(pl.multiple_of(rows_at(kn, c, r), 16), 16), :] = new[c]

    along_x(0, 0, flats[0])

    def orbital(kn, carry):
        kx, ky, kz, base, wt, scale = scalars_of(count, par_ref, w_ref, kn)
        ws = wt * scale
        keep = scale - ws * base
        if first:
            keep = keep + wt
        coef = (ws / 24.0, ws * kx / 12.0, ws * ky * (2.0 / 3.0), ws * kz * (2.0 / 3.0), keep, ws, wt)
        ahead = jnp.minimum(kn + 1, 11)
        for g in range(3):
            along_x(kn if g < 2 else ahead, (g + 1) % 3, flats[(g + 1) % 3])
            rows_of(kn, g, flats[g], coef)
        return carry

    lax.fori_loop(0, 12, orbital, 0)


def inner_step(count, par, weights, u, right, pot, matrix, orb):
    last = count == ITERS - 1
    return call(
        functools.partial(step_kernel, count),
        (par, weights) + ((u,) if count > 1 else ()) + (right, pot, matrix) + ((orb,) if last else ()),
        [(2 * ROWS * 16, 128) if last else ORBITALS],
        scratch=[pltpu.VMEM((256, 256), F32)] * 3,
        scalars=2,
        flops=60_000_000,
    )[0]


def face_terms(lap, g, beyond1, beyond2):
    first = [lap * (16.0 * beyond1[c] - beyond2[c]) for c in range(2)]
    grad1 = [g * (beyond1[c] - 0.125 * beyond2[c]) for c in range(2)]
    second = [-lap * beyond1[c] for c in range(2)]
    grad2 = [(-0.125 * g) * beyond1[c] for c in range(2)]
    return (
        (first[0] - grad1[1], first[1] + grad1[0]),
        (second[0] - grad2[1], second[1] + grad2[0]),
    )


def faces(count, par_ref, w_ref, pos_ref, kn, za, zb, ya, yb, add_plane, add_row):
    _, ky, kz, _, wt, scale = scalars_of(count, par_ref, w_ref, kn)
    ws = wt * scale
    lap = ws / 24.0
    gy, gz = ws * ky * (2.0 / 3.0), ws * kz * (2.0 / 3.0)
    from_z = (kn + 6) % 12

    def plane(ref, p):
        return [ref[pl.ds(pl.multiple_of(((kn * 2 + c) * 2 + p) * ROWS, 8), ROWS), :] for c in range(2)]

    def line(ref, r):
        return [ref[pl.ds(pl.multiple_of(((from_z * 2 + c) * 2 + r) * 16, 8), 16), :] for c in range(2)]

    def side(ref, layer, size, g, below, add, which):
        sign = (1 - 2 * below).astype(F32)
        first = (1 - below) * (size - 1)
        terms = face_terms(lap, sign * g, layer(ref, below), layer(ref, 1 - below))
        add(first, terms[0], which, 1 - below)
        add(first + 2 * below - 1, terms[1], which, below)

    odd = pos_ref[1] & 1
    side(ya, line, ROWS, gy, odd, add_row, 0)
    side(yb, line, ROWS, gy, 1 - odd, add_row, 1)
    odd = pos_ref[4] & 1
    side(za, plane, 16, gz, odd, add_plane, 0)
    side(zb, plane, 16, gz, 1 - odd, add_plane, 1)


def faces_kernel(count, par_ref, w_ref, pos_ref, u_in, za_in, zb_in, ya_in, yb_in, u_ref, za, zb, ya, yb):
    flat = u_ref.reshape(24 * TALL * DEEP, 128)

    def orbital(kn, carry):
        for c in range(2):
            clear_rows(u_ref, kn * 2 + c)
            for r in range(ROWS):
                clear_sides(u_ref, kn * 2 + c, r + 2)
                u_ref[kn * 2 + c, r + 2, 4:20, :] = u_in[pl.ds(pl.multiple_of(rows_at(kn, c, r), 16), 16), :]

        def add_plane(p, term, which, place):
            for c in range(2):
                at = pl.ds(field_rows(kn, c, 0, p), ROWS, stride=DEEP)
                value = flat[at, :] + term[c]
                flat[at, :] = value
                to = pl.ds(pl.multiple_of(((kn * 2 + c) * 2 + place) * ROWS, 8), ROWS)
                (za, zb)[which][to, :] = value

        def add_row(r, term, which, place):
            for c in range(2):
                u_ref[kn * 2 + c, r + 2, 4:20, :] = u_ref[kn * 2 + c, r + 2, 4:20, :] + term[c]

        faces(count, par_ref, w_ref, pos_ref, kn, za_in, zb_in, ya_in, yb_in, add_plane, add_row)
        cut_rows(u_ref, pos_ref, kn, ya, yb)
        return carry

    lax.fori_loop(0, 12, orbital, 0)


def add_faces(count, par, weights, pos, u, halos):
    return call(
        functools.partial(faces_kernel, count),
        (par, weights, pos, u, *halos),
        [FIELD, ZHALO, ZHALO, YHALO, YHALO],
        scalars=3,
    )


def density_kernel(par_ref, w_ref, pos_ref, d_in, za, zb, ya, yb, orb_ref, keep_ref, send_ref, d_ref):
    d_ref[...] = d_in[...]

    def orbital(kn, carry):
        def add(at, to, term):
            orb_r, orb_i = orb_ref[at[0], :], orb_ref[at[1], :]
            d_ref[to[0], :] = d_ref[to[0], :] + (orb_r * term[0] + orb_i * term[1])
            d_ref[to[1], :] = d_ref[to[1], :] + (orb_r * term[1] - orb_i * term[0])

        def add_plane(p, term, which, place):
            add(
                [pl.ds(rows_at(kn, c, 0) + p, ROWS, stride=16) for c in range(2)],
                [pl.ds(c * ROWS * 16 + p, ROWS, stride=16) for c in range(2)],
                term,
            )

        def add_row(r, term, which, place):
            add(
                [pl.ds(pl.multiple_of(rows_at(kn, c, r), 16), 16) for c in range(2)],
                [pl.ds(pl.multiple_of((c * ROWS + r) * 16, 16), 16) for c in range(2)],
                term,
            )

        faces(ITERS - 1, par_ref, w_ref, pos_ref, kn, za, zb, ya, yb, add_plane, add_row)
        return carry

    lax.fori_loop(0, 12, orbital, 0)
    ids = lane_ids()
    core = pos_ref[3]
    for ref, c in ((send_ref, 1 - core), (keep_ref, core)):
        for z in range(2):
            for g in range(6):
                rows = [
                    d_ref[pl.ds(pl.multiple_of((c * ROWS + 4 * g + j) * 16 + 8 * z, 8), 8), :] * (1.0 / 32.0)
                    for j in range(4)
                ]
                packed = pack_rows(*rows, ids)
                for v in range(3):
                    at = g * GROUP + v * 128
                    ref[z, :, at : at + 128] = packed[v]


TILE = (2, 8, CHUNK)


def tile_density(par, weights, pos, dens, halos, orb):
    return call(
        density_kernel,
        (par, weights, pos, dens, *halos, orb),
        [TILE, TILE],
        scratch=[pltpu.VMEM((2 * ROWS * 16, 128), F32)],
        scalars=3,
    )


def pair_kernel(a, b, out):
    out[...] = a[...] + b[...]


def split_kernel(pos_ref, s0, s1, s2, s3, mine, other):
    half = pos_ref[0]
    mine[...] = (s0[half] + s1[half]) + (s2[half] + s3[half])
    half = 1 - half
    other[...] = (s0[half] + s1[half]) + (s2[half] + s3[half])


def place_kernel(pos_ref, *refs):
    tiles, out_ref, sems = refs[:8], refs[8], refs[9]
    z, core = pos_ref[1], pos_ref[3]
    copies = []
    for i, tile in enumerate(tiles):
        component = core if i < 4 else 1 - core
        target = out_ref.at[component, :, pl.ds(pl.multiple_of((z ^ (i % 4)) * CHUNK, 128), CHUNK)]
        copies.append(pltpu.make_async_copy(tile, target, sems.at[i]))
    for copy in copies:
        copy.start()
    for copy in copies:
        copy.wait()


def place(pos, tiles):
    return pl.pallas_call(
        place_kernel,
        in_specs=[pl.BlockSpec(memory_space=pltpu.SMEM)] + [pl.BlockSpec(memory_space=pl.ANY)] * 8,
        out_specs=IN_HBM,
        out_shape=jax.ShapeDtypeStruct((2, 8, 4 * CHUNK), F32),
        scratch_shapes=[pltpu.SemaphoreType.DMA((8,))],
        compiler_params=pltpu.CompilerParams(vmem_limit_bytes=4 * 2**20),
        name="place",
    )(pos, *[pltpu.with_memory_space_constraint(t, pltpu.VMEM) for t in tiles])


def program(orbitals, partner_map, wave_vectors, levels, potential, perturbation, step_weights):
    zl, zh = lax.axis_index("zl"), lax.axis_index("zh")
    z = zh * 2 + zl
    pos = jnp.stack([zh, z, lax.axis_index("x"), lax.axis_index("c"), lax.axis_index("y")]).astype(jnp.int32)
    ncells = 64 * 4 * CHUNK
    matrix = jnp.asarray(x_matrix(), jnp.bfloat16)

    send3, send1, send2, small, mine = cut(pos, orbitals, perturbation, potential, wave_vectors, levels, partner_map)
    field = z_xor(small, 3)
    o3 = z_xor(send3, 3)
    o1 = z_xor(send1, 1)
    o2 = z_xor(send2, 2)
    shared = [field]
    for m in (1, 2, 3):
        shared.append(x_xor(field, m))
    got = jnp.stack(shared)
    swap = other_core(got)
    par = jnp.concatenate([mine[:2, :8], field[:2, HALF : HALF + 8]], 0)
    slots = par[:, 6].astype(jnp.int32)
    weights = step_weights.astype(F32) / 100.0

    part = products(pos, slots, orbitals, o1, perturbation)
    part = products(pos, slots, o2, o3, got, swap, part)
    orb, w, pot = orbital_rows(pos, [orbitals, o1, o2, o3], potential, perturbation, got, swap)

    def swapped(value):
        return jnp.concatenate([value[8:], value[:8]], 0)

    part = part + swapped(z_xor(part, 1)) + z_xor(part, 2) + swapped(z_xor(part, 3))
    sums = [part] + [y_xor(part, m) for m in (1, 2, 3)]
    orb, w, pot, sums = lax.optimization_barrier((orb, w, pot, sums))
    right, *edge = right_sides(float(ncells), slots, pos, sums, orb, w)
    u = right
    for count in range(1, ITERS):
        halos = exchange(*edge)
        u = inner_step(count, par, weights, u, right, pot, matrix, orb)
        if count < ITERS - 1:
            u, *edge = add_faces(count, par, weights, pos, u, halos)
    keep, send = tile_density(par, weights, pos, u, halos, orb)

    chip = call(pair_kernel, (keep, other_core(send)), [TILE])[0]
    parts = [chip]
    for m in (1, 2, 3):
        parts.append(x_xor(chip, m))
    same, cross = call(split_kernel, (pos, *parts), [(8, CHUNK)] * 2, scalars=1)
    tiles = [same, z_xor(same, 1), z_xor(cross, 2), z_xor(cross, 3)]
    return place(pos, tiles + [other_core(tile) for tile in tiles])


def solution(mesh):
    fine = Mesh(mesh.devices.reshape(2, 4, 2, 4, 2), ("zl", "x", "c", "y", "zh"))
    ka, grid = ("zl", "x", "c"), ("y", "zh")
    return jax.shard_map(
        program,
        mesh=fine,
        in_specs=(
            P(ka, None, None, grid, None),
            P(ka),
            P(ka, None),
            P(ka, None),
            P(grid, None),
            P(None, grid, None),
            P(),
        ),
        out_specs=P(None, grid, None),
        check_vma=False,
    )
```

```python
import functools

import jax
import jax.numpy as jnp
import numpy as np
from jax import lax
from jax.experimental import pallas as pl
from jax.experimental.pallas import tpu as pltpu
from jax.sharding import Mesh
from jax.sharding import PartitionSpec as P


NX = 96
ITERS = 4
ROWS = 24
CHUNK = ROWS * NX
GROUP = 4 * NX
F32 = jnp.float32
ZAX = ("zl", "zh")


def z_perm(to):
    index = lambda z: (z & 1) * 2 + (z >> 1)
    return [(index(z), index(to(z))) for z in range(4)]


def z_xor(value, m):
    return lax.ppermute(value, ZAX, z_perm(lambda z: z ^ m))


def other_core(value):
    return lax.ppermute(value, "c", [(0, 1), (1, 0)])


def x_xor(value, m):
    return lax.ppermute(value, "x", [(i, i ^ m) for i in range(4)])


def y_xor(value, m):
    return lax.ppermute(value, "y", [(i, i ^ m) for i in range(4)])


def lane_ids():
    return lax.broadcasted_iota(jnp.int32, (8, 128), 1)


def unpack_rows(a, b, c, lanes):
    r1 = pltpu.roll(jnp.where(lanes < 96, b, a), 32, 1)
    r2 = pltpu.roll(jnp.where(lanes < 64, c, b), 64, 1)
    r3 = pltpu.roll(c, 96, 1)
    return a, r1, r2, r3


def pack_rows(r0, r1, r2, r3, lanes):
    r1s = pltpu.roll(r1, 96, 1)
    r2s = pltpu.roll(r2, 64, 1)
    r3s = pltpu.roll(r3, 32, 1)
    return (
        jnp.where(lanes < 96, r0, r1s),
        jnp.where(lanes < 64, r1s, r2s),
        jnp.where(lanes < 32, r2s, r3s),
    )


def in_vmem(shape):
    return pltpu.VMEM(shape, F32)


def call(kernel, args, outs, scratch=(), scalars=0, aliases=None, flops=10_000_000, limit=8):
    specs = [pl.BlockSpec(memory_space=pltpu.SMEM)] * scalars
    specs += [pl.BlockSpec(memory_space=pltpu.VMEM)] * (len(args) - scalars)
    args = list(args[:scalars]) + [pltpu.with_memory_space_constraint(a, pltpu.VMEM) for a in args[scalars:]]
    return pl.pallas_call(
        kernel,
        in_specs=specs,
        out_specs=[pl.BlockSpec(memory_space=pltpu.VMEM)] * len(outs),
        out_shape=[in_vmem(o) for o in outs],
        scratch_shapes=list(scratch),
        input_output_aliases=aliases or {},
        compiler_params=pltpu.CompilerParams(vmem_limit_bytes=limit * 2**20),
        cost_estimate=pl.CostEstimate(flops=flops, bytes_accessed=10_000_000, transcendentals=0),
    )(*args)


def lanes_at(group, v, base=0):
    return pl.ds(pl.multiple_of(base + group * GROUP + v * 128, 128), 128)


HALF = CHUNK // 2
IN_HBM = pl.BlockSpec(memory_space=pltpu.HBM)


def rows_of_chunk(ref, z, extra=0, width=CHUNK):
    index = (slice(None),) * (len(ref.shape) - 1) + (pl.ds(pl.multiple_of(z * CHUNK + extra, 128), width),)
    return ref.at[index]


def cut_kernel(pos_ref, orb, pert, pot, wave, level, partner, send3, send1, send2, small, mine, wave_s, level_s, partner_s, sems):
    z, core = pos_ref[1], pos_ref[3]
    moves = [
        (wave, wave_s),
        (level, level_s),
        (partner, partner_s),
        (rows_of_chunk(orb, z ^ 3), send3),
        (rows_of_chunk(orb, z ^ 1), send1),
        (rows_of_chunk(orb, z ^ 2), send2),
    ]
    copies = [pltpu.make_async_copy(source, target, sems.at[i]) for i, (source, target) in enumerate(moves)]
    for copy in copies:
        copy.start()
    field = small.at[:, pl.ds(0, HALF)]
    of_pert = rows_of_chunk(pert, z ^ 3, core * HALF, HALF).at[jnp.minimum(pos_ref[2], 1)]
    pert_copy = pltpu.make_async_copy(of_pert, field, sems.at[6])
    pot_copy = pltpu.make_async_copy(rows_of_chunk(pot, z ^ 3, core * HALF, HALF), field, sems.at[6])
    pl.when(pos_ref[2] < 2)(pert_copy.start)
    pl.when(pos_ref[2] >= 2)(pot_copy.start)
    rows = lax.broadcasted_iota(jnp.int32, (8, 128), 0)
    cols = lax.broadcasted_iota(jnp.int32, (8, 128), 1)
    out = jnp.zeros((8, 128), F32)
    for copy in copies[:3]:
        copy.wait()
    for k in range(2):
        values = [wave_s[k, d] for d in range(3)] + [level_s[k, n] for n in range(3)]
        values.append((partner_s[k] & 1).astype(F32))
        for j, value in enumerate(values):
            out = jnp.where((rows == k) & (cols == j), value, out)
    mine[...] = out
    small[:, HALF:] = out
    pot_copy.wait()
    for copy in copies[3:]:
        copy.wait()


def cut(pos, orbitals, perturbation, potential, wave, level, partner_map):
    chunk = orbitals.shape[:-1] + (CHUNK,)
    return pl.pallas_call(
        cut_kernel,
        in_specs=[pl.BlockSpec(memory_space=pltpu.SMEM)] + [IN_HBM] * 6,
        out_specs=[pl.BlockSpec(memory_space=pltpu.VMEM)] * 5,
        out_shape=[in_vmem(chunk)] * 3 + [in_vmem((8, HALF + 128)), in_vmem((8, 128))],
        scratch_shapes=[
            pltpu.SMEM((2, 3), F32),
            pltpu.SMEM((2, 3), F32),
            pltpu.SMEM((2,), jnp.int32),
            pltpu.SemaphoreType.DMA((7,)),
        ],
        compiler_params=pltpu.CompilerParams(vmem_limit_bytes=4 * 2**20),
        name="cut",
    )(pos, *[pltpu.with_memory_space_constraint(a, pltpu.HBM) for a in (orbitals, perturbation, potential, wave, level, partner_map)])


def perturbed(field, pert_r, pert_i):
    re, im = field
    return pert_r * re - pert_i * im, pert_r * im + pert_i * re


def join_halves(pos_ref, got, swap, joined, fields):
    x, core = pos_ref[2], pos_ref[3]
    for to, i in enumerate(fields):
        joined[to, :, pl.ds(pl.multiple_of(core * HALF, 128), HALF)] = got[x ^ i, :, :HALF]
        joined[to, :, pl.ds(pl.multiple_of((1 - core) * HALF, 128), HALF)] = swap[x ^ i, :, :HALF]


def one_lane_each(rows):
    row = lax.broadcasted_iota(jnp.int32, (40, 128), 0)
    lane = lax.broadcasted_iota(jnp.int32, (40, 128), 1)
    return jnp.where(row == lane, rows, 0.0)


def over_lanes(rows):
    ones = jnp.full((128, 128), 1.0, F32)
    return jnp.dot(rows, ones, precision=lax.Precision.HIGHEST, preferred_element_type=F32)


def products_kernel(near, pos_ref, slot_ref, o0, o1, *refs):
    if near:
        pert, out_ref = refs
        base = pos_ref[1] * CHUNK
    else:
        got, swap, near_ref, sums_ref, pert, out_ref = refs
        join_halves(pos_ref, got, swap, pert, (0, 1))
        base = 0
    pair, bases = (o0, o1), (base, 0)
    for k in range(4):
        block, kk = k // 2, k % 2
        slot = slot_ref[k]

        def body(g, acc, block=block, kk=kk, slot=slot):
            acc = list(acc)
            own, mate = pair[block], pair[1 - block]
            for v in range(3):
                at, mate_at, pert_at = (lanes_at(g, v, start) for start in (bases[block], bases[1 - block], base))
                pr, pi = pert[0, :, pert_at], pert[1, :, pert_at]
                w = [perturbed((own[kk, n, 0, :, at], own[kk, n, 1, :, at]), pr, pi) for n in range(3)]
                for m in range(3):
                    mr, mi = mate[slot, m, 0, :, mate_at], mate[slot, m, 1, :, mate_at]
                    for n in range(3):
                        i = (m * 3 + n) * 2
                        acc[i] = acc[i] + (mr * w[n][0] + mi * w[n][1])
                        acc[i + 1] = acc[i + 1] + (mr * w[n][1] - mi * w[n][0])
            return tuple(acc)

        acc = lax.fori_loop(0, CHUNK // GROUP, body, (jnp.zeros((8, 128), F32),) * 18)
        for i in range(18):
            at = pl.ds(block * 40 + kk * 18 + i, 1)
            value = jnp.sum(acc[i], axis=0, keepdims=True)
            out_ref[at, :] = value if near else near_ref[at, :] + value
    for block in range(2):
        out_ref[block * 40 + 36 : block * 40 + 40, :] = jnp.zeros((4, 128), F32)
    if not near:
        total = over_lanes(out_ref[...])
        for block in range(2):
            row = jnp.sum(one_lane_each(total[block * 40 : block * 40 + 40]), axis=0, keepdims=True)
            sums_ref[block * 8 : block * 8 + 8, :] = jnp.broadcast_to(row, (8, 128))


def products(pos, slots, o0, o1, *pert):
    near = len(pert) == 1
    return call(
        functools.partial(products_kernel, near),
        (pos, slots, o0, o1, *pert),
        [(80, 128) if near else (16, 128)],
        scratch=() if near else [pltpu.VMEM((2, 8, CHUNK), F32), pltpu.VMEM((80, 128), F32)],
        scalars=2,
        flops=20_000_000,
    )[0]


TALL, DEEP = ROWS + 4, 24
FIELD = (24, TALL, DEEP, 128)
ORBITALS = (24 * ROWS * 16, 128)


def rows_at(kn, c, r):
    return ((kn * 2 + c) * ROWS + r) * 16


def orbital_rows_kernel(pos_ref, o0, o1, o2, o3, pot, pert, got, swap, orb_ref, w_ref, v_ref, joined):
    join_halves(pos_ref, got, swap, joined, (0, 1, 2))
    lanes = lane_ids()
    half = pos_ref[0]

    def rows_of(ref, index, g, base):
        return unpack_rows(*[ref[index + (slice(None), lanes_at(g, v, base))] for v in range(3)], lanes)

    def body(g, carry):
        near = pos_ref[1] * CHUNK
        fields = ((pert, (0,)), (pert, (1,)), (pot, ())), tuple((joined, (i,)) for i in range(3))
        for pair, local, z, base in (((o0, o1), fields[0], half, near), ((o2, o3), fields[1], 1 - half, 0)):
            pert_r, pert_i, rows = (rows_of(ref, index, g, base) for ref, index in local)
            for j in range(4):
                v_ref[pl.ds(pl.multiple_of((4 * g + j) * 16 + 8 * z, 8), 8), :] = rows[j]
            for k in range(4):
                start = base if k < 2 else 0
                for n in range(3):
                    field = [rows_of(pair[k // 2], (k % 2, n, c), g, start) for c in range(2)]
                    for j in range(4):
                        orb = field[0][j], field[1][j]
                        w = perturbed(orb, pert_r[j], pert_i[j])
                        for c in range(2):
                            at = pl.ds(pl.multiple_of(rows_at(k * 3 + n, c, 4 * g + j) + 8 * z, 8), 8)
                            orb_ref[at, :] = orb[c]
                            w_ref[at, :] = w[c]
        return carry

    lax.fori_loop(0, CHUNK // GROUP, body, 0)


def orbital_rows(pos, fields, *local):
    return call(
        orbital_rows_kernel,
        (pos, *fields, *local),
        [ORBITALS, ORBITALS, (ROWS * 16, 128)],
        scratch=[pltpu.VMEM((3, 8, CHUNK), F32)],
        scalars=1,
    )


ZHALO, YHALO = (48 * ROWS, 128), (24 * 32, 128)


def field_rows(kn, c, r, plane):
    return ((kn * 2 + c) * TALL + r + 2) * DEEP + 4 + plane


def clear_rows(u_ref, i):
    for r in (0, 1, TALL - 2, TALL - 1):
        u_ref[i, r] = jnp.zeros((DEEP, 128), F32)


def clear_sides(u_ref, i, r):
    u_ref[i, r, 0:4] = jnp.zeros((4, 128), F32)
    u_ref[i, r, 20:24] = jnp.zeros((4, 128), F32)


def near_face(parity, size):
    return (1 - parity) * (size - 2)


def cut_planes(flat, pos_ref, kn, za, zb):
    up = near_face(pos_ref[4] & 1, 16)
    for ref, first in ((za, up), (zb, 14 - up)):
        for c in range(2):
            for p in range(2):
                to = pl.ds(pl.multiple_of(((kn * 2 + c) * 2 + p) * ROWS, 8), ROWS)
                ref[to, :] = flat[pl.ds(field_rows(kn, c, 0, first + p), ROWS, stride=DEEP), :]


def cut_rows(u_ref, pos_ref, kn, ya, yb):
    up = near_face(pos_ref[1] & 1, ROWS)
    for ref, first in ((ya, up), (yb, ROWS - 2 - up)):
        for c in range(2):
            i = kn * 2 + c
            for p in range(2):
                to = pl.ds(pl.multiple_of((i * 2 + p) * 16, 8), 16)
                ref[to, :] = u_ref[i, 2 + first + p, 4:20, :]


def exchange(za, zb, ya, yb):
    got = []
    for move, value, m in ((y_xor, za, 1), (y_xor, zb, 3), (z_xor, ya, 1), (z_xor, yb, 3)):
        got.append(move(value, m))
    return got


def right_kernel(ncells, slot_ref, pos_ref, s0, s1, s2, s3, orb_ref, w_ref, r_ref, za, zb, ya, yb, prod_ref):
    total = (s0[...] + s1[...]) + (s2[...] + s3[...])
    spread = [one_lane_each(jnp.broadcast_to(total[8 * block : 8 * block + 1], (40, 128))) for block in range(2)]
    prod_ref[...] = over_lanes(jnp.concatenate(spread, 0)) / ncells
    for k in range(4):
        block, kk = k // 2, k % 2
        mate = (2 - 2 * block + slot_ref[k]) * 3

        def body(r, carry, k=k, block=block, kk=kk, mate=mate):
            def cells(ref, kn, c):
                return ref[pl.ds(pl.multiple_of(rows_at(kn, c, r), 16), 16), :]

            mates = [(cells(orb_ref, mate + m, 0), cells(orb_ref, mate + m, 1)) for m in range(3)]
            for n in range(3):
                gr, gi = -cells(w_ref, k * 3 + n, 0), -cells(w_ref, k * 3 + n, 1)
                for m, (mr, mi) in enumerate(mates):
                    row = block * 40 + kk * 18 + (m * 3 + n) * 2
                    qr, qi = prod_ref[pl.ds(row, 1), :], prod_ref[pl.ds(row + 1, 1), :]
                    gr = gr + (qr * mr - qi * mi)
                    gi = gi + (qi * mr + qr * mi)
                for c, value in enumerate((gr, gi)):
                    i = (k * 3 + n) * 2 + c
                    clear_sides(r_ref, i, r + 2)
                    r_ref[i, r + 2, 4:20, :] = value
            return carry

        lax.fori_loop(0, ROWS, body, 0, unroll=4)
    flat = r_ref.reshape(24 * TALL * DEEP, 128)

    def cut(kn, carry):
        for c in range(2):
            clear_rows(r_ref, kn * 2 + c)
        cut_planes(flat, pos_ref, kn, za, zb)
        cut_rows(r_ref, pos_ref, kn, ya, yb)
        return carry

    lax.fori_loop(0, 12, cut, 0, unroll=4)


def right_sides(ncells, slots, pos, sums, orb, w):
    return call(
        functools.partial(right_kernel, ncells),
        (slots, pos, *sums, orb, w),
        [FIELD, ZHALO, ZHALO, YHALO, YHALO],
        scratch=[pltpu.VMEM((80, 128), F32)],
        scalars=2,
        flops=20_000_000,
    )


def x_matrix():
    m = np.zeros((128, 256), np.float32)
    for i in range(NX):
        for s, lap, grad in ((1, 16, 8), (-1, 16, -8), (2, -1, -1), (-2, -1, 1)):
            m[(i + s) % NX, i] += lap
            m[(i + s) % NX, 128 + i] += grad
    return np.concatenate([m, m], 0)


def scalars_of(count, par_ref, w_ref, kn):
    k, n = kn // 3, kn % 3
    kx, ky, kz = par_ref[k, 0], par_ref[k, 1], par_ref[k, 2]
    base = 3.75 + 0.5 * (kx * kx + ky * ky + kz * kz) + par_ref[k, 3 + n]
    wt = w_ref[count]
    scale = w_ref[0] if count == 1 else jnp.float32(1.0)
    return kx, ky, kz, base, wt, scale


def step_kernel(count, par_ref, w_ref, *refs):
    last, first = count == ITERS - 1, count == 1
    if first:
        r_ref, v_ref, m_ref, *refs = refs
        u_ref = r_ref
    else:
        u_ref, r_ref, v_ref, m_ref, *refs = refs
    if last:
        orb_ref, out_ref, *flats = refs
        out_ref[...] = jnp.zeros_like(out_ref)
    else:
        out_ref, *flats = refs

    def along_x(kn, g, flat):
        cells = [u_ref[kn * 2 + c, 2 + 8 * g : 10 + 8 * g, 4:20, :].reshape(128, 128) for c in range(2)]
        u2 = jnp.concatenate(cells, 0)
        hi = u2.astype(jnp.bfloat16)
        lo = (u2 - hi.astype(F32)).astype(jnp.bfloat16)
        flat[...] = jnp.dot(jnp.concatenate([hi, lo], 1), m_ref[...], preferred_element_type=F32)

    def rows_of(kn, g, flat, coef):
        lap, gx, gy, gz, keep, pull, wt = coef
        for r in range(8 * g, 8 * g + 8):
            cells, second, grad = [], [], []
            for c in range(2):
                i = kn * 2 + c
                at = slice((c * 8 + r - 8 * g) * 16, (c * 8 + r - 8 * g + 1) * 16)
                yp1, ym1 = u_ref[i, r + 3, 4:20, :], u_ref[i, r + 1, 4:20, :]
                yp2, ym2 = u_ref[i, r + 4, 4:20, :], u_ref[i, r, 4:20, :]
                zp1, zm1 = u_ref[i, r + 2, 5:21, :], u_ref[i, r + 2, 3:19, :]
                zp2, zm2 = u_ref[i, r + 2, 6:22, :], u_ref[i, r + 2, 2:18, :]
                cells.append(u_ref[i, r + 2, 4:20, :])
                one = (yp1 + ym1) + (zp1 + zm1)
                two = (yp2 + ym2) + (zp2 + zm2)
                second.append(flat[at, 0:128] + (16.0 * one - two))
                dy = (yp1 - ym1) - 0.125 * (yp2 - ym2)
                dz = (zp1 - zm1) - 0.125 * (zp2 - zm2)
                grad.append(gx * flat[at, 128:256] + (gy * dy + gz * dz))
            center = keep - pull * v_ref[16 * r : 16 * r + 16, :]
            new = []
            for c in range(2):
                i = kn * 2 + c
                value = center * cells[c] + lap * second[c]
                if not first:
                    value = value + wt * r_ref[i, r + 2, 4:20, :]
                new.append(value - grad[1] if c == 0 else value + grad[0])
            if last:
                orb_r = orb_ref[pl.ds(pl.multiple_of(rows_at(kn, 0, r), 16), 16), :]
                orb_i = orb_ref[pl.ds(pl.multiple_of(rows_at(kn, 1, r), 16), 16), :]
                out_ref[16 * r : 16 * r + 16, :] += orb_r * new[0] + orb_i * new[1]
                out_ref[16 * (ROWS + r) : 16 * (ROWS + r) + 16, :] += orb_r * new[1] - orb_i * new[0]
            else:
                for c in range(2):
                    out_ref[pl.ds(pl.multiple_of(rows_at(kn, c, r), 16), 16), :] = new[c]

    along_x(0, 0, flats[0])

    def orbital(kn, carry):
        kx, ky, kz, base, wt, scale = scalars_of(count, par_ref, w_ref, kn)
        ws = wt * scale
        keep = scale - ws * base
        if first:
            keep = keep + wt
        coef = (ws / 24.0, ws * kx / 12.0, ws * ky * (2.0 / 3.0), ws * kz * (2.0 / 3.0), keep, ws, wt)
        ahead = jnp.minimum(kn + 1, 11)
        for g in range(3):
            along_x(kn if g < 2 else ahead, (g + 1) % 3, flats[(g + 1) % 3])
            rows_of(kn, g, flats[g], coef)
        return carry

    lax.fori_loop(0, 12, orbital, 0)


def inner_step(count, par, weights, u, right, pot, matrix, orb):
    last = count == ITERS - 1
    return call(
        functools.partial(step_kernel, count),
        (par, weights) + ((u,) if count > 1 else ()) + (right, pot, matrix) + ((orb,) if last else ()),
        [(2 * ROWS * 16, 128) if last else ORBITALS],
        scratch=[pltpu.VMEM((256, 256), F32)] * 3,
        scalars=2,
        flops=60_000_000,
    )[0]


def face_terms(lap, g, beyond1, beyond2):
    first = [lap * (16.0 * beyond1[c] - beyond2[c]) for c in range(2)]
    grad1 = [g * (beyond1[c] - 0.125 * beyond2[c]) for c in range(2)]
    second = [-lap * beyond1[c] for c in range(2)]
    grad2 = [(-0.125 * g) * beyond1[c] for c in range(2)]
    return (
        (first[0] - grad1[1], first[1] + grad1[0]),
        (second[0] - grad2[1], second[1] + grad2[0]),
    )


def faces(count, par_ref, w_ref, pos_ref, kn, za, zb, ya, yb, add_plane, add_row):
    _, ky, kz, _, wt, scale = scalars_of(count, par_ref, w_ref, kn)
    ws = wt * scale
    lap = ws / 24.0
    gy, gz = ws * ky * (2.0 / 3.0), ws * kz * (2.0 / 3.0)
    from_z = (kn + 6) % 12

    def plane(ref, p):
        return [ref[pl.ds(pl.multiple_of(((kn * 2 + c) * 2 + p) * ROWS, 8), ROWS), :] for c in range(2)]

    def line(ref, r):
        return [ref[pl.ds(pl.multiple_of(((from_z * 2 + c) * 2 + r) * 16, 8), 16), :] for c in range(2)]

    def side(ref, layer, size, g, below, add, which):
        sign = (1 - 2 * below).astype(F32)
        first = (1 - below) * (size - 1)
        terms = face_terms(lap, sign * g, layer(ref, below), layer(ref, 1 - below))
        add(first, terms[0], which, 1 - below)
        add(first + 2 * below - 1, terms[1], which, below)

    odd = pos_ref[1] & 1
    side(ya, line, ROWS, gy, odd, add_row, 0)
    side(yb, line, ROWS, gy, 1 - odd, add_row, 1)
    odd = pos_ref[4] & 1
    side(za, plane, 16, gz, odd, add_plane, 0)
    side(zb, plane, 16, gz, 1 - odd, add_plane, 1)


def faces_kernel(count, par_ref, w_ref, pos_ref, u_in, za_in, zb_in, ya_in, yb_in, u_ref, za, zb, ya, yb):
    flat = u_ref.reshape(24 * TALL * DEEP, 128)

    def orbital(kn, carry):
        for c in range(2):
            clear_rows(u_ref, kn * 2 + c)
            for r in range(ROWS):
                clear_sides(u_ref, kn * 2 + c, r + 2)
                u_ref[kn * 2 + c, r + 2, 4:20, :] = u_in[pl.ds(pl.multiple_of(rows_at(kn, c, r), 16), 16), :]

        def add_plane(p, term, which, place):
            for c in range(2):
                at = pl.ds(field_rows(kn, c, 0, p), ROWS, stride=DEEP)
                value = flat[at, :] + term[c]
                flat[at, :] = value
                to = pl.ds(pl.multiple_of(((kn * 2 + c) * 2 + place) * ROWS, 8), ROWS)
                (za, zb)[which][to, :] = value

        def add_row(r, term, which, place):
            for c in range(2):
                u_ref[kn * 2 + c, r + 2, 4:20, :] = u_ref[kn * 2 + c, r + 2, 4:20, :] + term[c]

        faces(count, par_ref, w_ref, pos_ref, kn, za_in, zb_in, ya_in, yb_in, add_plane, add_row)
        cut_rows(u_ref, pos_ref, kn, ya, yb)
        return carry

    lax.fori_loop(0, 12, orbital, 0)


def add_faces(count, par, weights, pos, u, halos):
    return call(
        functools.partial(faces_kernel, count),
        (par, weights, pos, u, *halos),
        [FIELD, ZHALO, ZHALO, YHALO, YHALO],
        scalars=3,
    )


def density_kernel(par_ref, w_ref, pos_ref, d_in, za, zb, ya, yb, orb_ref, keep_ref, send_ref, d_ref):
    d_ref[...] = d_in[...]

    def orbital(kn, carry):
        def add(at, to, term):
            orb_r, orb_i = orb_ref[at[0], :], orb_ref[at[1], :]
            d_ref[to[0], :] = d_ref[to[0], :] + (orb_r * term[0] + orb_i * term[1])
            d_ref[to[1], :] = d_ref[to[1], :] + (orb_r * term[1] - orb_i * term[0])

        def add_plane(p, term, which, place):
            add(
                [pl.ds(rows_at(kn, c, 0) + p, ROWS, stride=16) for c in range(2)],
                [pl.ds(c * ROWS * 16 + p, ROWS, stride=16) for c in range(2)],
                term,
            )

        def add_row(r, term, which, place):
            add(
                [pl.ds(pl.multiple_of(rows_at(kn, c, r), 16), 16) for c in range(2)],
                [pl.ds(pl.multiple_of((c * ROWS + r) * 16, 16), 16) for c in range(2)],
                term,
            )

        faces(ITERS - 1, par_ref, w_ref, pos_ref, kn, za, zb, ya, yb, add_plane, add_row)
        return carry

    lax.fori_loop(0, 12, orbital, 0, unroll=4)
    ids = lane_ids()
    core = pos_ref[3]
    for ref, c in ((send_ref, 1 - core), (keep_ref, core)):
        for z in range(2):
            for g in range(6):
                rows = [
                    d_ref[pl.ds(pl.multiple_of((c * ROWS + 4 * g + j) * 16 + 8 * z, 8), 8), :] * (1.0 / 32.0)
                    for j in range(4)
                ]
                packed = pack_rows(*rows, ids)
                for v in range(3):
                    at = g * GROUP + v * 128
                    ref[z, :, at : at + 128] = packed[v]


TILE = (2, 8, CHUNK)


def tile_density(par, weights, pos, dens, halos, orb):
    return call(
        density_kernel,
        (par, weights, pos, dens, *halos, orb),
        [TILE, TILE],
        scratch=[pltpu.VMEM((2 * ROWS * 16, 128), F32)],
        scalars=3,
    )


def pair_kernel(a, b, out):
    out[...] = a[...] + b[...]


def split_kernel(pos_ref, s0, s1, s2, s3, mine, other):
    half = pos_ref[0]
    mine[...] = (s0[half] + s1[half]) + (s2[half] + s3[half])
    half = 1 - half
    other[...] = (s0[half] + s1[half]) + (s2[half] + s3[half])


def place_kernel(pos_ref, *refs):
    tiles, out_ref, sems = refs[:8], refs[8], refs[9]
    z, core = pos_ref[1], pos_ref[3]
    copies = []
    for i, tile in enumerate(tiles):
        component = core if i < 4 else 1 - core
        target = out_ref.at[component, :, pl.ds(pl.multiple_of((z ^ (i % 4)) * CHUNK, 128), CHUNK)]
        copies.append(pltpu.make_async_copy(tile, target, sems.at[i]))
    for copy in copies:
        copy.start()
    for copy in copies:
        copy.wait()


def place(pos, tiles):
    return pl.pallas_call(
        place_kernel,
        in_specs=[pl.BlockSpec(memory_space=pltpu.SMEM)] + [pl.BlockSpec(memory_space=pl.ANY)] * 8,
        out_specs=IN_HBM,
        out_shape=jax.ShapeDtypeStruct((2, 8, 4 * CHUNK), F32),
        scratch_shapes=[pltpu.SemaphoreType.DMA((8,))],
        compiler_params=pltpu.CompilerParams(vmem_limit_bytes=4 * 2**20),
        name="place",
    )(pos, *[pltpu.with_memory_space_constraint(t, pltpu.VMEM) for t in tiles])


def program(orbitals, partner_map, wave_vectors, levels, potential, perturbation, step_weights):
    zl, zh = lax.axis_index("zl"), lax.axis_index("zh")
    z = zh * 2 + zl
    pos = jnp.stack([zh, z, lax.axis_index("x"), lax.axis_index("c"), lax.axis_index("y")]).astype(jnp.int32)
    ncells = 64 * 4 * CHUNK
    matrix = jnp.asarray(x_matrix(), jnp.bfloat16)

    send3, send1, send2, small, mine = cut(pos, orbitals, perturbation, potential, wave_vectors, levels, partner_map)
    field = z_xor(small, 3)
    o3 = z_xor(send3, 3)
    o1 = z_xor(send1, 1)
    o2 = z_xor(send2, 2)
    shared = [field]
    for m in (1, 2, 3):
        shared.append(x_xor(field, m))
    got = jnp.stack(shared)
    swap = other_core(got)
    par = jnp.concatenate([mine[:2, :8], field[:2, HALF : HALF + 8]], 0)
    slots = par[:, 6].astype(jnp.int32)
    weights = step_weights.astype(F32) / 100.0

    part = products(pos, slots, orbitals, o1, perturbation)
    part = products(pos, slots, o2, o3, got, swap, part)
    orb, w, pot = orbital_rows(pos, [orbitals, o1, o2, o3], potential, perturbation, got, swap)

    def swapped(value):
        return jnp.concatenate([value[8:], value[:8]], 0)

    part = part + swapped(z_xor(part, 1)) + z_xor(part, 2) + swapped(z_xor(part, 3))
    sums = [part] + [y_xor(part, m) for m in (1, 2, 3)]
    orb, w, pot, sums = lax.optimization_barrier((orb, w, pot, sums))
    right, *edge = right_sides(float(ncells), slots, pos, sums, orb, w)
    u = right
    for count in range(1, ITERS):
        halos = exchange(*edge)
        u = inner_step(count, par, weights, u, right, pot, matrix, orb)
        if count < ITERS - 1:
            u, *edge = add_faces(count, par, weights, pos, u, halos)
    keep, send = tile_density(par, weights, pos, u, halos, orb)

    chip = call(pair_kernel, (keep, other_core(send)), [TILE])[0]
    parts = [chip]
    for m in (1, 2, 3):
        parts.append(x_xor(chip, m))
    same, cross = call(split_kernel, (pos, *parts), [(8, CHUNK)] * 2, scalars=1)
    tiles = [same, z_xor(same, 1), z_xor(cross, 2), z_xor(cross, 3)]
    return place(pos, tiles + [other_core(tile) for tile in tiles])


def solution(mesh):
    fine = Mesh(mesh.devices.reshape(2, 4, 2, 4, 2), ("zl", "x", "c", "y", "zh"))
    ka, grid = ("zl", "x", "c"), ("y", "zh")
    return jax.shard_map(
        program,
        mesh=fine,
        in_specs=(
            P(ka, None, None, grid, None),
            P(ka),
            P(ka, None),
            P(ka, None),
            P(grid, None),
            P(None, grid, None),
            P(),
        ),
        out_specs=P(None, grid, None),
        check_vma=False,
    )
```
